32 devices in a mesh: dp: 16 (over z, y, x), tensor: 2 (over core).
Axes of the slice: x: 2, y: 2, z: 4, core: 2. Of those that a mesh axis runs over, the one named last changes fastest.
Arguments:
- hidden_in: bfloat16 [16384, 768], P(('dp', 'tensor')), may hold values from -6 to 6
- cotangent: bfloat16 [16384, 768], P(('dp', 'tensor')), may hold values from -6 to 6
- box_coords: int32 [4, 16384], P(None, ('dp', 'tensor')), may hold values from 0 to 999
- doc_ids: int32 [32, 512], P('dp'), may hold values from 0 to 7, never falling along the last dimension, each value on 1 to 128 neighbouring positions
- buckets: int32 [2, 32, 512, 512], P(None, 'dp'), may hold values from 0 to 31
- layout_weight: bfloat16 [256, 768], replicated, may hold values from -0.375 to 0.375
- norm_gains: bfloat16 [2, 768], replicated, may hold values from 0.5 to 1.5
- norm_shifts: bfloat16 [2, 768], replicated, may hold values from -3 to 3
- branch_biases: bfloat16 [2, 768], replicated, may hold values from -3 to 3
- qkv_weight: bfloat16 [3, 768, 768], P(None, None, 'tensor'), may hold values from -0.21875 to 0.21875
- query_value_bias: bfloat16 [2, 768], P(None, 'tensor'), may hold values from -3 to 3
- output_weight: bfloat16 [768, 768], P('tensor'), may hold values from -1.25 to 1.25
- ffn_in_weight: bfloat16 [768, 3072], P(None, 'tensor'), may hold values from -0.21875 to 0.21875
- ffn_in_bias: bfloat16 [3072], P('tensor'), may hold values from -3 to 3
- ffn_out_weight: bfloat16 [3072, 768], P('tensor'), may hold values from -0.15625 to 0.15625
- relative_table: bfloat16 [2, 32, 12], P(None, None, 'tensor'), may hold values from -4 to 4
- master_flat: float32 [2, 3643392], P('tensor', 'dp'), may hold values from -0.18 to 0.18
- moment_one: float32 [2, 3643392], P('tensor', 'dp'), may hold values from -0.00024 to 0.00024
- moment_two: float32 [2, 3643392], P('tensor', 'dp'), may hold values from 2e-11 to 5e-10
- ema_flat: float32 [2, 3643392], P('tensor', 'dp'), may hold values from -0.18 to 0.18
Outputs:
- hidden_out: bfloat16 [16384, 768], P(('dp', 'tensor'))
- input_grad: float32 [16384, 768], P(('dp', 'tensor'))
- layout_grad: float32 [256, 768], replicated
- gains_grad: float32 [2, 768], replicated
- shifts_grad: float32 [2, 768], replicated
- biases_grad: float32 [2, 768], replicated
- qkv_grad: float32 [3, 768, 768], P(None, None, 'tensor')
- qv_bias_grad: float32 [2, 768], P(None, 'tensor')
- output_grad: float32 [768, 768], P('tensor')
- ffn_in_grad: float32 [768, 3072], P(None, 'tensor')
- ffn_bias_grad: float32 [3072], P('tensor')
- ffn_out_grad: float32 [3072, 768], P('tensor')
- table_grad: float32 [2, 32, 12], P(None, None, 'tensor')
- grad_norm: float32 [], replicated
- new_master: float32 [2, 3643392], P('tensor', 'dp')
- new_moment_one: float32 [2, 3643392], P('tensor', 'dp')
- new_moment_two: float32 [2, 3643392], P('tensor', 'dp')
- new_ema: float32 [2, 3643392], P('tensor', 'dp')
- new_copy: bfloat16 [2, 3643392], P('tensor', 'dp')
The draws below stay inside these ranges and needn't reach their ends.
Inputs may be any that keep to these rules, and one draw needn't show every extreme that they name: `doc_ids`: in each window the ids never fall; every document holds 1 to 128 positions.
All inputs are finite; a program needn't handle non-finite values.
Results may differ from the reference program's by a relative error of at most 0.02.
The reference program's roundings to bfloat16 on the way count: a program that leaves them out, or rounds other values in their place, can miss the bound.
Values may be sent and summed in bfloat16 or wider, within the bound.
No kernel may reach another device: no remote copies, remote signals or barrier semaphores. Data moves between devices by JAX's collectives and lax.ppermute only.
A program may use at most 128 MiB of HBM per device.

```python
import math
import jax
import jax.numpy as jnp
import numpy as np
from jax import lax

D = 768
HEADS = 12
FF = 3072
NB = 32
FEAT = 256
SEQ = 512
STEP = 10
W_DEV = 2
HD = 64
WINDOWS = 32
TOKENS = 16384
FLAT = 3643392
N_DP = 16
N_TENSOR = 2


def place_ends(drawn, own_key, smallest, high):
    longest = drawn.shape.index(max(drawn.shape))
    spots = []
    for shift in (0, 1):
        where = [jax.random.randint(jax.random.fold_in(own_key, axis), (), 0, length) for axis, length in enumerate(drawn.shape)]
        where[longest] = (where[longest] + shift) % drawn.shape[longest]
        spots.append(tuple(where))
    return drawn.at[spots[0]].set(smallest).at[spots[1]].set(high)


def shard_levels(stream_key, dims, split, smallest, high):
    def one(axis_at, parts):
        heights = jax.random.uniform(jax.random.fold_in(jax.random.fold_in(stream_key, 6), axis_at), (parts,), jnp.float32, smallest / len(split), high / len(split))
        return jnp.repeat(jnp.exp(heights), dims[axis_at] // parts).reshape((-1,) + (1,) * (len(dims) - axis_at - 1))

    loudness = one(*split[0])
    for cut in split[1:]:
        loudness = loudness * one(*cut)
    return loudness


def profile(number_of, total, reach, skew):
    portions = [(1 << 20) // math.isqrt(rank ** skew) + 1 for rank in range(2, number_of + 1)]
    rest, given = total - reach - (number_of - 1), [1] * (number_of - 1)
    while rest > 0:
        free = [i for i in range(number_of - 1) if given[i] < reach]
        mass, budget = sum([portions[i] for i in free]), rest
        for i in free:
            extra = min(reach - given[i], max(1, budget * portions[i] // mass), rest)
            given[i] = given[i] + extra
            rest = rest - extra
    return np.array([reach] + given)


def uneven_parts(key, number_of, total, reach, slope):
    if number_of == 2:
        one = jax.random.randint(key, (), max(1, total - reach), min(reach, total - 1) + 1)
        return jnp.stack([one, total - one])
    tallies = jnp.asarray(profile(number_of, total, reach, slope), jnp.int32)
    twos = (number_of - 1) // 2
    donor, sink = tallies[1:1 + 2 * twos:2], tallies[2:2 + 2 * twos:2]
    room = jnp.minimum(donor - 1, reach - sink)
    moved = jax.random.randint(jax.random.fold_in(key, 1), (twos,), 0, 1 << 20) % (room + 1)
    tallies = tallies.at[1:1 + 2 * twos:2].set(donor - moved).at[2:2 + 2 * twos:2].set(sink + moved)
    return tallies[jax.random.permutation(jax.random.fold_in(key, 2), number_of)]


def scatter_about(own_key, extent, scale, reach, shards=(), held_as=jnp.bfloat16):
    factor_of = shard_levels(own_key, extent, shards, -0.22, 0.18) if shards else 1.0
    drawn = jax.random.normal(own_key, extent, jnp.float32) * scale * factor_of
    return jnp.minimum(jnp.maximum(drawn, -reach), reach).astype(held_as)


def setup_inputs(seed: int = 0) -> dict:
    streams_of = jax.random.split(jax.random.key(seed), 21)
    hidden_in = scatter_about(streams_of[0], (TOKENS, D), 1.0, 6.0, ((0, 32),))
    cotangent = scatter_about(streams_of[1], (TOKENS, D), 1.0, 6.0, ((0, 32),))
    box_coords = place_ends(jax.random.randint(streams_of[2], (4, TOKENS), 0, 1000), jax.random.fold_in(streams_of[2], 1), 0, 999).astype(jnp.int32)
    doc_ids = jax.vmap(lambda own: jnp.searchsorted(jnp.cumsum(uneven_parts(own, 8, SEQ, SEQ // 4, 2)), jnp.arange(SEQ), side="right"))(jax.random.split(streams_of[3], WINDOWS)).reshape((WINDOWS, SEQ)).astype(jnp.int32)
    buckets = place_ends(jax.random.randint(streams_of[4], (2, WINDOWS, SEQ, SEQ), 0, NB), jax.random.fold_in(streams_of[4], 1), 0, NB - 1).astype(jnp.int32)
    layout_weight = scatter_about(streams_of[5], (FEAT, D), FEAT ** -0.5, 0.375)
    norm_gains = jnp.clip(1.0 + 0.1 * jax.random.normal(streams_of[6], (2, D), jnp.float32), 0.5, 1.5).astype(jnp.bfloat16)
    norm_shifts = scatter_about(streams_of[7], (2, D), 0.5, 3.0)
    branch_biases = scatter_about(streams_of[8], (2, D), 0.5, 3.0)
    qkv_weight = scatter_about(streams_of[9], (3, D, D), D ** -0.5, 0.21875, ((2, 2),))
    query_value_bias = scatter_about(streams_of[10], (2, D), 0.5, 3.0, ((1, 2),))
    output_weight = scatter_about(streams_of[11], (D, D), (D // 32) ** -0.5, 1.25, ((0, 2),))
    ffn_in_weight = scatter_about(streams_of[12], (D, FF), D ** -0.5, 0.21875, ((1, 2),))
    ffn_in_bias = scatter_about(streams_of[13], (FF,), 0.5, 3.0, ((0, 2),))
    ffn_out_weight = scatter_about(streams_of[14], (FF, D), (FF // 2) ** -0.5, 0.15625, ((0, 2),))
    relative_table = scatter_about(streams_of[15], (2, NB, HEADS), 1.0, 4.0, ((2, 2),))
    master_flat = scatter_about(streams_of[16], (N_TENSOR, FLAT), 0.03, 0.18, ((0, 2), (1, 16)), jnp.float32)
    moment_one = scatter_about(streams_of[17], (N_TENSOR, FLAT), 0.00004, 0.00024, ((0, 2), (1, 16)), jnp.float32)
    moment_two = jnp.clip(jnp.exp(math.log(4.999999858590343e-10) - 3.218876 * jax.random.uniform(streams_of[18], (N_TENSOR, FLAT), jnp.float32) ** shard_levels(streams_of[18], (N_TENSOR, FLAT), ((0, 2), (1, 16)), -0.2, 0.2)), 1.9999999920083944e-11, 4.999999858590343e-10)
    ema_flat = scatter_about(streams_of[19], (N_TENSOR, FLAT), 0.03, 0.18, ((0, 2), (1, 16)), jnp.float32)
    return {"hidden_in": hidden_in, "cotangent": cotangent, "box_coords": box_coords, "doc_ids": doc_ids, "buckets": buckets, "layout_weight": layout_weight, "norm_gains": norm_gains, "norm_shifts": norm_shifts, "branch_biases": branch_biases, "qkv_weight": qkv_weight, "query_value_bias": query_value_bias, "output_weight": output_weight, "ffn_in_weight": ffn_in_weight, "ffn_in_bias": ffn_in_bias, "ffn_out_weight": ffn_out_weight, "relative_table": relative_table, "master_flat": master_flat, "moment_one": moment_one, "moment_two": moment_two, "ema_flat": ema_flat}


@jax.custom_vjp
def low(v):
    return lax.optimization_barrier(v.astype(jnp.bfloat16)).astype(jnp.float32)

@jax.custom_vjp
def low_back(v):
    return v

def low_keep(v):
    return (low(v), None)

def low_pass(kept, grad):
    return (grad,)

def back_keep(v):
    return (v, None)

def back_low(kept, grad):
    return (low(grad),)
low.defvjp(low_keep, low_pass)
low_back.defvjp(back_keep, back_low)
norm_eps = 1e-05
learn_rate = 0.02
beta_one = 0.9
beta_two = 0.999
adam_eps = 1e-08
decay_rate = 0.01
average_rate = 0.5
clip_limit = 1.0
mask_fill = -1e+30

def highest(left, right):
    return jnp.dot(left, right, precision=lax.Precision.HIGHEST)

def layer_norm(value, gain, shift):
    centre = value - lax.optimization_barrier(jnp.mean(value, axis=-1, keepdims=True))
    spread = lax.optimization_barrier(jnp.mean(centre * centre, axis=-1, keepdims=True))
    return centre * lax.rsqrt(spread + norm_eps) * gain + shift

def box_features(coords):
    count = FEAT // 8
    freqs = jnp.exp(-math.log(10000.0) * jnp.arange(count, dtype=jnp.float32) / count)
    angles = coords.astype(jnp.float32)[:, None, :] * freqs[None, :, None]
    waves = jnp.stack([jnp.sin(angles), jnp.cos(angles)], axis=1)
    return waves.reshape(FEAT, coords.shape[1])

def window_attention(query_win, keys_win, values_win, doc_win, bucket_win, bias_lookup):
    raw_scores = low_back(jnp.einsum('qhd,khd->hqk', query_win, keys_win, precision=lax.Precision.HIGHEST))
    bucket_codes = jnp.arange(NB, dtype=jnp.int32)
    pairwise_bias = jnp.zeros(raw_scores.shape, jnp.float32)
    for selector_index in range(2):
        indicator_matrix = (bucket_win[selector_index][None, :, :] == bucket_codes[:, None, None]).astype(jnp.float32)
        pairwise_bias = pairwise_bias + jnp.einsum('zta,zo->ota', indicator_matrix, bias_lookup[selector_index], precision=lax.Precision.HIGHEST)
    scores = raw_scores * (1.0 / math.sqrt(HD)) + pairwise_bias
    same_doc = doc_win[:, None] == doc_win[None, :]
    scores = jnp.where(same_doc[None], scores, mask_fill)
    probs = jax.nn.softmax(scores, axis=-1)
    return jnp.einsum('hqk,khd->qhd', low(probs), values_win, precision=lax.Precision.HIGHEST)

def forward(params, hidden_group, coords, doc_group, bucket_group):
    layout_weight, norm_gains, norm_shifts, branch_biases, qkv_weight, query_value_bias, output_weight, ffn_in_weight, ffn_in_bias, ffn_out_weight, relative_table = params
    rows = hidden_group.shape[0]
    features = low(box_features(coords).T)
    embedded = hidden_group + highest(features, layout_weight)
    inputs = low(embedded)
    query = low(low_back(highest(inputs, qkv_weight[0]) + query_value_bias[0]))
    keys = low(low_back(highest(inputs, qkv_weight[1])))
    values = low(low_back(highest(inputs, qkv_weight[2]) + query_value_bias[1]))
    shape4 = (W_DEV, SEQ, HEADS, HD)

    def per_window(packed):
        return window_attention(packed[0], packed[1], packed[2], packed[3], packed[4], relative_table)
    mixed = lax.map(jax.checkpoint(per_window), (query.reshape(shape4), keys.reshape(shape4), values.reshape(shape4), doc_group, bucket_group))
    context = low(low_back(mixed.reshape(rows, D)))
    attn_out = low_back(highest(context, output_weight)) + branch_biases[0]
    mid = layer_norm(embedded + attn_out, norm_gains[0], norm_shifts[0])
    hidden_pre = low_back(highest(low(mid), ffn_in_weight) + ffn_in_bias)
    hidden = low(jax.nn.gelu(hidden_pre, approximate=False))
    branch = low_back(highest(hidden, ffn_out_weight)) + branch_biases[1]
    return layer_norm(mid + branch, norm_gains[1], norm_shifts[1])

def tensor_piece(array, dim, index):
    width = array.shape[dim] // N_TENSOR
    return lax.slice_in_dim(array, index * width, (index + 1) * width, axis=dim).reshape(-1)

def reference(hidden_in, cotangent, box_coords, doc_ids, buckets, layout_weight, norm_gains, norm_shifts, branch_biases, qkv_weight, query_value_bias, output_weight, ffn_in_weight, ffn_in_bias, ffn_out_weight, relative_table, master_flat, moment_one, moment_two, ema_flat):
    params = tuple((p.astype(jnp.float32) for p in (layout_weight, norm_gains, norm_shifts, branch_biases, qkv_weight, query_value_bias, output_weight, ffn_in_weight, ffn_in_bias, ffn_out_weight, relative_table)))
    rows = W_DEV * SEQ
    groups = N_DP
    hidden_groups = hidden_in.astype(jnp.float32).reshape(groups, rows, D)
    cot_groups = cotangent.astype(jnp.float32).reshape(groups, rows, D)
    coord_groups = jnp.transpose(box_coords.reshape(4, groups, rows), (1, 0, 2))
    doc_groups = doc_ids.reshape(groups, W_DEV, SEQ)
    bucket_groups = jnp.transpose(buckets.reshape(2, groups, W_DEV, SEQ, SEQ), (1, 2, 0, 3, 4))

    def one_group(totals, packed):
        hidden_group, cot_group, coords, doc_group, bucket_group = packed
        result, pullback = jax.vjp(lambda weights, value: forward(weights, value, coords, doc_group, bucket_group), params, hidden_group)
        weight_grads, value_grad = pullback(cot_group)
        totals = jax.tree.map(jnp.add, totals, weight_grads)
        return (totals, (result.astype(jnp.bfloat16), value_grad))
    zeros = jax.tree.map(jnp.zeros_like, params)
    grads, (outputs, input_grads) = lax.scan(one_group, zeros, (hidden_groups, cot_groups, coord_groups, doc_groups, bucket_groups))
    layout_grad, gains_grad, shifts_grad, biases_grad, qkv_grad, qv_bias_grad, output_grad, ffn_in_grad, ffn_bias_grad, ffn_out_grad, table_grad = grads
    shared = jnp.concatenate([layout_grad.reshape(-1), gains_grad.reshape(-1), shifts_grad.reshape(-1), biases_grad.reshape(-1)])
    half_len = shared.shape[0] // N_TENSOR
    flat_rows = []
    for index in range(N_TENSOR):
        pieces = [tensor_piece(ffn_in_grad, 1, index), tensor_piece(ffn_bias_grad, 0, index), tensor_piece(ffn_out_grad, 0, index), tensor_piece(qkv_grad, 2, index), tensor_piece(qv_bias_grad, 1, index), tensor_piece(output_grad, 0, index), tensor_piece(table_grad, 2, index), shared[index * half_len:(index + 1) * half_len]]
        joined = jnp.concatenate(pieces)
        flat_rows.append(jnp.concatenate([joined, jnp.zeros((FLAT - joined.shape[0],), jnp.float32)]))
    grad_flat = jnp.stack(flat_rows)
    grad_norm = jnp.sqrt(jnp.sum(grad_flat * grad_flat))
    clipped = grad_flat * (clip_limit / jnp.maximum(grad_norm, clip_limit))
    new_moment_one = beta_one * moment_one + (1.0 - beta_one) * clipped
    new_moment_two = beta_two * moment_two + (1.0 - beta_two) * clipped * clipped
    step_size = new_moment_one / (1.0 - beta_one ** STEP) / (jnp.sqrt(new_moment_two / (1.0 - beta_two ** STEP)) + adam_eps)
    new_master = master_flat - learn_rate * (step_size + decay_rate * master_flat)
    new_ema = average_rate * ema_flat + (1.0 - average_rate) * new_master
    return (outputs.reshape(TOKENS, D), input_grads.reshape(TOKENS, D), layout_grad, gains_grad, shifts_grad, biases_grad, qkv_grad, qv_bias_grad, output_grad, ffn_in_grad, ffn_bias_grad, ffn_out_grad, table_grad, grad_norm, new_master, new_moment_one, new_moment_two, new_ema, new_master.astype(jnp.bfloat16))
```

```python
from functools import partial
import math

import jax
import jax.numpy as jnp
from jax import lax
from jax.experimental import pallas as pl
from jax.experimental.pallas import tpu as pltpu
from jax.sharding import PartitionSpec as P

NB = 32
FEAT = 256
STEP = 10
BLOCK = 128


norm_eps = 1e-05
learn_rate = 0.02
beta_one = 0.9
beta_two = 0.999
adam_eps = 1e-08
decay_rate = 0.01
average_rate = 0.5
clip_limit = 1.0
mask_fill = -1e30

F32 = jnp.float32
BF16 = jnp.bfloat16
NT = (((1,), (1,)), ((), ()))
TN = (((0,), (0,)), ((), ()))


def dot(left, right):
    return jnp.dot(left, right, preferred_element_type=F32)


def dot_nt(left, right):
    return lax.dot_general(left, right, NT, preferred_element_type=F32)


def dot_tn(left, right):
    return lax.dot_general(left, right, TN, preferred_element_type=F32)


def box_features(coords):
    count = FEAT // 8
    freqs = jnp.exp(-math.log(10000.0) * jnp.arange(count, dtype=F32) / count)
    angles = coords.astype(F32)[:, None, :] * freqs[None, :, None]
    waves = jnp.stack([jnp.sin(angles), jnp.cos(angles)], axis=1)
    return waves.reshape(FEAT, coords.shape[1])


def normalize(value):
    centre = value - jnp.mean(value, axis=-1, keepdims=True)
    inv_std = lax.rsqrt(jnp.mean(centre * centre, axis=-1, keepdims=True) + norm_eps)
    return (centre * inv_std, inv_std)


def norm_back(grad_out, normed, inv_std, gain):
    scaled = grad_out * gain
    return inv_std * (
        scaled
        - jnp.mean(scaled, axis=-1, keepdims=True)
        - normed * jnp.mean(scaled * normed, axis=-1, keepdims=True)
    )


def attend(which, qkv, docs, buckets, table):
    _, rows, width = qkv.shape
    nb, heads = table.shape[1:]
    pairs = heads // 2
    half = width // heads
    span = 3 * BLOCK
    blocks = rows // BLOCK
    scale = 1.0 / math.sqrt(half)
    lookup = jnp.pad(
        jnp.concatenate([table[0], table[1]], axis=0).astype(F32).T,
        ((0, 0), (0, BLOCK - 2 * nb)),
    ).reshape(heads, 1, BLOCK)
    doc_row = docs[:, None, :]
    doc_col = docs[:, :, None]

    def body(which_ref, qkv_ref, dr_ref, dc_ref, b_ref, t_ref, ctx_ref, p_ref):
        block = pl.program_id(0)
        start = pl.multiple_of(jnp.clip(block - 1, 0, blocks - 3) * BLOCK, BLOCK)
        own_rows = pl.ds(pl.multiple_of(block * BLOCK, BLOCK), BLOCK)
        key_rows = pl.ds(start, span)
        same = dc_ref[0] == dr_ref[0, :, key_rows]
        first = b_ref[0, 0, :, key_rows]
        second = b_ref[1, 0, :, key_rows] + nb
        low_lane = lax.broadcasted_iota(jnp.int32, (BLOCK, 2 * half), 1) < half

        def one_pair(p, carry):
            cols = pl.ds(pl.multiple_of(p * 2 * half, 2 * half), 2 * half)
            q2 = qkv_ref[0, own_rows, cols]
            k2 = qkv_ref[1, key_rows, cols]
            v2 = qkv_ref[2, key_rows, cols]
            outs = []
            for e in range(2):
                qm = jnp.where(low_lane == (e == 0), q2, jnp.zeros_like(q2))
                raw = dot_nt(qm, k2)
                trow = jnp.broadcast_to(t_ref[2 * p + e], (BLOCK, BLOCK))
                bias = jnp.concatenate(
                    [
                        jnp.take_along_axis(
                            trow, first[:, c : c + BLOCK], axis=1, mode="promise_in_bounds"
                        )
                        + jnp.take_along_axis(
                            trow, second[:, c : c + BLOCK], axis=1, mode="promise_in_bounds"
                        )
                        for c in range(0, span, BLOCK)
                    ],
                    axis=1,
                )
                scores = jnp.where(same, raw * scale + bias, mask_fill)
                top = jnp.max(scores, axis=1, keepdims=True)
                weights = jnp.exp(scores - top)
                probs = weights * (1.0 / jnp.sum(weights, axis=1, keepdims=True))
                p_ref[2 * p + e, 0] = probs
                outs.append(dot(probs.astype(BF16), v2))
            ctx_ref[:, cols] = jnp.where(low_lane, outs[0], outs[1]).astype(BF16)
            return carry

        lax.fori_loop(0, pairs, one_pair, 0, unroll=True)

    return pl.pallas_call(
        body,
        grid_spec=pltpu.PrefetchScalarGridSpec(
            num_scalar_prefetch=1,
            grid=(blocks,),
            in_specs=[
                pl.BlockSpec((3, rows, width), lambda i, w: (0, 0, 0)),
                pl.BlockSpec((1, 1, rows), lambda i, w: (w[0], 0, 0)),
                pl.BlockSpec((1, BLOCK, 1), lambda i, w: (w[0], i, 0)),
                pl.BlockSpec((2, 1, BLOCK, rows), lambda i, w: (0, w[0], i, 0)),
                pl.BlockSpec((heads, 1, BLOCK), lambda i, w: (0, 0, 0)),
            ],
            out_specs=[
                pl.BlockSpec((BLOCK, width), lambda i, w: (i, 0)),
                pl.BlockSpec((heads, 1, BLOCK, span), lambda i, w: (0, i, 0, 0)),
            ],
        ),
        out_shape=[
            jax.ShapeDtypeStruct((rows, width), BF16),
            jax.ShapeDtypeStruct((heads, blocks, BLOCK, span), F32),
        ],
        name="attend",
    )(which, qkv, doc_row, doc_col, buckets, lookup)


def attend_back(which, qkvs, grads, probs, buckets, nb):
    _, rows, width = qkvs[0].shape
    heads, blocks, _, span = probs[0].shape
    pairs = heads // 2
    half = width // heads
    scale = 1.0 / math.sqrt(half)
    group = 8
    codes = 2 * nb
    lanes = 2 * 2 * heads * group

    def body(
        which_ref, qkv_a, qkv_b, g_a, g_b, p_a, p_b, b_ref, d_a, d_b, tab_ref, gs_ref, acc_a, acc_b, acc_ref
    ):
        block = pl.program_id(0)
        start = pl.multiple_of(jnp.clip(block - 1, 0, blocks - 3) * BLOCK, BLOCK)
        own_rows = pl.ds(pl.multiple_of(block * BLOCK, BLOCK), BLOCK)
        key_rows = pl.ds(start, span)
        low_lane = lax.broadcasted_iota(jnp.int32, (BLOCK, 2 * half), 1) < half

        @pl.when(block == 0)
        def _():
            acc_a[...] = jnp.zeros_like(acc_a)
            acc_b[...] = jnp.zeros_like(acc_b)
            acc_ref[...] = jnp.zeros_like(acc_ref)

        for side, (qkv_ref, g_ref, p_ref, d_ref, sums) in enumerate(
            ((qkv_a, g_a, p_a, d_a, acc_a), (qkv_b, g_b, p_b, d_b, acc_b))
        ):

            def one_pair(p, carry):
                cols = pl.ds(pl.multiple_of(p * 2 * half, 2 * half), 2 * half)
                q2 = qkv_ref[0, own_rows, cols]
                g2 = g_ref[:, cols]
                k2 = qkv_ref[1, key_rows, cols]
                v2 = qkv_ref[2, key_rows, cols]
                dqs = []
                dk = sums[0, key_rows, cols]
                dv = sums[1, key_rows, cols]
                for e in range(2):
                    mine = low_lane == (e == 0)
                    qm = jnp.where(mine, q2, jnp.zeros_like(q2))
                    gm = jnp.where(mine, g2, jnp.zeros_like(g2))
                    pr = p_ref[2 * p + e, 0]
                    gp = dot_nt(gm, v2)
                    gs = pr * (gp - jnp.sum(pr * gp, axis=1, keepdims=True))
                    gs_ref[side * heads + 2 * p + e] = gs
                    raw = (gs * scale).astype(BF16)
                    dqs.append(dot(raw, k2))
                    dk = dk + dot_tn(raw, qm)
                    dv = dv + dot_tn(pr.astype(BF16), gm)
                d_ref[0, own_rows, cols] = jnp.where(low_lane, dqs[0], dqs[1]).astype(BF16)
                sums[0, key_rows, cols] = dk
                sums[1, key_rows, cols] = dv
                return carry

            lax.fori_loop(0, pairs, one_pair, 0, unroll=True)

        code_ids = lax.broadcasted_iota(jnp.int32, (nb, span), 0)

        def one_group(g, carry):
            r8 = pl.ds(pl.multiple_of(g * group, group), group)
            b0 = b_ref[0, 0, r8, key_rows]
            b1 = b_ref[1, 0, r8, key_rows]
            pieces = []
            for r in range(group):
                for b in (b0, b1):
                    row = jnp.broadcast_to(b[r : r + 1], (nb, span))
                    pieces.append(jnp.where(row == code_ids, 1.0, 0.0).astype(BF16))
            onehot = jnp.concatenate(pieces, axis=0)
            gg = gs_ref[:, r8, :].reshape(2 * heads * group, span)
            upper = gg.astype(BF16)
            lower = (gg - upper.astype(F32)).astype(BF16)
            both = jnp.concatenate([upper, lower], axis=0)
            acc_ref[...] += dot_nt(onehot, both)
            return carry

        lax.fori_loop(0, BLOCK // group, one_group, 0)

        @pl.when(block == blocks - 1)
        def _():
            for d_ref, sums in ((d_a, acc_a), (d_b, acc_b)):
                d_ref[1] = sums[0].astype(BF16)
                d_ref[2] = sums[1].astype(BF16)
            lane_row = lax.broadcasted_iota(jnp.int32, (codes, lanes), 1) % group
            total = jnp.zeros((codes, lanes), F32)
            for r in range(group):
                total = total + jnp.where(
                    lane_row == r, acc_ref[r * codes : (r + 1) * codes, :], 0.0
                )
            tab_ref[...] = total

    whole = pl.BlockSpec((3, rows, width), lambda i, w: (0, 0, 0))
    part = pl.BlockSpec((BLOCK, width), lambda i, w: (i, 0))
    prob = pl.BlockSpec((heads, 1, BLOCK, span), lambda i, w: (0, i, 0, 0))
    shape = jax.ShapeDtypeStruct((3, rows, width), BF16)
    d_a, d_b, tab = pl.pallas_call(
        body,
        grid_spec=pltpu.PrefetchScalarGridSpec(
            num_scalar_prefetch=1,
            grid=(blocks,),
            in_specs=[
                whole, whole, part, part, prob, prob,
                pl.BlockSpec((2, 1, BLOCK, rows), lambda i, w: (0, w[0], i, 0)),
            ],
            out_specs=[whole, whole, pl.BlockSpec((codes, lanes), lambda i, w: (0, 0))],
            scratch_shapes=[
                pltpu.VMEM((2 * heads, BLOCK, span), F32),
                pltpu.VMEM((2, rows, width), F32),
                pltpu.VMEM((2, rows, width), F32),
                pltpu.VMEM((group * codes, lanes), F32),
            ],
        ),
        out_shape=[shape, shape, jax.ShapeDtypeStruct((codes, lanes), F32)],
        name="attend_back",
    )(which, *qkvs, *grads, *probs, buckets)
    total = tab.reshape(2, nb, 2, 2, heads, group).sum(axis=(2, 5))
    return d_a, d_b, total[:, :, 0], total[:, :, 1]


def swap(value):
    size = lax.axis_size("tensor")
    return lax.ppermute(value, "tensor", [(i, (i + 1) % size) for i in range(size)])


def per_device(
    hidden_in,
    cotangent,
    box_coords,
    doc_ids,
    buckets,
    layout_weight,
    norm_gains,
    norm_shifts,
    branch_biases,
    qkv_weight,
    query_value_bias,
    output_weight,
    ffn_in_weight,
    ffn_in_bias,
    ffn_out_weight,
    relative_table,
    master_flat,
    moment_one,
    moment_two,
    ema_flat,
):
    turn = lax.axis_index("tensor")
    window = turn.astype(jnp.int32).reshape(1)
    gains = norm_gains.astype(F32)
    norm_offsets = norm_shifts.astype(F32)
    biases = branch_biases.astype(F32)

    small_own = jnp.concatenate(
        [query_value_bias.reshape(-1), ffn_in_bias, relative_table.reshape(-1)]
    )
    qkv_other = swap(qkv_weight)
    small_other = swap(small_own)
    output_other = swap(output_weight)
    ffn_in_other = swap(ffn_in_weight)
    ffn_out_other = swap(ffn_out_weight)
    cuts = (query_value_bias.size, query_value_bias.size + ffn_in_bias.size)
    qv_bias_other = small_other[: cuts[0]].reshape(query_value_bias.shape)
    ffn_bias_other = small_other[cuts[0] : cuts[1]]
    table_other = small_other[cuts[1] :].reshape(relative_table.shape)

    features = box_features(box_coords).astype(BF16)
    embedded = hidden_in.astype(F32) + dot_tn(features, layout_weight)
    inputs = embedded.astype(BF16)
    inputs_swap = swap(inputs)

    def project(weight, bias):
        shift = jnp.stack([bias[0], jnp.zeros_like(bias[0]), bias[1]]).astype(F32)
        projected = jnp.einsum("rd,cde->cre", inputs, weight, preferred_element_type=F32)
        return (projected + shift[:, None, :]).astype(BF16)

    qkv_a = project(qkv_weight, query_value_bias)
    context_a, probs_a = attend(window, qkv_a, doc_ids, buckets, relative_table)
    qkv_b = project(qkv_other, qv_bias_other)
    context_b, probs_b = attend(window, qkv_b, doc_ids, buckets, table_other)
    context_swap = swap(context_b)
    attn_out = dot(context_a, output_weight) + dot(context_b, output_other) + biases[0]
    normed_one, inv_std_one = normalize(embedded + attn_out)
    mid_norm = normed_one * gains[0] + norm_offsets[0]
    mid_low = mid_norm.astype(BF16)
    mid_swap = swap(mid_low)

    gelu = partial(jax.nn.gelu, approximate=False)

    def expand(weight, bias):
        pre = dot(mid_low, weight) + bias.astype(F32)
        hidden, back = jax.vjp(gelu, pre)
        return hidden.astype(BF16), back

    hidden_a, gelu_back_a = expand(ffn_in_weight, ffn_in_bias)
    hidden_b, gelu_back_b = expand(ffn_in_other, ffn_bias_other)
    hidden_swap = swap(hidden_b)
    branch = dot(hidden_a, ffn_out_weight) + dot(hidden_b, ffn_out_other) + biases[1]
    normed_two, inv_std_two = normalize(mid_norm + branch)
    hidden_out = (normed_two * gains[1] + norm_offsets[1]).astype(BF16)
    grad_out = cotangent.astype(F32)
    gain_two = jnp.sum(grad_out * normed_two, axis=0)
    shift_two = jnp.sum(grad_out, axis=0)
    grad_sum_two = norm_back(grad_out, normed_two, inv_std_two, gains[1])
    bias_two = jnp.sum(grad_sum_two, axis=0)
    grad_branch = grad_sum_two.astype(BF16)
    grad_branch_swap = swap(grad_branch)

    grad_pre_b = gelu_back_b(dot_nt(grad_branch, ffn_out_other))[0].astype(BF16)
    grad_pre_swap = swap(grad_pre_b)
    grad_pre_a = gelu_back_a(dot_nt(grad_branch, ffn_out_weight))[0].astype(BF16)
    ffn_out_grad = dot_tn(hidden_a, grad_branch) + dot_tn(hidden_swap, grad_branch_swap)
    ffn_in_grad = dot_tn(mid_low, grad_pre_a) + dot_tn(mid_swap, grad_pre_swap)
    ffn_bias_grad = jnp.sum(grad_pre_a.astype(F32), axis=0) + jnp.sum(
        grad_pre_swap.astype(F32), axis=0
    )
    grad_mid = (
        grad_sum_two + dot_nt(grad_pre_a, ffn_in_weight) + dot_nt(grad_pre_b, ffn_in_other)
    )
    gain_one = jnp.sum(grad_mid * normed_one, axis=0)
    shift_one = jnp.sum(grad_mid, axis=0)
    grad_sum_one = norm_back(grad_mid, normed_one, inv_std_one, gains[0])
    bias_one = jnp.sum(grad_sum_one, axis=0)
    grad_attn = grad_sum_one.astype(BF16)
    grad_attn_swap = swap(grad_attn)
    output_grad = dot_tn(context_a, grad_attn) + dot_tn(context_swap, grad_attn_swap)
    grad_context_a = dot_nt(grad_attn, output_weight).astype(BF16)
    grad_context_b = dot_nt(grad_attn, output_other).astype(BF16)

    grads_a, grads_b, table_a, table_b = attend_back(
        window, (qkv_a, qkv_b), (grad_context_a, grad_context_b), (probs_a, probs_b), buckets, NB
    )
    grads_swap = swap(grads_b)
    table_grad = table_a + swap(table_b)
    qv_bias_grad = jnp.stack(
        [
            jnp.sum(grads_a[c].astype(F32), axis=0) + jnp.sum(grads_swap[c].astype(F32), axis=0)
            for c in (0, 2)
        ]
    )
    qkv_grad = jnp.einsum(
        "rd,cre->cde", inputs, grads_a, preferred_element_type=F32
    ) + jnp.einsum("rd,cre->cde", inputs_swap, grads_swap, preferred_element_type=F32)
    input_grad = (
        grad_sum_one
        + jnp.einsum("cre,cde->rd", grads_a, qkv_weight, preferred_element_type=F32)
        + jnp.einsum("cre,cde->rd", grads_b, qkv_other, preferred_element_type=F32)
    )
    layout_part = dot(features, input_grad.astype(BF16))

    def total(value):
        share = lax.psum_scatter(value.astype(BF16), "dp", scatter_dimension=0, tiled=True)
        return lax.all_gather(share, "dp", axis=0, tiled=True).astype(F32)

    shared = lax.psum(
        (
            layout_part,
            jnp.stack([gain_one, gain_two]),
            jnp.stack([shift_one, shift_two]),
            jnp.stack([bias_one, bias_two]),
        ),
        ("dp", "tensor"),
    )
    ffn_bias_grad, qv_bias_grad, table_grad = lax.psum(
        (ffn_bias_grad, qv_bias_grad, table_grad), "dp"
    )
    totals = (
        total(ffn_in_grad),
        ffn_bias_grad,
        total(ffn_out_grad),
        total(qkv_grad.reshape(-1, qkv_grad.shape[2])).reshape(qkv_grad.shape),
        qv_bias_grad,
        total(output_grad),
        table_grad,
    )
    shared_flat = jnp.concatenate([member.reshape(-1) for member in shared])
    half_len = shared_flat.shape[0] // lax.axis_size("tensor")
    own_shared = lax.dynamic_slice_in_dim(shared_flat, turn * half_len, half_len, 0)
    split_flat = jnp.concatenate([member.reshape(-1) for member in totals])
    share_len = master_flat.shape[1]
    flat_len = share_len * lax.axis_size("dp")
    flat_row = jnp.concatenate(
        [
            split_flat,
            own_shared,
            jnp.zeros((flat_len - split_flat.shape[0] - half_len,), F32),
        ]
    )
    square_total = lax.psum(jnp.sum(flat_row * flat_row), "tensor")
    grad_norm = jnp.sqrt(square_total)
    clip_factor = clip_limit / jnp.maximum(grad_norm, clip_limit)
    own_part = (
        lax.dynamic_slice_in_dim(flat_row, lax.axis_index("dp") * share_len, share_len, 0)[None, :]
        * clip_factor
    )
    new_moment_one = beta_one * moment_one + (1.0 - beta_one) * own_part
    new_moment_two = beta_two * moment_two + (1.0 - beta_two) * own_part * own_part
    step_size = (
        new_moment_one
        / (1.0 - beta_one**STEP)
        / (jnp.sqrt(new_moment_two / (1.0 - beta_two**STEP)) + adam_eps)
    )
    new_master = master_flat - learn_rate * (step_size + decay_rate * master_flat)
    new_ema = average_rate * ema_flat + (1.0 - average_rate) * new_master
    return (
        hidden_out,
        input_grad,
        shared[0],
        shared[1],
        shared[2],
        shared[3],
        totals[3],
        totals[4],
        totals[5],
        totals[0],
        totals[1],
        totals[2],
        totals[6],
        grad_norm,
        new_master,
        new_moment_one,
        new_moment_two,
        new_ema,
        new_master.astype(BF16),
    )


def solution(mesh):
    return jax.shard_map(
        per_device,
        mesh=mesh,
        in_specs=(
            P(("dp", "tensor"), None),
            P(("dp", "tensor"), None),
            P(None, ("dp", "tensor")),
            P("dp", None),
            P(None, "dp", None, None),
            P(),
            P(),
            P(),
            P(),
            P(None, None, "tensor"),
            P(None, "tensor"),
            P("tensor", None),
            P(None, "tensor"),
            P("tensor"),
            P("tensor", None),
            P(None, None, "tensor"),
            P("tensor", "dp"),
            P("tensor", "dp"),
            P("tensor", "dp"),
            P("tensor", "dp"),
        ),
        out_specs=(
            P(("dp", "tensor"), None),
            P(("dp", "tensor"), None),
            P(),
            P(),
            P(),
            P(),
            P(None, None, "tensor"),
            P(None, "tensor"),
            P("tensor", None),
            P(None, "tensor"),
            P("tensor"),
            P("tensor", None),
            P(None, None, "tensor"),
            P(),
            P("tensor", "dp"),
            P("tensor", "dp"),
            P("tensor", "dp"),
            P("tensor", "dp"),
            P("tensor", "dp"),
        ),
        check_vma=False,
    )
```

```python
from functools import partial
import math

import jax
import jax.numpy as jnp
from jax import lax
from jax.experimental import pallas as pl
from jax.experimental.pallas import tpu as pltpu
from jax.sharding import PartitionSpec as P

NB = 32
FEAT = 256
STEP = 10
BLOCK = 128


norm_eps = 1e-05
learn_rate = 0.02
beta_one = 0.9
beta_two = 0.999
adam_eps = 1e-08
decay_rate = 0.01
average_rate = 0.5
clip_limit = 1.0
mask_fill = -1e30

F32 = jnp.float32
BF16 = jnp.bfloat16
NT = (((1,), (1,)), ((), ()))
TN = (((0,), (0,)), ((), ()))


def dot(left, right):
    return jnp.dot(left, right, preferred_element_type=F32)


def dot_nt(left, right):
    return lax.dot_general(left, right, NT, preferred_element_type=F32)


def dot_tn(left, right):
    return lax.dot_general(left, right, TN, preferred_element_type=F32)


def box_features(coords):
    count = FEAT // 8
    freqs = jnp.exp(-math.log(10000.0) * jnp.arange(count, dtype=F32) / count)
    angles = coords.astype(F32)[:, None, :] * freqs[None, :, None]
    waves = jnp.stack([jnp.sin(angles), jnp.cos(angles)], axis=1)
    return waves.reshape(FEAT, coords.shape[1])


def normalize(value):
    centre = value - jnp.mean(value, axis=-1, keepdims=True)
    inv_std = lax.rsqrt(jnp.mean(centre * centre, axis=-1, keepdims=True) + norm_eps)
    return (centre * inv_std, inv_std)


def norm_back(grad_out, normed, inv_std, gain):
    scaled = grad_out * gain
    return inv_std * (
        scaled
        - jnp.mean(scaled, axis=-1, keepdims=True)
        - normed * jnp.mean(scaled * normed, axis=-1, keepdims=True)
    )


def attend(which, qkv, docs, buckets, table):
    _, rows, width = qkv.shape
    nb, heads = table.shape[1:]
    pairs = heads // 2
    half = width // heads
    span = 3 * BLOCK
    blocks = rows // BLOCK
    scale = 1.0 / math.sqrt(half)
    lookup = jnp.pad(
        jnp.concatenate([table[0], table[1]], axis=0).astype(F32).T,
        ((0, 0), (0, BLOCK - 2 * nb)),
    ).reshape(heads, 1, BLOCK)
    doc_row = docs[:, None, :]
    doc_col = docs[:, :, None]

    def body(which_ref, qkv_ref, dr_ref, dc_ref, b_ref, t_ref, ctx_ref, p_ref):
        block = pl.program_id(0)
        start = pl.multiple_of(jnp.clip(block - 1, 0, blocks - 3) * BLOCK, BLOCK)
        own_rows = pl.ds(pl.multiple_of(block * BLOCK, BLOCK), BLOCK)
        key_rows = pl.ds(start, span)
        same = dc_ref[0] == dr_ref[0, :, key_rows]
        first = b_ref[0, 0, :, key_rows]
        second = b_ref[1, 0, :, key_rows] + nb
        low_lane = lax.broadcasted_iota(jnp.int32, (BLOCK, 2 * half), 1) < half

        def one_pair(p, carry):
            cols = pl.ds(pl.multiple_of(p * 2 * half, 2 * half), 2 * half)
            q2 = qkv_ref[0, own_rows, cols]
            k2 = qkv_ref[1, key_rows, cols]
            v2 = qkv_ref[2, key_rows, cols]
            outs = []
            for e in range(2):
                qm = jnp.where(low_lane == (e == 0), q2, jnp.zeros_like(q2))
                raw = dot_nt(qm, k2)
                trow = jnp.broadcast_to(t_ref[2 * p + e], (BLOCK, BLOCK))
                bias = jnp.concatenate(
                    [
                        jnp.take_along_axis(
                            trow, first[:, c : c + BLOCK], axis=1, mode="promise_in_bounds"
                        )
                        + jnp.take_along_axis(
                            trow, second[:, c : c + BLOCK], axis=1, mode="promise_in_bounds"
                        )
                        for c in range(0, span, BLOCK)
                    ],
                    axis=1,
                )
                scores = jnp.where(same, raw * scale + bias, mask_fill)
                top = jnp.max(scores, axis=1, keepdims=True)
                weights = jnp.exp(scores - top)
                probs = weights * (1.0 / jnp.sum(weights, axis=1, keepdims=True))
                p_ref[2 * p + e, 0] = probs
                outs.append(dot(probs.astype(BF16), v2))
            ctx_ref[:, cols] = jnp.where(low_lane, outs[0], outs[1]).astype(BF16)
            return carry

        lax.fori_loop(0, pairs, one_pair, 0, unroll=True)

    return pl.pallas_call(
        body,
        grid_spec=pltpu.PrefetchScalarGridSpec(
            num_scalar_prefetch=1,
            grid=(blocks,),
            in_specs=[
                pl.BlockSpec((3, rows, width), lambda i, w: (0, 0, 0)),
                pl.BlockSpec((1, 1, rows), lambda i, w: (w[0], 0, 0)),
                pl.BlockSpec((1, BLOCK, 1), lambda i, w: (w[0], i, 0)),
                pl.BlockSpec((2, 1, BLOCK, rows), lambda i, w: (0, w[0], i, 0)),
                pl.BlockSpec((heads, 1, BLOCK), lambda i, w: (0, 0, 0)),
            ],
            out_specs=[
                pl.BlockSpec((BLOCK, width), lambda i, w: (i, 0)),
                pl.BlockSpec((heads, 1, BLOCK, span), lambda i, w: (0, i, 0, 0)),
            ],
        ),
        out_shape=[
            jax.ShapeDtypeStruct((rows, width), BF16),
            jax.ShapeDtypeStruct((heads, blocks, BLOCK, span), F32),
        ],
        name="attend",
    )(which, qkv, doc_row, doc_col, buckets, lookup)


def attend_back(which, qkvs, grads, probs, buckets, nb):
    _, rows, width = qkvs[0].shape
    heads, blocks, _, span = probs[0].shape
    pairs = heads // 2
    half = width // heads
    scale = 1.0 / math.sqrt(half)
    group = 8
    codes = 2 * nb
    lanes = 2 * 2 * heads * group

    def body(
        which_ref, qkv_a, qkv_b, g_a, g_b, p_a, p_b, b_ref, d_a, d_b, tab_ref, gs_ref, acc_a, acc_b, acc_ref
    ):
        block = pl.program_id(0)
        start = pl.multiple_of(jnp.clip(block - 1, 0, blocks - 3) * BLOCK, BLOCK)
        own_rows = pl.ds(pl.multiple_of(block * BLOCK, BLOCK), BLOCK)
        key_rows = pl.ds(start, span)
        low_lane = lax.broadcasted_iota(jnp.int32, (BLOCK, 2 * half), 1) < half

        @pl.when(block == 0)
        def _():
            acc_a[...] = jnp.zeros_like(acc_a)
            acc_b[...] = jnp.zeros_like(acc_b)
            acc_ref[...] = jnp.zeros_like(acc_ref)

        for side, (qkv_ref, g_ref, p_ref, d_ref, sums) in enumerate(
            ((qkv_a, g_a, p_a, d_a, acc_a), (qkv_b, g_b, p_b, d_b, acc_b))
        ):

            def one_pair(p, carry):
                cols = pl.ds(pl.multiple_of(p * 2 * half, 2 * half), 2 * half)
                q2 = qkv_ref[0, own_rows, cols]
                g2 = g_ref[:, cols]
                k2 = qkv_ref[1, key_rows, cols]
                v2 = qkv_ref[2, key_rows, cols]
                dqs = []
                dk = sums[0, key_rows, cols]
                dv = sums[1, key_rows, cols]
                for e in range(2):
                    mine = low_lane == (e == 0)
                    qm = jnp.where(mine, q2, jnp.zeros_like(q2))
                    gm = jnp.where(mine, g2, jnp.zeros_like(g2))
                    pr = p_ref[2 * p + e, 0]
                    gp = dot_nt(gm, v2)
                    gs = pr * (gp - jnp.sum(pr * gp, axis=1, keepdims=True))
                    gs_ref[side * heads + 2 * p + e] = gs
                    raw = (gs * scale).astype(BF16)
                    dqs.append(dot(raw, k2))
                    dk = dk + dot_tn(raw, qm)
                    dv = dv + dot_tn(pr.astype(BF16), gm)
                d_ref[0, own_rows, cols] = jnp.where(low_lane, dqs[0], dqs[1]).astype(BF16)
                sums[0, key_rows, cols] = dk
                sums[1, key_rows, cols] = dv
                return carry

            lax.fori_loop(0, pairs, one_pair, 0, unroll=True)

        code_ids = lax.broadcasted_iota(jnp.int32, (nb, span), 0)

        def one_group(g, carry):
            r8 = pl.ds(pl.multiple_of(g * group, group), group)
            b0 = b_ref[0, 0, r8, key_rows]
            b1 = b_ref[1, 0, r8, key_rows]
            pieces = []
            for r in range(group):
                for b in (b0, b1):
                    row = jnp.broadcast_to(b[r : r + 1], (nb, span))
                    pieces.append(jnp.where(row == code_ids, 1.0, 0.0).astype(BF16))
            onehot = jnp.concatenate(pieces, axis=0)
            gg = gs_ref[:, r8, :].reshape(2 * heads * group, span)
            upper = gg.astype(BF16)
            lower = (gg - upper.astype(F32)).astype(BF16)
            both = jnp.concatenate([upper, lower], axis=0)
            acc_ref[...] += dot_nt(onehot, both)
            return carry

        lax.fori_loop(0, BLOCK // group, one_group, 0)

        @pl.when(block == blocks - 1)
        def _():
            for d_ref, sums in ((d_a, acc_a), (d_b, acc_b)):
                d_ref[1] = sums[0].astype(BF16)
                d_ref[2] = sums[1].astype(BF16)
            lane_row = lax.broadcasted_iota(jnp.int32, (codes, lanes), 1) % group
            total = jnp.zeros((codes, lanes), F32)
            for r in range(group):
                total = total + jnp.where(
                    lane_row == r, acc_ref[r * codes : (r + 1) * codes, :], 0.0
                )
            tab_ref[...] = total

    whole = pl.BlockSpec((3, rows, width), lambda i, w: (0, 0, 0))
    part = pl.BlockSpec((BLOCK, width), lambda i, w: (i, 0))
    prob = pl.BlockSpec((heads, 1, BLOCK, span), lambda i, w: (0, i, 0, 0))
    shape = jax.ShapeDtypeStruct((3, rows, width), BF16)
    d_a, d_b, tab = pl.pallas_call(
        body,
        grid_spec=pltpu.PrefetchScalarGridSpec(
            num_scalar_prefetch=1,
            grid=(blocks,),
            in_specs=[
                whole, whole, part, part, prob, prob,
                pl.BlockSpec((2, 1, BLOCK, rows), lambda i, w: (0, w[0], i, 0)),
            ],
            out_specs=[whole, whole, pl.BlockSpec((codes, lanes), lambda i, w: (0, 0))],
            scratch_shapes=[
                pltpu.VMEM((2 * heads, BLOCK, span), F32),
                pltpu.VMEM((2, rows, width), F32),
                pltpu.VMEM((2, rows, width), F32),
                pltpu.VMEM((group * codes, lanes), F32),
            ],
        ),
        out_shape=[shape, shape, jax.ShapeDtypeStruct((codes, lanes), F32)],
        name="attend_back",
    )(which, *qkvs, *grads, *probs, buckets)
    total = tab.reshape(2, nb, 2, 2, heads, group).sum(axis=(2, 5))
    return d_a, d_b, total[:, :, 0], total[:, :, 1]


def swap(value):
    size = lax.axis_size("tensor")
    return lax.ppermute(value, "tensor", [(i, (i + 1) % size) for i in range(size)])


def ring_bits(turned):
    size = lax.axis_size("dp")
    bits = [1 << k for k in range(size.bit_length() - 1)]
    if turned:
        bits[0], bits[1] = bits[1], bits[0]
    return bits


def across(value, bit):
    size = lax.axis_size("dp")
    return lax.ppermute(value, "dp", [(i, i ^ bit) for i in range(size)])


def ring_scatter(value, bits):
    index = lax.axis_index("dp")
    for bit in bits:
        side = (index // bit) % 2
        half = value.shape[0] // 2
        keep = lax.dynamic_slice_in_dim(value, side * half, half, 0)
        send = lax.dynamic_slice_in_dim(value, (1 - side) * half, half, 0)
        value = keep + across(send, bit)
    return value


def ring_gather(value, bits):
    index = lax.axis_index("dp")
    for bit in reversed(bits):
        low_side = (index // bit) % 2 == 0
        other = across(value, bit)
        value = jnp.concatenate(
            [jnp.where(low_side, value, other), jnp.where(low_side, other, value)]
        )
    return value


def ring_sum(value, turned):
    bits = ring_bits(turned)
    return ring_gather(ring_scatter(value, bits), bits)


def update(clip_factor, grads, state):
    share = state[0].shape[1] // BLOCK
    start = lax.axis_index("dp").astype(jnp.int32) * share
    wide, wide_info, thin, thin_info = [], [], [], []
    base = 0
    row = 0
    for grad in grads:
        rows = grad.size // BLOCK
        if grad.ndim == 2 and grad.shape[1] % BLOCK == 0 and grad.shape[0] > 16:
            lanes = grad.shape[1] // BLOCK
            grad = jnp.pad(grad, ((0, -grad.shape[0] % 8), (0, 0)))
            slab = min(grad.shape[0], -(-(share // lanes + 18) // 8) * 8)
            wide.append(grad)
            wide_info.append((base, lanes, grad.shape[0], slab))
        else:
            thin.append(jnp.pad(grad.reshape(rows, BLOCK), ((0, -rows % 8), (0, 0))))
            thin_info.append((base, row, rows))
            row += rows + -rows % 8
        base += rows
    thin_all = jnp.concatenate(thin)
    margin = -(-max(info[1] * info[3] for info in wide_info) // 8) * 8 + 8

    def slab_start(first, info):
        base, lanes, rows, slab = info
        wanted = jnp.maximum(first - base, 0) // (lanes * 8) * 8
        return pl.multiple_of(jnp.minimum(wanted, rows - slab), 8)

    def body(start_ref, clip_ref, *refs):
        wide_refs = refs[: len(wide)]
        thin_ref = refs[len(wide)]
        master, one, two, ema = refs[len(wide) + 1 : len(wide) + 5]
        new_master, new_one, new_two, new_ema, copy, own = refs[len(wide) + 5 :]
        first = start_ref[0]
        own[margin : margin + share, :] = jnp.zeros((share, BLOCK), F32)
        for ref, info in zip(wide_refs, wide_info):
            base, lanes, rows, slab = info

            @pl.when((first < base + rows * lanes) & (first + share > base))
            def _():
                place = margin + base + slab_start(first, info) * lanes - first
                for k in range(lanes):
                    own[pl.ds(place + k, slab, stride=lanes), :] = ref[
                        :, k * BLOCK : (k + 1) * BLOCK
                    ]

        for base, row, rows in thin_info:

            @pl.when((first < base + rows) & (first + share > base))
            def _():
                own[pl.ds(margin + base - first, rows), :] = thin_ref[row : row + rows, :]

        grad = own[margin : margin + share, :] * clip_ref[0]
        moment = beta_one * one[...] + (1.0 - beta_one) * grad
        second = beta_two * two[...] + (1.0 - beta_two) * grad * grad
        new_one[...] = moment
        new_two[...] = second
        step_size = (
            moment
            / (1.0 - beta_one**STEP)
            / (jnp.sqrt(second / (1.0 - beta_two**STEP)) + adam_eps)
        )
        weight = master[...]
        weight = weight - learn_rate * (step_size + decay_rate * weight)
        new_master[...] = weight
        new_ema[...] = average_rate * ema[...] + (1.0 - average_rate) * weight
        copy[...] = weight.astype(BF16)

    plain = pl.BlockSpec((share, BLOCK), lambda i, s: (0, 0))
    specs = [pl.BlockSpec(memory_space=pltpu.SMEM)]
    for grad, info in zip(wide, wide_info):
        specs.append(
            pl.BlockSpec(
                (pl.Element(info[3]), pl.Element(grad.shape[1])),
                lambda i, s, info=info: (slab_start(s[0], info), 0),
            )
        )
    specs.append(pl.BlockSpec(thin_all.shape, lambda i, s: (0, 0)))
    flat = jax.ShapeDtypeStruct((share, BLOCK), F32)
    results = pl.pallas_call(
        body,
        grid_spec=pltpu.PrefetchScalarGridSpec(
            num_scalar_prefetch=1,
            grid=(1,),
            in_specs=specs + [plain] * 4,
            out_specs=[plain] * 5,
            scratch_shapes=[pltpu.VMEM((2 * margin + share, BLOCK), F32)],
        ),
        out_shape=[flat] * 4 + [jax.ShapeDtypeStruct((share, BLOCK), BF16)],
        name="update",
    )(
        start.reshape(1),
        clip_factor.reshape(1),
        *wide,
        thin_all,
        *(member.reshape(share, BLOCK) for member in state),
    )
    new_master, new_one, new_two, new_ema, copy = (r.reshape(1, -1) for r in results)
    return new_master, new_one, new_two, new_ema, copy


def per_device(
    hidden_in,
    cotangent,
    box_coords,
    doc_ids,
    buckets,
    layout_weight,
    norm_gains,
    norm_shifts,
    branch_biases,
    qkv_weight,
    query_value_bias,
    output_weight,
    ffn_in_weight,
    ffn_in_bias,
    ffn_out_weight,
    relative_table,
    master_flat,
    moment_one,
    moment_two,
    ema_flat,
):
    turn = lax.axis_index("tensor")
    window = turn.astype(jnp.int32).reshape(1)
    gains = norm_gains.astype(F32)
    norm_offsets = norm_shifts.astype(F32)
    biases = branch_biases.astype(F32)

    small_own = jnp.concatenate(
        [query_value_bias.reshape(-1), ffn_in_bias, relative_table.reshape(-1)]
    )
    qkv_other = swap(qkv_weight)
    small_other = swap(small_own)
    output_other = swap(output_weight)
    ffn_in_other = swap(ffn_in_weight)
    ffn_out_other = swap(ffn_out_weight)
    cuts = (query_value_bias.size, query_value_bias.size + ffn_in_bias.size)
    qv_bias_other = small_other[: cuts[0]].reshape(query_value_bias.shape)
    ffn_bias_other = small_other[cuts[0] : cuts[1]]
    table_other = small_other[cuts[1] :].reshape(relative_table.shape)

    features = box_features(box_coords).astype(BF16)
    embedded = hidden_in.astype(F32) + dot_tn(features, layout_weight)
    inputs = embedded.astype(BF16)
    inputs_swap = swap(inputs)

    def project(weight, bias):
        shift = jnp.stack([bias[0], jnp.zeros_like(bias[0]), bias[1]]).astype(F32)
        projected = jnp.einsum("rd,cde->cre", inputs, weight, preferred_element_type=F32)
        return (projected + shift[:, None, :]).astype(BF16)

    qkv_a = project(qkv_weight, query_value_bias)
    context_a, probs_a = attend(window, qkv_a, doc_ids, buckets, relative_table)
    qkv_b = project(qkv_other, qv_bias_other)
    context_b, probs_b = attend(window, qkv_b, doc_ids, buckets, table_other)
    context_swap = swap(context_b)
    attn_out = dot(context_a, output_weight) + dot(context_b, output_other) + biases[0]
    normed_one, inv_std_one = normalize(embedded + attn_out)
    mid_norm = normed_one * gains[0] + norm_offsets[0]
    mid_low = mid_norm.astype(BF16)
    mid_swap = swap(mid_low)

    gelu = partial(jax.nn.gelu, approximate=False)

    def expand(weight, bias):
        pre = dot(mid_low, weight) + bias.astype(F32)
        hidden, back = jax.vjp(gelu, pre)
        return hidden.astype(BF16), back

    hidden_a, gelu_back_a = expand(ffn_in_weight, ffn_in_bias)
    hidden_b, gelu_back_b = expand(ffn_in_other, ffn_bias_other)
    hidden_swap = swap(hidden_b)
    branch = dot(hidden_a, ffn_out_weight) + dot(hidden_b, ffn_out_other) + biases[1]
    normed_two, inv_std_two = normalize(mid_norm + branch)
    hidden_out = (normed_two * gains[1] + norm_offsets[1]).astype(BF16)
    grad_out = cotangent.astype(F32)
    gain_two = jnp.sum(grad_out * normed_two, axis=0)
    shift_two = jnp.sum(grad_out, axis=0)
    grad_sum_two = norm_back(grad_out, normed_two, inv_std_two, gains[1])
    bias_two = jnp.sum(grad_sum_two, axis=0)
    grad_branch = grad_sum_two.astype(BF16)
    grad_branch_swap = swap(grad_branch)

    grad_pre_b = gelu_back_b(dot_nt(grad_branch, ffn_out_other))[0].astype(BF16)
    grad_pre_swap = swap(grad_pre_b)
    grad_pre_a = gelu_back_a(dot_nt(grad_branch, ffn_out_weight))[0].astype(BF16)
    ffn_out_low = (
        dot_tn(hidden_a, grad_branch) + dot_tn(hidden_swap, grad_branch_swap)
    ).astype(BF16)
    ffn_in_low = (dot_tn(mid_low, grad_pre_a) + dot_tn(mid_swap, grad_pre_swap)).astype(BF16)
    ffn_bias_grad = jnp.sum(grad_pre_a.astype(F32), axis=0) + jnp.sum(
        grad_pre_swap.astype(F32), axis=0
    )
    grad_mid = (
        grad_sum_two + dot_nt(grad_pre_a, ffn_in_weight) + dot_nt(grad_pre_b, ffn_in_other)
    )
    gain_one = jnp.sum(grad_mid * normed_one, axis=0)
    shift_one = jnp.sum(grad_mid, axis=0)
    grad_sum_one = norm_back(grad_mid, normed_one, inv_std_one, gains[0])
    bias_one = jnp.sum(grad_sum_one, axis=0)
    grad_attn = grad_sum_one.astype(BF16)
    grad_attn_swap = swap(grad_attn)
    output_grad = dot_tn(context_a, grad_attn) + dot_tn(context_swap, grad_attn_swap)
    grad_context_a = dot_nt(grad_attn, output_weight).astype(BF16)
    grad_context_b = dot_nt(grad_attn, output_other).astype(BF16)

    grad_context_a, grad_context_b, ffn_out_low, ffn_in_low = lax.optimization_barrier(
        (grad_context_a, grad_context_b, ffn_out_low, ffn_in_low)
    )
    grads_a, grads_b, table_a, table_b = attend_back(
        window, (qkv_a, qkv_b), (grad_context_a, grad_context_b), (probs_a, probs_b), buckets, NB
    )
    grads_swap = swap(grads_b)
    table_grad = table_a + swap(table_b)
    qv_bias_grad = jnp.stack(
        [
            jnp.sum(grads_a[c].astype(F32), axis=0) + jnp.sum(grads_swap[c].astype(F32), axis=0)
            for c in (0, 2)
        ]
    )
    qkv_grad = jnp.einsum(
        "rd,cre->cde", inputs, grads_a, preferred_element_type=F32
    ) + jnp.einsum("rd,cre->cde", inputs_swap, grads_swap, preferred_element_type=F32)
    input_grad = (
        grad_sum_one
        + jnp.einsum("cre,cde->rd", grads_a, qkv_weight, preferred_element_type=F32)
        + jnp.einsum("cre,cde->rd", grads_b, qkv_other, preferred_element_type=F32)
    )
    layout_part = dot(features, input_grad.astype(BF16))
    shared = jnp.concatenate(
        [
            layout_part,
            jnp.stack([gain_one, gain_two, shift_one, shift_two, bias_one, bias_two]),
        ]
    )
    cut = shared.shape[0] // lax.axis_size("tensor")
    first_turn = turn == 0
    own_shared = jnp.where(first_turn, shared[:cut], shared[cut:])
    own_shared = own_shared + swap(
        jnp.where(first_turn, shared[cut:], shared[:cut]).astype(BF16)
    ).astype(F32)

    width = qkv_grad.shape[2]
    qkv_rows = qkv_grad.reshape(-1, width).astype(BF16)
    late = [
        output_grad[:, :width].astype(BF16),
        output_grad[:, width:].astype(BF16),
        own_shared[:, :width].astype(BF16),
        own_shared[:, width:].astype(BF16),
        ffn_bias_grad.astype(BF16).reshape(-1, width),
        qv_bias_grad.astype(BF16).reshape(-1, width),
        table_grad.astype(BF16).reshape(-1, width),
    ]
    used = qkv_rows.shape[0] + sum(member.shape[0] for member in late)
    unit = 16 * max(lax.axis_size("dp"), 16)
    half_rows = -(-used // unit) * unit // 2
    late.append(jnp.zeros((2 * half_rows - used, width), BF16))
    pack_a = qkv_rows[:half_rows]
    pack_b = jnp.concatenate([qkv_rows[half_rows:]] + late)

    ffn_out_low = ring_sum(ffn_out_low, 0)
    ffn_in_low = ring_sum(ffn_in_low, 1)
    pack_a = ring_sum(pack_a, 0)
    pack_b = ring_sum(pack_b, 1)

    square = sum(
        jnp.sum(jnp.square(member.astype(F32)))
        for member in (ffn_out_low, ffn_in_low, pack_a, pack_b)
    )
    ffn_out_grad = ffn_out_low.astype(F32)
    ffn_in_grad = ffn_in_low.astype(F32)
    rest = qkv_rows.shape[0] - half_rows
    qkv_flat = jnp.concatenate([pack_a, pack_b[:rest]]).astype(F32)
    pieces, place = [], rest
    for member in late[:-1]:
        pieces.append(pack_b[place : place + member.shape[0]])
        place += member.shape[0]
    output_grad = jnp.concatenate(pieces[0:2], axis=1).astype(F32)
    own_low = jnp.concatenate(pieces[2:4], axis=1)
    other_low = swap(own_low)
    shared = jnp.where(
        first_turn,
        jnp.concatenate([own_low, other_low]),
        jnp.concatenate([other_low, own_low]),
    ).astype(F32)
    ffn_bias_grad = pieces[4].astype(F32).reshape(-1)
    qv_bias_grad = pieces[5].astype(F32)
    table_grad = pieces[6].astype(F32).reshape(table_grad.shape)
    layout_grad = shared[: layout_part.shape[0]]
    gains_grad, shifts_grad, biases_grad = jnp.split(shared[layout_part.shape[0] :], 3)

    grad_norm = jnp.sqrt(square + swap(square))
    clip_factor = clip_limit / jnp.maximum(grad_norm, clip_limit)
    updated = update(
        clip_factor,
        (
            ffn_in_grad,
            ffn_bias_grad,
            ffn_out_grad,
            qkv_flat,
            qv_bias_grad,
            output_grad,
            table_grad,
            own_low.astype(F32),
        ),
        (master_flat, moment_one, moment_two, ema_flat),
    )
    return (
        hidden_out,
        input_grad,
        layout_grad,
        gains_grad,
        shifts_grad,
        biases_grad,
        qkv_flat.reshape(qkv_grad.shape),
        qv_bias_grad,
        output_grad,
        ffn_in_grad,
        ffn_bias_grad,
        ffn_out_grad,
        table_grad,
        grad_norm,
    ) + tuple(updated)


def solution(mesh):
    return jax.shard_map(
        per_device,
        mesh=mesh,
        in_specs=(
            P(("dp", "tensor"), None),
            P(("dp", "tensor"), None),
            P(None, ("dp", "tensor")),
            P("dp", None),
            P(None, "dp", None, None),
            P(),
            P(),
            P(),
            P(),
            P(None, None, "tensor"),
            P(None, "tensor"),
            P("tensor", None),
            P(None, "tensor"),
            P("tensor"),
            P("tensor", None),
            P(None, None, "tensor"),
            P("tensor", "dp"),
            P("tensor", "dp"),
            P("tensor", "dp"),
            P("tensor", "dp"),
        ),
        out_specs=(
            P(("dp", "tensor"), None),
            P(("dp", "tensor"), None),
            P(),
            P(),
            P(),
            P(),
            P(None, None, "tensor"),
            P(None, "tensor"),
            P("tensor", None),
            P(None, "tensor"),
            P("tensor"),
            P("tensor", None),
            P(None, None, "tensor"),
            P(),
            P("tensor", "dp"),
            P("tensor", "dp"),
            P("tensor", "dp"),
            P("tensor", "dp"),
            P("tensor", "dp"),
        ),
        check_vma=False,
    )
```

```python
from functools import partial
import math

import jax
import jax.numpy as jnp
from jax import lax
from jax.experimental import pallas as pl
from jax.experimental.pallas import tpu as pltpu
from jax.sharding import PartitionSpec as P

NB = 32
FEAT = 256
STEP = 10
BLOCK = 128
CHUNK = 32
ATTEND_FLOPS = 1 << 33
BACK_FLOPS = 1 << 35


norm_eps = 1e-05
learn_rate = 0.02
beta_one = 0.9
beta_two = 0.999
adam_eps = 1e-08
decay_rate = 0.01
average_rate = 0.5
clip_limit = 1.0
mask_fill = -1e30

F32 = jnp.float32
BF16 = jnp.bfloat16
NT = (((1,), (1,)), ((), ()))
TN = (((0,), (0,)), ((), ()))


def dot(left, right):
    return jnp.dot(left, right, preferred_element_type=F32)


def dot_nt(left, right):
    return lax.dot_general(left, right, NT, preferred_element_type=F32)


def dot_tn(left, right):
    return lax.dot_general(left, right, TN, preferred_element_type=F32)


def box_features(coords):
    count = FEAT // 8
    freqs = jnp.exp(-math.log(10000.0) * jnp.arange(count, dtype=F32) / count)
    angles = coords.astype(F32)[:, None, :] * freqs[None, :, None]
    waves = jnp.stack([jnp.sin(angles), jnp.cos(angles)], axis=1)
    return waves.reshape(FEAT, coords.shape[1])


def normalize(value):
    centre = value - jnp.mean(value, axis=-1, keepdims=True)
    inv_std = lax.rsqrt(jnp.mean(centre * centre, axis=-1, keepdims=True) + norm_eps)
    return (centre * inv_std, inv_std)


def norm_back(grad_out, normed, inv_std, gain):
    scaled = grad_out * gain
    return inv_std * (
        scaled
        - jnp.mean(scaled, axis=-1, keepdims=True)
        - normed * jnp.mean(scaled * normed, axis=-1, keepdims=True)
    )


def attend(which, qkv, docs, buckets, table):
    _, rows, width = qkv.shape
    nb, heads = table.shape[1:]
    pairs = heads // 2
    half = width // heads
    span = 3 * BLOCK
    blocks = rows // BLOCK
    scale = 1.0 / math.sqrt(half)
    lookup = jnp.pad(
        jnp.concatenate([table[0], table[1]], axis=0).astype(F32).T,
        ((0, 0), (0, BLOCK - 2 * nb)),
    ).reshape(heads, 1, BLOCK)
    doc_row = docs[:, None, :]
    doc_col = docs[:, :, None]

    def body(which_ref, qkv_ref, dr_ref, dc_ref, b_ref, t_ref, ctx_ref, p_ref):
        block = pl.program_id(0)
        start = pl.multiple_of(jnp.clip(block - 1, 0, blocks - 3) * BLOCK, BLOCK)
        own_rows = pl.ds(pl.multiple_of(block * BLOCK, BLOCK), BLOCK)
        key_rows = pl.ds(start, span)
        same = dc_ref[0] == dr_ref[0, :, key_rows]
        first = b_ref[0, 0, :, key_rows]
        second = b_ref[1, 0, :, key_rows] + nb
        low_lane = lax.broadcasted_iota(jnp.int32, (BLOCK, 2 * half), 1) < half

        def one_pair(p, carry):
            cols = pl.ds(pl.multiple_of(p * 2 * half, 2 * half), 2 * half)
            q2 = qkv_ref[0, own_rows, cols]
            k2 = qkv_ref[1, key_rows, cols]
            v2 = qkv_ref[2, key_rows, cols]
            outs = []
            for e in range(2):
                qm = jnp.where(low_lane == (e == 0), q2, jnp.zeros_like(q2))
                raw = dot_nt(qm, k2)
                trow = jnp.broadcast_to(t_ref[2 * p + e], (BLOCK, BLOCK))
                bias = jnp.concatenate(
                    [
                        jnp.take_along_axis(
                            trow, first[:, c : c + BLOCK], axis=1, mode="promise_in_bounds"
                        )
                        + jnp.take_along_axis(
                            trow, second[:, c : c + BLOCK], axis=1, mode="promise_in_bounds"
                        )
                        for c in range(0, span, BLOCK)
                    ],
                    axis=1,
                )
                scores = jnp.where(same, raw * scale + bias, mask_fill)
                top = jnp.max(scores, axis=1, keepdims=True)
                weights = jnp.exp(scores - top)
                probs = weights * (1.0 / jnp.sum(weights, axis=1, keepdims=True))
                p_ref[2 * p + e, 0] = probs
                outs.append(dot(probs.astype(BF16), v2))
            ctx_ref[:, cols] = jnp.where(low_lane, outs[0], outs[1]).astype(BF16)
            return carry

        lax.fori_loop(0, pairs, one_pair, 0, unroll=True)

    return pl.pallas_call(
        body,
        grid_spec=pltpu.PrefetchScalarGridSpec(
            num_scalar_prefetch=1,
            grid=(blocks,),
            in_specs=[
                pl.BlockSpec((3, rows, width), lambda i, w: (0, 0, 0)),
                pl.BlockSpec((1, 1, rows), lambda i, w: (w[0], 0, 0)),
                pl.BlockSpec((1, BLOCK, 1), lambda i, w: (w[0], i, 0)),
                pl.BlockSpec((2, 1, BLOCK, rows), lambda i, w: (0, w[0], i, 0)),
                pl.BlockSpec((heads, 1, BLOCK), lambda i, w: (0, 0, 0)),
            ],
            out_specs=[
                pl.BlockSpec((BLOCK, width), lambda i, w: (i, 0)),
                pl.BlockSpec((heads, 1, BLOCK, span), lambda i, w: (0, i, 0, 0)),
            ],
        ),
        out_shape=[
            jax.ShapeDtypeStruct((rows, width), BF16),
            jax.ShapeDtypeStruct((heads, blocks, BLOCK, span), F32),
        ],
        cost_estimate=pl.CostEstimate(flops=ATTEND_FLOPS, transcendentals=0, bytes_accessed=1 << 23),
        name="attend",
    )(which, qkv, doc_row, doc_col, buckets, lookup)


def attend_back(which, qkvs, grads, probs, buckets, nb):
    _, rows, width = qkvs[0].shape
    heads, blocks, _, span = probs[0].shape
    pairs = heads // 2
    half = width // heads
    scale = 1.0 / math.sqrt(half)
    group = 8
    codes = 2 * nb
    lanes = 2 * 2 * heads * group

    def body(
        which_ref, qkv_a, qkv_b, g_a, g_b, p_a, p_b, b_ref, d_a, d_b, tab_ref, gs_ref, acc_a, acc_b, acc_ref
    ):
        block = pl.program_id(0)
        start = pl.multiple_of(jnp.clip(block - 1, 0, blocks - 3) * BLOCK, BLOCK)
        own_rows = pl.ds(pl.multiple_of(block * BLOCK, BLOCK), BLOCK)
        key_rows = pl.ds(start, span)
        low_lane = lax.broadcasted_iota(jnp.int32, (BLOCK, 2 * half), 1) < half

        @pl.when(block == 0)
        def _():
            acc_a[...] = jnp.zeros_like(acc_a)
            acc_b[...] = jnp.zeros_like(acc_b)
            acc_ref[...] = jnp.zeros_like(acc_ref)

        for side, (qkv_ref, g_ref, p_ref, d_ref, sums) in enumerate(
            ((qkv_a, g_a, p_a, d_a, acc_a), (qkv_b, g_b, p_b, d_b, acc_b))
        ):

            def one_pair(p, carry):
                cols = pl.ds(pl.multiple_of(p * 2 * half, 2 * half), 2 * half)
                q2 = qkv_ref[0, own_rows, cols]
                g2 = g_ref[:, cols]
                k2 = qkv_ref[1, key_rows, cols]
                v2 = qkv_ref[2, key_rows, cols]
                dqs = []
                dk = sums[0, key_rows, cols]
                dv = sums[1, key_rows, cols]
                for e in range(2):
                    mine = low_lane == (e == 0)
                    qm = jnp.where(mine, q2, jnp.zeros_like(q2))
                    gm = jnp.where(mine, g2, jnp.zeros_like(g2))
                    pr = p_ref[2 * p + e, 0]
                    gp = dot_nt(gm, v2)
                    gs = pr * (gp - jnp.sum(pr * gp, axis=1, keepdims=True))
                    gs_ref[side * heads + 2 * p + e] = gs
                    raw = (gs * scale).astype(BF16)
                    dqs.append(dot(raw, k2))
                    dk = dk + dot_tn(raw, qm)
                    dv = dv + dot_tn(pr.astype(BF16), gm)
                d_ref[0, own_rows, cols] = jnp.where(low_lane, dqs[0], dqs[1]).astype(BF16)
                sums[0, key_rows, cols] = dk
                sums[1, key_rows, cols] = dv
                return carry

            lax.fori_loop(0, pairs, one_pair, 0, unroll=True)

        code_ids = lax.broadcasted_iota(jnp.int32, (nb, span), 0)

        def one_group(g, carry):
            r8 = pl.ds(pl.multiple_of(g * group, group), group)
            b0 = b_ref[0, 0, r8, key_rows]
            b1 = b_ref[1, 0, r8, key_rows]
            pieces = []
            for r in range(group):
                for b in (b0, b1):
                    row = jnp.broadcast_to(b[r : r + 1], (nb, span))
                    pieces.append(jnp.where(row == code_ids, 1.0, 0.0).astype(BF16))
            onehot = jnp.concatenate(pieces, axis=0)
            gg = gs_ref[:, r8, :].reshape(2 * heads * group, span)
            upper = gg.astype(BF16)
            lower = (gg - upper.astype(F32)).astype(BF16)
            both = jnp.concatenate([upper, lower], axis=0)
            acc_ref[...] += dot_nt(onehot, both)
            return carry

        lax.fori_loop(0, BLOCK // group, one_group, 0)

        @pl.when(block == blocks - 1)
        def _():
            for d_ref, sums in ((d_a, acc_a), (d_b, acc_b)):
                d_ref[1] = sums[0].astype(BF16)
                d_ref[2] = sums[1].astype(BF16)
            lane_row = lax.broadcasted_iota(jnp.int32, (codes, lanes), 1) % group
            total = jnp.zeros((codes, lanes), F32)
            for r in range(group):
                total = total + jnp.where(
                    lane_row == r, acc_ref[r * codes : (r + 1) * codes, :], 0.0
                )
            tab_ref[...] = total

    whole = pl.BlockSpec((3, rows, width), lambda i, w: (0, 0, 0))
    part = pl.BlockSpec((BLOCK, width), lambda i, w: (i, 0))
    prob = pl.BlockSpec((heads, 1, BLOCK, span), lambda i, w: (0, i, 0, 0))
    shape = jax.ShapeDtypeStruct((3, rows, width), BF16)
    d_a, d_b, tab = pl.pallas_call(
        body,
        grid_spec=pltpu.PrefetchScalarGridSpec(
            num_scalar_prefetch=1,
            grid=(blocks,),
            in_specs=[
                whole, whole, part, part, prob, prob,
                pl.BlockSpec((2, 1, BLOCK, rows), lambda i, w: (0, w[0], i, 0)),
            ],
            out_specs=[whole, whole, pl.BlockSpec((codes, lanes), lambda i, w: (0, 0))],
            scratch_shapes=[
                pltpu.VMEM((2 * heads, BLOCK, span), F32),
                pltpu.VMEM((2, rows, width), F32),
                pltpu.VMEM((2, rows, width), F32),
                pltpu.VMEM((group * codes, lanes), F32),
            ],
        ),
        out_shape=[shape, shape, jax.ShapeDtypeStruct((codes, lanes), F32)],
        cost_estimate=pl.CostEstimate(
            flops=BACK_FLOPS, transcendentals=0, bytes_accessed=1 << 24
        ),
        name="attend_back",
    )(which, *qkvs, *grads, *probs, buckets)
    total = tab.reshape(2, nb, 2, 2, heads, group).sum(axis=(2, 5))
    return d_a, d_b, total[:, :, 0], total[:, :, 1]


def swap(value):
    size = lax.axis_size("tensor")
    return lax.ppermute(value, "tensor", [(i, (i + 1) % size) for i in range(size)])


def ring_bits(turned):
    size = lax.axis_size("dp")
    bits = [1 << k for k in range(size.bit_length() - 1)]
    if turned:
        bits[0], bits[1] = bits[1], bits[0]
    return bits


def across(value, bit):
    size = lax.axis_size("dp")
    return lax.ppermute(value, "dp", [(i, i ^ bit) for i in range(size)])


def side_of(bit):
    return (lax.axis_index("dp") >> (bit.bit_length() - 1)) & 1


def parted(value, bit):
    side = side_of(bit)
    half = value.shape[0] // 2
    keep = lax.dynamic_slice_in_dim(value, side * half, half, 0, allow_negative_indices=False)
    send = lax.dynamic_slice_in_dim(
        value, (1 - side) * half, half, 0, allow_negative_indices=False
    )
    return keep, send


def ring_scatter(value, bits):
    for bit in bits:
        keep, send = parted(value, bit)
        value = keep + across(send, bit)
    return value


def ring_gather(value, bits):
    for bit in reversed(bits):
        low_side = side_of(bit) == 0
        other = across(value, bit)
        value = jnp.concatenate(
            [jnp.where(low_side, value, other), jnp.where(low_side, other, value)]
        )
    return value


def update(clip_factor, grads, state):
    share = state[0].shape[1] // BLOCK
    start = lax.axis_index("dp").astype(jnp.int32) * share
    wide, wide_info, thin, thin_info = [], [], [], []
    base = 0
    row = 0
    for grad in grads:
        rows = grad.size // BLOCK
        if grad.ndim == 2 and grad.shape[1] % BLOCK == 0 and grad.shape[0] > 16:
            lanes = grad.shape[1] // BLOCK
            grad = jnp.pad(grad, ((0, -grad.shape[0] % 8), (0, 0)))
            slab = min(grad.shape[0], -(-(share // lanes + 18) // 8) * 8)
            wide.append(grad)
            wide_info.append((base, lanes, grad.shape[0], slab))
        else:
            thin.append(jnp.pad(grad.reshape(rows, BLOCK), ((0, -rows % 8), (0, 0))))
            thin_info.append((base, row, rows))
            row += rows + -rows % 8
        base += rows
    thin_all = jnp.concatenate(thin)
    margin = -(-max(info[1] * info[3] for info in wide_info) // 8) * 8 + 8

    def slab_start(first, info):
        base, lanes, rows, slab = info
        wanted = jnp.maximum(first - base, 0) // (lanes * 8) * 8
        return pl.multiple_of(jnp.minimum(wanted, rows - slab), 8)

    def body(start_ref, clip_ref, *refs):
        wide_refs = refs[: len(wide)]
        thin_ref = refs[len(wide)]
        master, one, two, ema = refs[len(wide) + 1 : len(wide) + 5]
        new_master, new_one, new_two, new_ema, copy, own = refs[len(wide) + 5 :]
        first = start_ref[0]
        own[margin : margin + share, :] = jnp.zeros((share, BLOCK), F32)
        for ref, info in zip(wide_refs, wide_info):
            base, lanes, rows, slab = info

            @pl.when((first < base + rows * lanes) & (first + share > base))
            def _():
                place = margin + base + slab_start(first, info) * lanes - first
                for k in range(lanes):
                    own[pl.ds(place + k, slab, stride=lanes), :] = ref[
                        :, k * BLOCK : (k + 1) * BLOCK
                    ]

        for base, row, rows in thin_info:

            @pl.when((first < base + rows) & (first + share > base))
            def _():
                own[pl.ds(margin + base - first, rows), :] = thin_ref[row : row + rows, :]

        scale = clip_ref[0]

        def advance(row, rows):
            many = -(-rows // 8) * 8
            grad = own[pl.ds(pl.multiple_of(margin + row, 8), many), :].reshape(1, many * BLOCK)
            grad = grad[:, : rows * BLOCK] * scale
            place = (slice(None), pl.ds(pl.multiple_of(row * BLOCK, 8 * BLOCK), rows * BLOCK))
            moment = beta_one * one[place] + (1.0 - beta_one) * grad
            second = beta_two * two[place] + (1.0 - beta_two) * grad * grad
            new_one[place] = moment
            new_two[place] = second
            step_size = (
                moment
                / (1.0 - beta_one**STEP)
                / (jnp.sqrt(second / (1.0 - beta_two**STEP)) + adam_eps)
            )
            weight = master[place]
            weight = weight - learn_rate * (step_size + decay_rate * weight)
            new_master[place] = weight
            new_ema[place] = average_rate * ema[place] + (1.0 - average_rate) * weight
            copy[place] = weight.astype(BF16)

        def many_rows(number, carry):
            advance(number * CHUNK, CHUNK)
            return carry

        lax.fori_loop(0, share // CHUNK, many_rows, 0)
        if share % CHUNK:
            advance(share // CHUNK * CHUNK, share % CHUNK)

    plain = pl.BlockSpec((1, share * BLOCK), lambda i, s: (0, 0))
    specs = [pl.BlockSpec(memory_space=pltpu.SMEM)]
    for grad, info in zip(wide, wide_info):
        specs.append(
            pl.BlockSpec(
                (pl.Element(info[3]), pl.Element(grad.shape[1])),
                lambda i, s, info=info: (slab_start(s[0], info), 0),
            )
        )
    specs.append(pl.BlockSpec(thin_all.shape, lambda i, s: (0, 0)))
    flat = jax.ShapeDtypeStruct((1, share * BLOCK), F32)
    return pl.pallas_call(
        body,
        grid_spec=pltpu.PrefetchScalarGridSpec(
            num_scalar_prefetch=1,
            grid=(1,),
            in_specs=specs + [plain] * 4,
            out_specs=[plain] * 5,
            scratch_shapes=[pltpu.VMEM((2 * margin + share + 8, BLOCK), F32)],
        ),
        out_shape=[flat] * 4 + [jax.ShapeDtypeStruct((1, share * BLOCK), BF16)],
        name="update",
    )(
        start.reshape(1),
        clip_factor.reshape(1),
        *wide,
        thin_all,
        *state,
    )


def per_device(
    hidden_in,
    cotangent,
    box_coords,
    doc_ids,
    buckets,
    layout_weight,
    norm_gains,
    norm_shifts,
    branch_biases,
    qkv_weight,
    query_value_bias,
    output_weight,
    ffn_in_weight,
    ffn_in_bias,
    ffn_out_weight,
    relative_table,
    master_flat,
    moment_one,
    moment_two,
    ema_flat,
):
    turn = lax.axis_index("tensor")
    window = turn.astype(jnp.int32).reshape(1)
    gains = norm_gains.astype(F32)
    norm_offsets = norm_shifts.astype(F32)
    biases = branch_biases.astype(F32)

    small_own = jnp.concatenate(
        [query_value_bias.reshape(-1), ffn_in_bias, relative_table.reshape(-1)]
    )
    qkv_other = swap(qkv_weight)
    small_other = swap(small_own)
    output_other = swap(output_weight)
    ffn_in_other = swap(ffn_in_weight)
    ffn_out_other = swap(ffn_out_weight)
    cuts = (query_value_bias.size, query_value_bias.size + ffn_in_bias.size)
    qv_bias_other = small_other[: cuts[0]].reshape(query_value_bias.shape)
    ffn_bias_other = small_other[cuts[0] : cuts[1]]
    table_other = small_other[cuts[1] :].reshape(relative_table.shape)

    features = box_features(box_coords).astype(BF16)
    embedded = hidden_in.astype(F32) + dot_tn(features, layout_weight)
    inputs = embedded.astype(BF16)
    inputs_swap = swap(inputs)

    def project(weight, bias):
        shift = jnp.stack([bias[0], jnp.zeros_like(bias[0]), bias[1]]).astype(F32)
        projected = jnp.einsum("rd,cde->cre", inputs, weight, preferred_element_type=F32)
        return (projected + shift[:, None, :]).astype(BF16)

    qkv_a = project(qkv_weight, query_value_bias)
    context_a, probs_a = attend(window, qkv_a, doc_ids, buckets, relative_table)
    qkv_b = project(qkv_other, qv_bias_other)
    context_b, probs_b = attend(window, qkv_b, doc_ids, buckets, table_other)
    context_swap = swap(context_b)
    attn_out = dot(context_a, output_weight) + dot(context_b, output_other) + biases[0]
    normed_one, inv_std_one = normalize(embedded + attn_out)
    mid_norm = normed_one * gains[0] + norm_offsets[0]
    mid_low = mid_norm.astype(BF16)
    mid_swap = swap(mid_low)

    gelu = partial(jax.nn.gelu, approximate=False)

    def expand(weight, bias):
        pre = dot(mid_low, weight) + bias.astype(F32)
        hidden, back = jax.vjp(gelu, pre)
        return hidden.astype(BF16), back

    hidden_a, gelu_back_a = expand(ffn_in_weight, ffn_in_bias)
    hidden_b, gelu_back_b = expand(ffn_in_other, ffn_bias_other)
    hidden_swap = swap(hidden_b)
    branch = dot(hidden_a, ffn_out_weight) + dot(hidden_b, ffn_out_other) + biases[1]
    normed_two, inv_std_two = normalize(mid_norm + branch)
    hidden_out = (normed_two * gains[1] + norm_offsets[1]).astype(BF16)
    grad_out = cotangent.astype(F32)
    gain_two = jnp.sum(grad_out * normed_two, axis=0)
    shift_two = jnp.sum(grad_out, axis=0)
    grad_sum_two = norm_back(grad_out, normed_two, inv_std_two, gains[1])
    bias_two = jnp.sum(grad_sum_two, axis=0)
    grad_branch = grad_sum_two.astype(BF16)
    grad_branch_swap = swap(grad_branch)

    grad_pre_b = gelu_back_b(dot_nt(grad_branch, ffn_out_other))[0].astype(BF16)
    grad_pre_swap = swap(grad_pre_b)
    grad_pre_a = gelu_back_a(dot_nt(grad_branch, ffn_out_weight))[0].astype(BF16)
    ffn_out_low = (
        dot_tn(hidden_a, grad_branch) + dot_tn(hidden_swap, grad_branch_swap)
    ).astype(BF16)
    ffn_in_low = (dot_tn(mid_low, grad_pre_a) + dot_tn(mid_swap, grad_pre_swap)).astype(BF16)
    ffn_bias_grad = jnp.sum(grad_pre_a.astype(F32), axis=0) + jnp.sum(
        grad_pre_swap.astype(F32), axis=0
    )
    grad_mid = (
        grad_sum_two + dot_nt(grad_pre_a, ffn_in_weight) + dot_nt(grad_pre_b, ffn_in_other)
    )
    gain_one = jnp.sum(grad_mid * normed_one, axis=0)
    shift_one = jnp.sum(grad_mid, axis=0)
    grad_sum_one = norm_back(grad_mid, normed_one, inv_std_one, gains[0])
    bias_one = jnp.sum(grad_sum_one, axis=0)
    grad_attn = grad_sum_one.astype(BF16)
    grad_attn_swap = swap(grad_attn)
    output_grad = dot_tn(context_a, grad_attn) + dot_tn(context_swap, grad_attn_swap)
    grad_context_a = dot_nt(grad_attn, output_weight).astype(BF16)
    grad_context_b = dot_nt(grad_attn, output_other).astype(BF16)

    bits_a, bits_b = ring_bits(False), ring_bits(True)
    out_keep, out_send = parted(ffn_out_low, bits_a[0])
    in_keep, in_send = parted(ffn_in_low, bits_b[0])
    grad_context_a, grad_context_b, out_send, in_send = lax.optimization_barrier(
        (grad_context_a, grad_context_b, out_send, in_send)
    )
    out_sum = out_keep + across(out_send, bits_a[0])
    in_sum = in_keep + across(in_send, bits_b[0])
    grads_a, grads_b, table_a, table_b = attend_back(
        window, (qkv_a, qkv_b), (grad_context_a, grad_context_b), (probs_a, probs_b), buckets, NB
    )
    out_keep, out_send = parted(out_sum, bits_a[1])
    in_keep, in_send = parted(in_sum, bits_b[1])
    grads_a, grads_b, table_a, table_b, out_send, in_send = lax.optimization_barrier(
        (grads_a, grads_b, table_a, table_b, out_send, in_send)
    )
    out_sum = out_keep + across(out_send, bits_a[1])
    in_sum = in_keep + across(in_send, bits_b[1])
    grads_swap = swap(grads_b)
    table_grad = table_a + swap(table_b)
    qv_bias_grad = jnp.stack(
        [
            jnp.sum(grads_a[c].astype(F32), axis=0) + jnp.sum(grads_swap[c].astype(F32), axis=0)
            for c in (0, 2)
        ]
    )
    qkv_parts = [
        (dot_tn(inputs, grads_a[c]) + dot_tn(inputs_swap, grads_swap[c])).astype(BF16)
        for c in range(3)
    ]
    input_grad = (
        grad_sum_one
        + jnp.einsum("cre,cde->rd", grads_a, qkv_weight, preferred_element_type=F32)
        + jnp.einsum("cre,cde->rd", grads_b, qkv_other, preferred_element_type=F32)
    )
    layout_part = dot(features, input_grad.astype(BF16))
    shared = jnp.concatenate(
        [
            layout_part,
            jnp.stack([gain_one, gain_two, shift_one, shift_two, bias_one, bias_two]),
        ]
    )
    cut = shared.shape[0] // lax.axis_size("tensor")
    first_turn = turn == 0
    own_shared = jnp.where(first_turn, shared[:cut], shared[cut:])
    own_shared = own_shared + swap(
        jnp.where(first_turn, shared[cut:], shared[:cut]).astype(BF16)
    ).astype(F32)

    width = qkv_weight.shape[2]
    half_width = lambda value: (value[:, :width], value[:, width:])

    def aligned(value):
        value = value.astype(BF16).reshape(-1, width)
        return jnp.pad(value, ((0, -value.shape[0] % 16), (0, 0)))

    late = [aligned(v) for v in half_width(output_grad) + half_width(own_shared)]
    late += [aligned(v) for v in (ffn_bias_grad, qv_bias_grad, table_grad)]
    qkv_rows = sum(member.shape[0] for member in qkv_parts)
    used = qkv_rows + sum(member.shape[0] for member in late)
    unit = 16 * max(lax.axis_size("dp"), 16)
    half_rows = -(-used // unit) * unit // 2
    rest = qkv_rows - half_rows
    late.append(jnp.zeros((2 * half_rows - used, width), BF16))
    kept = qkv_parts[2].shape[0] - rest
    pack_a = jnp.concatenate(qkv_parts[:2] + [qkv_parts[2][:kept]])
    pack_b = jnp.concatenate([qkv_parts[2][kept:]] + late)

    pack_a, late_a = parted(pack_a, bits_a[0])
    pack_b, late_b = parted(pack_b, bits_b[0])
    out_keep, out_send = parted(out_sum, bits_a[2])
    in_keep, in_send = parted(in_sum, bits_b[2])
    late_a, late_b, out_send, in_send = lax.optimization_barrier(
        (late_a, late_b, out_send, in_send)
    )
    pack_a = pack_a + across(late_a, bits_a[0])
    pack_b = pack_b + across(late_b, bits_b[0])
    out_sum = out_keep + across(out_send, bits_a[2])
    in_sum = in_keep + across(in_send, bits_b[2])
    ffn_out_low = ring_gather(ring_scatter(out_sum, bits_a[3:]), bits_a)
    ffn_in_low = ring_gather(ring_scatter(in_sum, bits_b[3:]), bits_b)
    pack_a = ring_gather(ring_scatter(pack_a, bits_a[1:]), bits_a)
    pack_b = ring_gather(ring_scatter(pack_b, bits_b[1:]), bits_b)

    square = sum(
        jnp.sum(jnp.square(member.astype(F32)))
        for member in (ffn_out_low, ffn_in_low, pack_a, pack_b)
    )
    ffn_out_grad = ffn_out_low.astype(F32)
    ffn_in_grad = ffn_in_low.astype(F32)
    qkv_flat = jnp.concatenate([pack_a, pack_b[:rest]]).astype(F32)
    pieces, place = [], rest
    for member in late[:-1]:
        pieces.append(pack_b[place : place + member.shape[0]])
        place += member.shape[0]
    output_grad = jnp.concatenate(pieces[0:2], axis=1).astype(F32)
    own_low = jnp.concatenate(pieces[2:4], axis=1)[:cut]
    other_low = swap(own_low)
    shared = jnp.where(
        first_turn,
        jnp.concatenate([own_low, other_low]),
        jnp.concatenate([other_low, own_low]),
    ).astype(F32)
    ffn_bias_grad, qv_bias_grad, table_grad = (
        piece[: member.size // width].astype(F32).reshape(member.shape)
        for piece, member in zip(pieces[4:7], (ffn_bias_grad, qv_bias_grad, table_grad))
    )
    layout_grad = shared[: layout_part.shape[0]]
    gains_grad, shifts_grad, biases_grad = jnp.split(shared[layout_part.shape[0] :], 3)

    grad_norm = jnp.sqrt(square + swap(square))
    clip_factor = clip_limit / jnp.maximum(grad_norm, clip_limit)
    updated = update(
        clip_factor,
        (
            ffn_in_grad,
            ffn_bias_grad,
            ffn_out_grad,
            qkv_flat,
            qv_bias_grad,
            output_grad,
            table_grad,
            own_low.astype(F32),
        ),
        (master_flat, moment_one, moment_two, ema_flat),
    )
    return (
        hidden_out,
        input_grad,
        layout_grad,
        gains_grad,
        shifts_grad,
        biases_grad,
        qkv_flat.reshape(qkv_weight.shape),
        qv_bias_grad,
        output_grad,
        ffn_in_grad,
        ffn_bias_grad,
        ffn_out_grad,
        table_grad,
        grad_norm,
    ) + tuple(updated)


def solution(mesh):
    return jax.shard_map(
        per_device,
        mesh=mesh,
        in_specs=(
            P(("dp", "tensor"), None),
            P(("dp", "tensor"), None),
            P(None, ("dp", "tensor")),
            P("dp", None),
            P(None, "dp", None, None),
            P(),
            P(),
            P(),
            P(),
            P(None, None, "tensor"),
            P(None, "tensor"),
            P("tensor", None),
            P(None, "tensor"),
            P("tensor"),
            P("tensor", None),
            P(None, None, "tensor"),
            P("tensor", "dp"),
            P("tensor", "dp"),
            P("tensor", "dp"),
            P("tensor", "dp"),
        ),
        out_specs=(
            P(("dp", "tensor"), None),
            P(("dp", "tensor"), None),
            P(),
            P(),
            P(),
            P(),
            P(None, None, "tensor"),
            P(None, "tensor"),
            P("tensor", None),
            P(None, "tensor"),
            P("tensor"),
            P("tensor", None),
            P(None, None, "tensor"),
            P(),
            P("tensor", "dp"),
            P("tensor", "dp"),
            P("tensor", "dp"),
            P("tensor", "dp"),
            P("tensor", "dp"),
        ),
        check_vma=False,
    )
```

```python
import math

import jax
import jax.numpy as jnp
from jax import lax
from jax.experimental import pallas as pl
from jax.experimental.pallas import tpu as pltpu
from jax.sharding import PartitionSpec as P

NB = 32
FEAT = 256
STEP = 10
BLOCK = 128
CHUNK = 32
ATTEND_FLOPS = 1 << 33
BACK_FLOPS = 1 << 35


norm_eps = 1e-05
learn_rate = 0.02
beta_one = 0.9
beta_two = 0.999
adam_eps = 1e-08
decay_rate = 0.01
average_rate = 0.5
clip_limit = 1.0
mask_fill = -1e30

F32 = jnp.float32
BF16 = jnp.bfloat16
NT = (((1,), (1,)), ((), ()))
TN = (((0,), (0,)), ((), ()))


def dot(left, right):
    return jnp.dot(left, right, preferred_element_type=F32)


def dot_nt(left, right):
    return lax.dot_general(left, right, NT, preferred_element_type=F32)


def dot_tn(left, right):
    return lax.dot_general(left, right, TN, preferred_element_type=F32)


def box_features(coords):
    count = FEAT // 8
    freqs = jnp.exp(-math.log(10000.0) * jnp.arange(count, dtype=F32) / count)
    angles = coords.astype(F32)[:, None, :] * freqs[None, :, None]
    waves = jnp.stack([jnp.sin(angles), jnp.cos(angles)], axis=1)
    return waves.reshape(FEAT, coords.shape[1])


def normalize(value):
    centre = value - jnp.mean(value, axis=-1, keepdims=True)
    inv_std = lax.rsqrt(jnp.mean(centre * centre, axis=-1, keepdims=True) + norm_eps)
    return (centre * inv_std, inv_std)


def norm_back(grad_out, normed, inv_std, gain):
    scaled = grad_out * gain
    return inv_std * (
        scaled
        - jnp.mean(scaled, axis=-1, keepdims=True)
        - normed * jnp.mean(scaled * normed, axis=-1, keepdims=True)
    )


def attend(which, qkv, docs, buckets, table):
    rows, width = qkv.shape[0], qkv.shape[1] // 3
    nb, heads = table.shape[1:]
    pairs = heads // 2
    half = width // heads
    span = 3 * BLOCK
    blocks = rows // BLOCK
    scale = 1.0 / math.sqrt(half)
    lookup = jnp.pad(
        jnp.concatenate([table[0], table[1]], axis=0).astype(F32).T,
        ((0, 0), (0, BLOCK - 2 * nb)),
    ).reshape(heads, 1, BLOCK)
    doc_row = docs[:, None, :]
    doc_col = docs[:, :, None]

    def body(which_ref, qkv_ref, dr_ref, dc_ref, b_ref, t_ref, ctx_ref, p_ref):
        block = pl.program_id(0)
        start = pl.multiple_of(jnp.clip(block - 1, 0, blocks - 3) * BLOCK, BLOCK)
        own_rows = pl.ds(pl.multiple_of(block * BLOCK, BLOCK), BLOCK)
        key_rows = pl.ds(start, span)
        same = dc_ref[0] == dr_ref[0, :, key_rows]
        first = b_ref[0, 0, :, key_rows]
        second = b_ref[1, 0, :, key_rows] + nb
        low_lane = lax.broadcasted_iota(jnp.int32, (BLOCK, 2 * half), 1) < half

        def shifted(p, c):
            return pl.ds(pl.multiple_of(c * width + p * 2 * half, 2 * half), 2 * half)

        def one_pair(p, carry):
            cols = shifted(p, 0)
            q2 = qkv_ref[own_rows, cols]
            k2 = qkv_ref[key_rows, shifted(p, 1)]
            v2 = qkv_ref[key_rows, shifted(p, 2)]
            outs = []
            for e in range(2):
                qm = jnp.where(low_lane == (e == 0), q2, jnp.zeros_like(q2))
                raw = dot_nt(qm, k2)
                trow = jnp.broadcast_to(t_ref[2 * p + e], (BLOCK, BLOCK))
                bias = jnp.concatenate(
                    [
                        jnp.take_along_axis(
                            trow, first[:, c : c + BLOCK], axis=1, mode="promise_in_bounds"
                        )
                        + jnp.take_along_axis(
                            trow, second[:, c : c + BLOCK], axis=1, mode="promise_in_bounds"
                        )
                        for c in range(0, span, BLOCK)
                    ],
                    axis=1,
                )
                scores = jnp.where(same, raw * scale + bias, mask_fill)
                top = jnp.max(scores, axis=1, keepdims=True)
                weights = jnp.exp(scores - top)
                probs = weights * (1.0 / jnp.sum(weights, axis=1, keepdims=True))
                p_ref[2 * p + e, 0] = probs
                outs.append(dot(probs.astype(BF16), v2))
            ctx_ref[:, cols] = jnp.where(low_lane, outs[0], outs[1]).astype(BF16)
            return carry

        lax.fori_loop(0, pairs, one_pair, 0, unroll=True)

    return pl.pallas_call(
        body,
        grid_spec=pltpu.PrefetchScalarGridSpec(
            num_scalar_prefetch=1,
            grid=(blocks,),
            in_specs=[
                pl.BlockSpec((rows, 3 * width), lambda i, w: (0, 0)),
                pl.BlockSpec((1, 1, rows), lambda i, w: (w[0], 0, 0)),
                pl.BlockSpec((1, BLOCK, 1), lambda i, w: (w[0], i, 0)),
                pl.BlockSpec((2, 1, BLOCK, rows), lambda i, w: (0, w[0], i, 0)),
                pl.BlockSpec((heads, 1, BLOCK), lambda i, w: (0, 0, 0)),
            ],
            out_specs=[
                pl.BlockSpec((BLOCK, width), lambda i, w: (i, 0)),
                pl.BlockSpec((heads, 1, BLOCK, span), lambda i, w: (0, i, 0, 0)),
            ],
        ),
        out_shape=[
            jax.ShapeDtypeStruct((rows, width), BF16),
            jax.ShapeDtypeStruct((heads, blocks, BLOCK, span), F32),
        ],
        cost_estimate=pl.CostEstimate(flops=ATTEND_FLOPS, transcendentals=0, bytes_accessed=1 << 23),
        name="attend",
    )(which, qkv, doc_row, doc_col, buckets, lookup)


def attend_back(which, qkvs, grads, probs, buckets, nb):
    rows, width = qkvs[0].shape[0], qkvs[0].shape[1] // 3
    heads, blocks, _, span = probs[0].shape
    pairs = heads // 2
    half = width // heads
    scale = 1.0 / math.sqrt(half)
    group = 8
    codes = 2 * nb
    lanes = 2 * 2 * heads * group

    def body(
        which_ref, qkv_a, qkv_b, g_a, g_b, p_a, p_b, b_ref, d_a, d_b, tab_ref, gs_ref, acc_a, acc_b, acc_ref
    ):
        block = pl.program_id(0)
        start = pl.multiple_of(jnp.clip(block - 1, 0, blocks - 3) * BLOCK, BLOCK)
        own_rows = pl.ds(pl.multiple_of(block * BLOCK, BLOCK), BLOCK)
        key_rows = pl.ds(start, span)
        low_lane = lax.broadcasted_iota(jnp.int32, (BLOCK, 2 * half), 1) < half

        @pl.when(block == 0)
        def _():
            acc_a[...] = jnp.zeros_like(acc_a)
            acc_b[...] = jnp.zeros_like(acc_b)
            acc_ref[...] = jnp.zeros_like(acc_ref)

        for side, (qkv_ref, g_ref, p_ref, d_ref, sums) in enumerate(
            ((qkv_a, g_a, p_a, d_a, acc_a), (qkv_b, g_b, p_b, d_b, acc_b))
        ):

            def shifted(p, c):
                return pl.ds(pl.multiple_of(c * width + p * 2 * half, 2 * half), 2 * half)

            def one_pair(p, carry):
                cols = shifted(p, 0)
                q2 = qkv_ref[own_rows, cols]
                g2 = g_ref[:, cols]
                k2 = qkv_ref[key_rows, shifted(p, 1)]
                v2 = qkv_ref[key_rows, shifted(p, 2)]
                dqs = []
                dk = sums[0, key_rows, cols]
                dv = sums[1, key_rows, cols]
                for e in range(2):
                    mine = low_lane == (e == 0)
                    qm = jnp.where(mine, q2, jnp.zeros_like(q2))
                    gm = jnp.where(mine, g2, jnp.zeros_like(g2))
                    pr = p_ref[2 * p + e, 0]
                    gp = dot_nt(gm, v2)
                    gs = pr * (gp - jnp.sum(pr * gp, axis=1, keepdims=True))
                    gs_ref[side * heads + 2 * p + e] = gs
                    raw = (gs * scale).astype(BF16)
                    dqs.append(dot(raw, k2))
                    dk = dk + dot_tn(raw, qm)
                    dv = dv + dot_tn(pr.astype(BF16), gm)
                d_ref[own_rows, cols] = jnp.where(low_lane, dqs[0], dqs[1]).astype(BF16)
                sums[0, key_rows, cols] = dk
                sums[1, key_rows, cols] = dv
                return carry

            lax.fori_loop(0, pairs, one_pair, 0, unroll=True)

        code_ids = lax.broadcasted_iota(jnp.int32, (nb, span), 0)

        def one_group(g, carry):
            r8 = pl.ds(pl.multiple_of(g * group, group), group)
            b0 = b_ref[0, 0, r8, key_rows]
            b1 = b_ref[1, 0, r8, key_rows]
            pieces = []
            for r in range(group):
                for b in (b0, b1):
                    row = jnp.broadcast_to(b[r : r + 1], (nb, span))
                    pieces.append(jnp.where(row == code_ids, 1.0, 0.0).astype(BF16))
            onehot = jnp.concatenate(pieces, axis=0)
            gg = gs_ref[:, r8, :].reshape(2 * heads * group, span)
            upper = gg.astype(BF16)
            lower = (gg - upper.astype(F32)).astype(BF16)
            both = jnp.concatenate([upper, lower], axis=0)
            acc_ref[...] += dot_nt(onehot, both)
            return carry

        lax.fori_loop(0, BLOCK // group, one_group, 0)

        @pl.when(block == blocks - 1)
        def _():
            for d_ref, sums in ((d_a, acc_a), (d_b, acc_b)):
                d_ref[:, width : 2 * width] = sums[0].astype(BF16)
                d_ref[:, 2 * width :] = sums[1].astype(BF16)
            lane_row = lax.broadcasted_iota(jnp.int32, (codes, lanes), 1) % group
            total = jnp.zeros((codes, lanes), F32)
            for r in range(group):
                total = total + jnp.where(
                    lane_row == r, acc_ref[r * codes : (r + 1) * codes, :], 0.0
                )
            tab_ref[...] = total

    whole = pl.BlockSpec((rows, 3 * width), lambda i, w: (0, 0))
    part = pl.BlockSpec((BLOCK, width), lambda i, w: (i, 0))
    prob = pl.BlockSpec((heads, 1, BLOCK, span), lambda i, w: (0, i, 0, 0))
    shape = jax.ShapeDtypeStruct((rows, 3 * width), BF16)
    d_a, d_b, tab = pl.pallas_call(
        body,
        grid_spec=pltpu.PrefetchScalarGridSpec(
            num_scalar_prefetch=1,
            grid=(blocks,),
            in_specs=[
                whole, whole, part, part, prob, prob,
                pl.BlockSpec((2, 1, BLOCK, rows), lambda i, w: (0, w[0], i, 0)),
            ],
            out_specs=[whole, whole, pl.BlockSpec((codes, lanes), lambda i, w: (0, 0))],
            scratch_shapes=[
                pltpu.VMEM((2 * heads, BLOCK, span), F32),
                pltpu.VMEM((2, rows, width), F32),
                pltpu.VMEM((2, rows, width), F32),
                pltpu.VMEM((group * codes, lanes), F32),
            ],
        ),
        out_shape=[shape, shape, jax.ShapeDtypeStruct((codes, lanes), F32)],
        cost_estimate=pl.CostEstimate(
            flops=BACK_FLOPS, transcendentals=0, bytes_accessed=1 << 24
        ),
        name="attend_back",
    )(which, *qkvs, *grads, *probs, buckets)
    total = tab.reshape(2, nb, 2, 2, heads, group).sum(axis=(2, 5))
    return d_a, d_b, total[:, :, 0], total[:, :, 1]


def swap(value):
    size = lax.axis_size("tensor")
    return lax.ppermute(value, "tensor", [(i, (i + 1) % size) for i in range(size)])


def ring_bits(turned):
    size = lax.axis_size("dp")
    bits = [1 << k for k in range(size.bit_length() - 1)]
    if turned:
        bits[0], bits[1] = bits[1], bits[0]
    return bits


def across(value, bit):
    size = lax.axis_size("dp")
    return lax.ppermute(value, "dp", [(i, i ^ bit) for i in range(size)])


def side_of(bit):
    return (lax.axis_index("dp") >> (bit.bit_length() - 1)) & 1


def parted(value, bit):
    side = side_of(bit)
    half = value.shape[0] // 2
    keep = lax.dynamic_slice_in_dim(value, side * half, half, 0, allow_negative_indices=False)
    send = lax.dynamic_slice_in_dim(
        value, (1 - side) * half, half, 0, allow_negative_indices=False
    )
    return keep, send


def ring_scatter(value, bits):
    for bit in bits:
        keep, send = parted(value, bit)
        value = keep + across(send, bit)
    return value


def ring_gather(value, bits):
    for bit in reversed(bits):
        low_side = side_of(bit) == 0
        other = across(value, bit)
        value = jnp.concatenate(
            [jnp.where(low_side, value, other), jnp.where(low_side, other, value)]
        )
    return value


def update(clip_factor, grads, state):
    share = state[0].shape[1] // BLOCK
    start = lax.axis_index("dp").astype(jnp.int32) * share
    wide, wide_info, thin, thin_info = [], [], [], []
    base = 0
    row = 0
    for grad in grads:
        rows = grad.size // BLOCK
        if grad.ndim == 2 and grad.shape[1] % BLOCK == 0 and grad.shape[0] > 16:
            lanes = grad.shape[1] // BLOCK
            grad = jnp.pad(grad, ((0, -grad.shape[0] % 8), (0, 0)))
            slab = min(grad.shape[0], -(-(share // lanes + 18) // 8) * 8)
            wide.append(grad)
            wide_info.append((base, lanes, grad.shape[0], slab))
        else:
            thin.append(jnp.pad(grad.reshape(rows, BLOCK), ((0, -rows % 8), (0, 0))))
            thin_info.append((base, row, rows))
            row += rows + -rows % 8
        base += rows
    thin_all = jnp.concatenate(thin)
    margin = -(-max(info[1] * info[3] for info in wide_info) // 8) * 8 + 8

    def slab_start(first, info):
        base, lanes, rows, slab = info
        wanted = jnp.maximum(first - base, 0) // (lanes * 8) * 8
        return pl.multiple_of(jnp.minimum(wanted, rows - slab), 8)

    def body(start_ref, clip_ref, *refs):
        wide_refs = refs[: len(wide)]
        thin_ref = refs[len(wide)]
        master, one, two, ema = refs[len(wide) + 1 : len(wide) + 5]
        new_master, new_one, new_two, new_ema, copy, own = refs[len(wide) + 5 :]
        first = start_ref[0]
        own[margin : margin + share, :] = jnp.zeros((share, BLOCK), F32)
        for ref, info in zip(wide_refs, wide_info):
            base, lanes, rows, slab = info

            @pl.when((first < base + rows * lanes) & (first + share > base))
            def _():
                place = margin + base + slab_start(first, info) * lanes - first
                for k in range(lanes):
                    own[pl.ds(place + k, slab, stride=lanes), :] = ref[
                        :, k * BLOCK : (k + 1) * BLOCK
                    ]

        for base, row, rows in thin_info:

            @pl.when((first < base + rows) & (first + share > base))
            def _():
                own[pl.ds(margin + base - first, rows), :] = thin_ref[row : row + rows, :]

        scale = clip_ref[0]

        def advance(row, rows):
            many = -(-rows // 8) * 8
            grad = own[pl.ds(pl.multiple_of(margin + row, 8), many), :].reshape(1, many * BLOCK)
            grad = grad[:, : rows * BLOCK] * scale
            place = (slice(None), pl.ds(pl.multiple_of(row * BLOCK, 8 * BLOCK), rows * BLOCK))
            moment = beta_one * one[place] + (1.0 - beta_one) * grad
            second = beta_two * two[place] + (1.0 - beta_two) * grad * grad
            new_one[place] = moment
            new_two[place] = second
            step_size = (
                moment
                / (1.0 - beta_one**STEP)
                / (jnp.sqrt(second / (1.0 - beta_two**STEP)) + adam_eps)
            )
            weight = master[place]
            weight = weight - learn_rate * (step_size + decay_rate * weight)
            new_master[place] = weight
            new_ema[place] = average_rate * ema[place] + (1.0 - average_rate) * weight
            copy[place] = weight.astype(BF16)

        def many_rows(number, carry):
            advance(number * CHUNK, CHUNK)
            return carry

        lax.fori_loop(0, share // CHUNK, many_rows, 0)
        if share % CHUNK:
            advance(share // CHUNK * CHUNK, share % CHUNK)

    plain = pl.BlockSpec((1, share * BLOCK), lambda i, s: (0, 0))
    specs = [pl.BlockSpec(memory_space=pltpu.SMEM)]
    for grad, info in zip(wide, wide_info):
        specs.append(
            pl.BlockSpec(
                (pl.Element(info[3]), pl.Element(grad.shape[1])),
                lambda i, s, info=info: (slab_start(s[0], info), 0),
            )
        )
    specs.append(pl.BlockSpec(thin_all.shape, lambda i, s: (0, 0)))
    flat = jax.ShapeDtypeStruct((1, share * BLOCK), F32)
    return pl.pallas_call(
        body,
        grid_spec=pltpu.PrefetchScalarGridSpec(
            num_scalar_prefetch=1,
            grid=(1,),
            in_specs=specs + [plain] * 4,
            out_specs=[plain] * 5,
            scratch_shapes=[pltpu.VMEM((2 * margin + share + 8, BLOCK), F32)],
        ),
        out_shape=[flat] * 4 + [jax.ShapeDtypeStruct((1, share * BLOCK), BF16)],
        name="update",
    )(
        start.reshape(1),
        clip_factor.reshape(1),
        *wide,
        thin_all,
        *state,
    )


def per_device(
    hidden_in,
    cotangent,
    box_coords,
    doc_ids,
    buckets,
    layout_weight,
    norm_gains,
    norm_shifts,
    branch_biases,
    qkv_weight,
    query_value_bias,
    output_weight,
    ffn_in_weight,
    ffn_in_bias,
    ffn_out_weight,
    relative_table,
    master_flat,
    moment_one,
    moment_two,
    ema_flat,
):
    turn = lax.axis_index("tensor")
    window = turn.astype(jnp.int32).reshape(1)
    gains = norm_gains.astype(F32)
    norm_offsets = norm_shifts.astype(F32)
    biases = branch_biases.astype(F32)

    small_own = jnp.concatenate(
        [query_value_bias.reshape(-1), ffn_in_bias, relative_table.reshape(-1)]
    )
    qkv_other = swap(qkv_weight)
    small_other = swap(small_own)
    output_other = swap(output_weight)
    ffn_in_other = swap(ffn_in_weight)
    ffn_out_other = swap(ffn_out_weight)
    cuts = (query_value_bias.size, query_value_bias.size + ffn_in_bias.size)
    qv_bias_other = small_other[: cuts[0]].reshape(query_value_bias.shape)
    ffn_bias_other = small_other[cuts[0] : cuts[1]]
    table_other = small_other[cuts[1] :].reshape(relative_table.shape)

    features = box_features(box_coords).astype(BF16)
    embedded = hidden_in.astype(F32) + dot_tn(features, layout_weight)
    inputs = embedded.astype(BF16)
    inputs_swap = swap(inputs)

    def project(weight, bias):
        shift = jnp.stack([bias[0], jnp.zeros_like(bias[0]), bias[1]]).astype(F32)
        return jnp.concatenate(
            [(dot(inputs, weight[c]) + shift[c]).astype(BF16) for c in range(3)], axis=1
        )

    qkv_a = project(qkv_weight, query_value_bias)
    context_a, probs_a = attend(window, qkv_a, doc_ids, buckets, relative_table)
    qkv_b = project(qkv_other, qv_bias_other)
    context_b, probs_b = attend(window, qkv_b, doc_ids, buckets, table_other)
    context_swap = swap(context_b)
    attn_out = dot(context_a, output_weight) + dot(context_b, output_other) + biases[0]
    normed_one, inv_std_one = normalize(embedded + attn_out)
    mid_norm = normed_one * gains[0] + norm_offsets[0]
    mid_low = mid_norm.astype(BF16)
    mid_swap = swap(mid_low)

    def expand(weight, bias):
        pre = dot(mid_low, weight) + bias.astype(F32)
        share = 0.5 + 0.5 * lax.erf(pre * math.sqrt(0.5))
        slope = share + pre * (math.sqrt(0.5 / math.pi) * jnp.exp(-0.5 * pre * pre))
        return (pre * share).astype(BF16), slope

    hidden_a, slope_a = expand(ffn_in_weight, ffn_in_bias)
    hidden_b, slope_b = expand(ffn_in_other, ffn_bias_other)
    hidden_swap = swap(hidden_b)
    branch = dot(hidden_a, ffn_out_weight) + dot(hidden_b, ffn_out_other) + biases[1]
    normed_two, inv_std_two = normalize(mid_norm + branch)
    hidden_out = (normed_two * gains[1] + norm_offsets[1]).astype(BF16)
    grad_out = cotangent.astype(F32)
    gain_two = jnp.sum(grad_out * normed_two, axis=0)
    shift_two = jnp.sum(grad_out, axis=0)
    grad_sum_two = norm_back(grad_out, normed_two, inv_std_two, gains[1])
    bias_two = jnp.sum(grad_sum_two, axis=0)
    grad_branch = grad_sum_two.astype(BF16)
    grad_branch_swap = swap(grad_branch)

    grad_pre_b = (slope_b * dot_nt(grad_branch, ffn_out_other)).astype(BF16)
    grad_pre_swap = swap(grad_pre_b)
    grad_pre_a = (slope_a * dot_nt(grad_branch, ffn_out_weight)).astype(BF16)
    ffn_out_low = (
        dot_tn(hidden_a, grad_branch) + dot_tn(hidden_swap, grad_branch_swap)
    ).astype(BF16)
    ffn_in_low = (dot_tn(mid_low, grad_pre_a) + dot_tn(mid_swap, grad_pre_swap)).astype(BF16)
    ffn_bias_grad = jnp.sum(grad_pre_a.astype(F32), axis=0) + jnp.sum(
        grad_pre_swap.astype(F32), axis=0
    )
    grad_mid = (
        grad_sum_two + dot_nt(grad_pre_a, ffn_in_weight) + dot_nt(grad_pre_b, ffn_in_other)
    )
    gain_one = jnp.sum(grad_mid * normed_one, axis=0)
    shift_one = jnp.sum(grad_mid, axis=0)
    grad_sum_one = norm_back(grad_mid, normed_one, inv_std_one, gains[0])
    bias_one = jnp.sum(grad_sum_one, axis=0)
    grad_attn = grad_sum_one.astype(BF16)
    grad_attn_swap = swap(grad_attn)
    output_grad = dot_tn(context_a, grad_attn) + dot_tn(context_swap, grad_attn_swap)
    grad_context_a = dot_nt(grad_attn, output_weight).astype(BF16)
    grad_context_b = dot_nt(grad_attn, output_other).astype(BF16)

    bits_a, bits_b = ring_bits(False), ring_bits(True)
    out_keep, out_send = parted(
        jnp.concatenate([ffn_out_low, output_grad.astype(BF16)]), bits_a[0]
    )
    in_keep, in_send = parted(ffn_in_low, bits_b[0])
    grad_context_a, grad_context_b, out_send, in_send = lax.optimization_barrier(
        (grad_context_a, grad_context_b, out_send, in_send)
    )
    out_sum = out_keep + across(out_send, bits_a[0])
    in_sum = in_keep + across(in_send, bits_b[0])
    grads_a, grads_b, table_a, table_b = attend_back(
        window, (qkv_a, qkv_b), (grad_context_a, grad_context_b), (probs_a, probs_b), buckets, NB
    )
    out_keep, out_send = parted(out_sum, bits_a[1])
    in_keep, in_send = parted(in_sum, bits_b[1])
    grads_a, grads_b, table_a, table_b, out_send, in_send = lax.optimization_barrier(
        (grads_a, grads_b, table_a, table_b, out_send, in_send)
    )
    out_sum = out_keep + across(out_send, bits_a[1])
    in_sum = in_keep + across(in_send, bits_b[1])
    width = qkv_weight.shape[2]
    grads_swap = swap(grads_b)
    table_grad = table_a + swap(table_b)
    halves = jnp.split(inputs, 2, axis=1)
    halves_swap = jnp.split(inputs_swap, 2, axis=1)
    pack_a, pack_b = (
        (dot_tn(left, grads_a) + dot_tn(right, grads_swap)).astype(BF16)
        for left, right in zip(halves, halves_swap)
    )
    qv_sums = jnp.sum(grads_a.astype(F32), axis=0) + jnp.sum(grads_swap.astype(F32), axis=0)
    qv_bias_grad = jnp.stack([qv_sums[:width], qv_sums[2 * width :]])
    input_grad = grad_sum_one + sum(
        dot_nt(grads[:, c * width : (c + 1) * width], weight[c])
        for grads, weight in ((grads_a, qkv_weight), (grads_b, qkv_other))
        for c in range(3)
    )
    layout_part = dot(features, input_grad.astype(BF16))
    shared = jnp.concatenate(
        [
            layout_part,
            jnp.stack([gain_one, gain_two, shift_one, shift_two, bias_one, bias_two]),
        ]
    )
    cut = shared.shape[0] // lax.axis_size("tensor")
    first_turn = turn == 0
    own_shared = jnp.where(first_turn, shared[:cut], shared[cut:])
    own_shared = own_shared + swap(
        jnp.where(first_turn, shared[cut:], shared[:cut]).astype(BF16)
    ).astype(F32)

    model = layout_part.shape[1]
    small = jnp.concatenate(
        [ffn_bias_grad, qv_bias_grad.reshape(-1), table_grad.reshape(-1)]
    ).astype(BF16)
    small = jnp.pad(small, (0, -small.size % (16 * model))).reshape(-1, model)
    own_rows = own_shared.shape[0] + -own_shared.shape[0] % 16
    unit = 8 * lax.axis_size("dp")
    fill = -(own_rows + small.shape[0]) % unit
    pack_c = jnp.concatenate(
        [
            jnp.pad(own_shared.astype(BF16), ((0, own_rows - own_shared.shape[0]), (0, 0))),
            jnp.pad(small, ((0, fill), (0, 0))),
        ]
    )

    pack_a, late_a = parted(pack_a, bits_a[0])
    pack_b, late_b = parted(pack_b, bits_b[0])
    out_keep, out_send = parted(out_sum, bits_a[2])
    in_keep, in_send = parted(in_sum, bits_b[2])
    late_a, late_b, out_send, in_send = lax.optimization_barrier(
        (late_a, late_b, out_send, in_send)
    )
    pack_a = pack_a + across(late_a, bits_a[0])
    pack_b = pack_b + across(late_b, bits_b[0])
    out_sum = out_keep + across(out_send, bits_a[2])
    in_sum = in_keep + across(in_send, bits_b[2])
    out_all = ring_gather(ring_scatter(out_sum, bits_a[3:]), bits_a)
    ffn_in_low = ring_gather(ring_scatter(in_sum, bits_b[3:]), bits_b)
    pack_a = ring_gather(ring_scatter(pack_a, bits_a[1:]), bits_a)
    pack_b = ring_gather(ring_scatter(pack_b, bits_b[1:]), bits_b)
    pack_c = ring_gather(ring_scatter(pack_c, bits_b), bits_b)

    square = sum(
        jnp.sum(jnp.square(member.astype(F32)))
        for member in (out_all, ffn_in_low, pack_a, pack_b, pack_c)
    )
    ffn_out_grad = out_all[: ffn_out_low.shape[0]].astype(F32)
    output_grad = out_all[ffn_out_low.shape[0] :].astype(F32)
    ffn_in_grad = ffn_in_low.astype(F32)
    qkv_grad = jnp.stack(
        [
            jnp.concatenate([part[:, c * width : (c + 1) * width] for part in (pack_a, pack_b)])
            for c in range(3)
        ]
    ).astype(F32)
    own_low = pack_c[:cut]
    small = pack_c[own_rows:].reshape(-1).astype(F32)
    place = 0
    smalls = []
    for member in (ffn_bias_grad, qv_bias_grad, table_grad):
        smalls.append(small[place : place + member.size].reshape(member.shape))
        place += member.size
    ffn_bias_grad, qv_bias_grad, table_grad = smalls
    other_low = swap(own_low)
    shared = jnp.where(
        first_turn,
        jnp.concatenate([own_low, other_low]),
        jnp.concatenate([other_low, own_low]),
    ).astype(F32)
    layout_grad = shared[: layout_part.shape[0]]
    gains_grad, shifts_grad, biases_grad = jnp.split(shared[layout_part.shape[0] :], 3)

    grad_norm = jnp.sqrt(square + swap(square))
    clip_factor = clip_limit / jnp.maximum(grad_norm, clip_limit)
    updated = update(
        clip_factor,
        (
            ffn_in_grad,
            ffn_bias_grad,
            ffn_out_grad,
            qkv_grad.reshape(-1, width),
            qv_bias_grad,
            output_grad,
            table_grad,
            own_low.astype(F32),
        ),
        (master_flat, moment_one, moment_two, ema_flat),
    )
    return (
        hidden_out,
        input_grad,
        layout_grad,
        gains_grad,
        shifts_grad,
        biases_grad,
        qkv_grad,
        qv_bias_grad,
        output_grad,
        ffn_in_grad,
        ffn_bias_grad,
        ffn_out_grad,
        table_grad,
        grad_norm,
    ) + tuple(updated)


def solution(mesh):
    return jax.shard_map(
        per_device,
        mesh=mesh,
        in_specs=(
            P(("dp", "tensor"), None),
            P(("dp", "tensor"), None),
            P(None, ("dp", "tensor")),
            P("dp", None),
            P(None, "dp", None, None),
            P(),
            P(),
            P(),
            P(),
            P(None, None, "tensor"),
            P(None, "tensor"),
            P("tensor", None),
            P(None, "tensor"),
            P("tensor"),
            P("tensor", None),
            P(None, None, "tensor"),
            P("tensor", "dp"),
            P("tensor", "dp"),
            P("tensor", "dp"),
            P("tensor", "dp"),
        ),
        out_specs=(
            P(("dp", "tensor"), None),
            P(("dp", "tensor"), None),
            P(),
            P(),
            P(),
            P(),
            P(None, None, "tensor"),
            P(None, "tensor"),
            P("tensor", None),
            P(None, "tensor"),
            P("tensor"),
            P("tensor", None),
            P(None, None, "tensor"),
            P(),
            P("tensor", "dp"),
            P("tensor", "dp"),
            P("tensor", "dp"),
            P("tensor", "dp"),
            P("tensor", "dp"),
        ),
        check_vma=False,
    )
```

```python
import math

import jax
import jax.numpy as jnp
from jax import lax
from jax.experimental import pallas as pl
from jax.experimental.pallas import tpu as pltpu
from jax.sharding import PartitionSpec as P

NB = 32
FEAT = 256
STEP = 10
BLOCK = 128
CHUNK = 32
ATTEND_FLOPS = 1 << 33
BACK_FLOPS = 1 << 35
NO_COST = pl.CostEstimate(flops=1, transcendentals=0, bytes_accessed=1)


norm_eps = 1e-05
learn_rate = 0.02
beta_one = 0.9
beta_two = 0.999
adam_eps = 1e-08
decay_rate = 0.01
average_rate = 0.5
clip_limit = 1.0
mask_fill = -1e30

F32 = jnp.float32
BF16 = jnp.bfloat16
NT = (((1,), (1,)), ((), ()))
TN = (((0,), (0,)), ((), ()))


def dot(left, right):
    return jnp.dot(left, right, preferred_element_type=F32)


def dot_nt(left, right):
    return lax.dot_general(left, right, NT, preferred_element_type=F32)


def dot_tn(left, right):
    return lax.dot_general(left, right, TN, preferred_element_type=F32)


def box_features(coords):
    count = FEAT // 8
    freqs = jnp.exp(-math.log(10000.0) * jnp.arange(count, dtype=F32) / count)
    angles = coords.astype(F32)[:, None, :] * freqs[None, :, None]
    waves = jnp.stack([jnp.sin(angles), jnp.cos(angles)], axis=1)
    return waves.reshape(FEAT, coords.shape[1])


def normalize(value):
    centre = value - jnp.mean(value, axis=-1, keepdims=True)
    inv_std = lax.rsqrt(jnp.mean(centre * centre, axis=-1, keepdims=True) + norm_eps)
    return (centre * inv_std, inv_std)


def norm_back(grad_out, normed, inv_std, gain):
    scaled = grad_out * gain
    return inv_std * (
        scaled
        - jnp.mean(scaled, axis=-1, keepdims=True)
        - normed * jnp.mean(scaled * normed, axis=-1, keepdims=True)
    )


def attend(which, qkv, docs, buckets, table):
    rows, width = qkv.shape[0], qkv.shape[1] // 3
    nb, heads = table.shape[1:]
    pairs = heads // 2
    half = width // heads
    span = 3 * BLOCK
    blocks = rows // BLOCK
    scale = 1.0 / math.sqrt(half)
    lookup = jnp.pad(
        jnp.concatenate([table[0], table[1]], axis=0).astype(F32).T,
        ((0, 0), (0, BLOCK - 2 * nb)),
    ).reshape(heads, 1, BLOCK)
    doc_row = docs[:, None, :]
    doc_col = docs[:, :, None]

    def body(which_ref, qkv_ref, dr_ref, dc_ref, b_ref, t_ref, ctx_ref, p_ref):
        block = pl.program_id(0)
        start = pl.multiple_of(jnp.clip(block - 1, 0, blocks - 3) * BLOCK, BLOCK)
        own_rows = pl.ds(pl.multiple_of(block * BLOCK, BLOCK), BLOCK)
        key_rows = pl.ds(start, span)
        same = dc_ref[0] == dr_ref[0, :, key_rows]
        first = b_ref[0, 0, :, key_rows]
        second = b_ref[1, 0, :, key_rows] + nb
        low_lane = lax.broadcasted_iota(jnp.int32, (BLOCK, 2 * half), 1) < half

        def shifted(p, c):
            return pl.ds(pl.multiple_of(c * width + p * 2 * half, 2 * half), 2 * half)

        def one_pair(p, carry):
            cols = shifted(p, 0)
            q2 = qkv_ref[own_rows, cols]
            k2 = qkv_ref[key_rows, shifted(p, 1)]
            v2 = qkv_ref[key_rows, shifted(p, 2)]
            outs = []
            for e in range(2):
                qm = jnp.where(low_lane == (e == 0), q2, jnp.zeros_like(q2))
                raw = dot_nt(qm, k2)
                trow = jnp.broadcast_to(t_ref[2 * p + e], (BLOCK, BLOCK))
                bias = jnp.concatenate(
                    [
                        jnp.take_along_axis(
                            trow, first[:, c : c + BLOCK], axis=1, mode="promise_in_bounds"
                        )
                        + jnp.take_along_axis(
                            trow, second[:, c : c + BLOCK], axis=1, mode="promise_in_bounds"
                        )
                        for c in range(0, span, BLOCK)
                    ],
                    axis=1,
                )
                scores = jnp.where(same, raw * scale + bias, mask_fill)
                top = jnp.max(scores, axis=1, keepdims=True)
                weights = jnp.exp(scores - top)
                probs = weights * (1.0 / jnp.sum(weights, axis=1, keepdims=True))
                p_ref[2 * p + e, 0] = probs
                outs.append(dot(probs.astype(BF16), v2))
            ctx_ref[:, cols] = jnp.where(low_lane, outs[0], outs[1]).astype(BF16)
            return carry

        lax.fori_loop(0, pairs, one_pair, 0, unroll=True)

    return pl.pallas_call(
        body,
        grid_spec=pltpu.PrefetchScalarGridSpec(
            num_scalar_prefetch=1,
            grid=(blocks,),
            in_specs=[
                pl.BlockSpec((rows, 3 * width), lambda i, w: (0, 0)),
                pl.BlockSpec((1, 1, rows), lambda i, w: (w[0], 0, 0)),
                pl.BlockSpec((1, BLOCK, 1), lambda i, w: (w[0], i, 0)),
                pl.BlockSpec((2, 1, BLOCK, rows), lambda i, w: (0, w[0], i, 0)),
                pl.BlockSpec((heads, 1, BLOCK), lambda i, w: (0, 0, 0)),
            ],
            out_specs=[
                pl.BlockSpec((BLOCK, width), lambda i, w: (i, 0)),
                pl.BlockSpec((heads, 1, BLOCK, span), lambda i, w: (0, i, 0, 0)),
            ],
        ),
        out_shape=[
            jax.ShapeDtypeStruct((rows, width), BF16),
            jax.ShapeDtypeStruct((heads, blocks, BLOCK, span), F32),
        ],
        cost_estimate=pl.CostEstimate(flops=ATTEND_FLOPS, transcendentals=0, bytes_accessed=1 << 23),
        name="attend",
    )(which, qkv, doc_row, doc_col, buckets, lookup)


def attend_back(which, qkvs, grads, probs):
    rows, width = qkvs[0].shape[0], qkvs[0].shape[1] // 3
    heads, blocks, _, span = probs[0].shape
    pairs = heads // 2
    half = width // heads
    scale = 1.0 / math.sqrt(half)

    def body(qkv_a, qkv_b, g_a, g_b, p_a, p_b, d_a, d_b, s_a, s_b, acc_a, acc_b):
        block = pl.program_id(0)
        start = pl.multiple_of(jnp.clip(block - 1, 0, blocks - 3) * BLOCK, BLOCK)
        own_rows = pl.ds(pl.multiple_of(block * BLOCK, BLOCK), BLOCK)
        key_rows = pl.ds(start, span)
        low_lane = lax.broadcasted_iota(jnp.int32, (BLOCK, 2 * half), 1) < half

        @pl.when(block == 0)
        def _():
            acc_a[...] = jnp.zeros_like(acc_a)
            acc_b[...] = jnp.zeros_like(acc_b)

        for qkv_ref, g_ref, p_ref, d_ref, s_ref, sums in (
            (qkv_a, g_a, p_a, d_a, s_a, acc_a),
            (qkv_b, g_b, p_b, d_b, s_b, acc_b),
        ):

            def shifted(p, c):
                return pl.ds(pl.multiple_of(c * width + p * 2 * half, 2 * half), 2 * half)

            def one_pair(p, carry):
                cols = shifted(p, 0)
                q2 = qkv_ref[own_rows, cols]
                g2 = g_ref[:, cols]
                k2 = qkv_ref[key_rows, shifted(p, 1)]
                v2 = qkv_ref[key_rows, shifted(p, 2)]
                dqs = []
                dk = sums[0, key_rows, cols]
                dv = sums[1, key_rows, cols]
                for e in range(2):
                    mine = low_lane == (e == 0)
                    qm = jnp.where(mine, q2, jnp.zeros_like(q2))
                    gm = jnp.where(mine, g2, jnp.zeros_like(g2))
                    pr = p_ref[2 * p + e, 0]
                    gp = dot_nt(gm, v2)
                    gs = pr * (gp - jnp.sum(pr * gp, axis=1, keepdims=True))
                    s_ref[2 * p + e, 0] = gs
                    raw = (gs * scale).astype(BF16)
                    dqs.append(dot(raw, k2))
                    dk = dk + dot_tn(raw, qm)
                    dv = dv + dot_tn(pr.astype(BF16), gm)
                d_ref[own_rows, cols] = jnp.where(low_lane, dqs[0], dqs[1]).astype(BF16)
                sums[0, key_rows, cols] = dk
                sums[1, key_rows, cols] = dv
                return carry

            lax.fori_loop(0, pairs, one_pair, 0, unroll=True)

        @pl.when(block == blocks - 1)
        def _():
            for d_ref, sums in ((d_a, acc_a), (d_b, acc_b)):
                d_ref[:, width : 2 * width] = sums[0].astype(BF16)
                d_ref[:, 2 * width :] = sums[1].astype(BF16)

    whole = pl.BlockSpec((rows, 3 * width), lambda i: (0, 0))
    part = pl.BlockSpec((BLOCK, width), lambda i: (i, 0))
    prob = pl.BlockSpec((heads, 1, BLOCK, span), lambda i: (0, i, 0, 0))
    shape = jax.ShapeDtypeStruct((rows, 3 * width), BF16)
    score = jax.ShapeDtypeStruct(probs[0].shape, F32)
    return pl.pallas_call(
        body,
        grid=(blocks,),
        in_specs=[whole, whole, part, part, prob, prob],
        out_specs=[whole, whole, prob, prob],
        scratch_shapes=[
            pltpu.VMEM((2, rows, width), F32),
            pltpu.VMEM((2, rows, width), F32),
        ],
        out_shape=[shape, shape, score, score],
        input_output_aliases={4: 2, 5: 3},
        cost_estimate=pl.CostEstimate(
            flops=BACK_FLOPS, transcendentals=0, bytes_accessed=1 << 24
        ),
        name="attend_back",
    )(*qkvs, *grads, *probs)


def table_sums(which, scores, buckets, nb):
    heads, blocks, _, span = scores[0].shape
    rows = blocks * BLOCK
    group = 8
    codes = 2 * nb
    lanes = 2 * 2 * heads * group

    def body(which_ref, s_a, s_b, b_ref, tab_ref, acc_ref):
        block = pl.program_id(0)
        start = pl.multiple_of(jnp.clip(block - 1, 0, blocks - 3) * BLOCK, BLOCK)
        key_rows = pl.ds(start, span)

        @pl.when(block == 0)
        def _():
            acc_ref[...] = jnp.zeros_like(acc_ref)

        code_ids = lax.broadcasted_iota(jnp.int32, (nb, span), 0)

        def one_group(g, carry):
            r8 = pl.ds(pl.multiple_of(g * group, group), group)
            b0 = b_ref[0, 0, r8, key_rows]
            b1 = b_ref[1, 0, r8, key_rows]
            pieces = []
            for r in range(group):
                for b in (b0, b1):
                    row = jnp.broadcast_to(b[r : r + 1], (nb, span))
                    pieces.append(jnp.where(row == code_ids, 1.0, 0.0).astype(BF16))
            onehot = jnp.concatenate(pieces, axis=0)
            gg = jnp.concatenate(
                [ref[:, 0, r8, :].reshape(heads * group, span) for ref in (s_a, s_b)], axis=0
            )
            upper = gg.astype(BF16)
            lower = (gg - upper.astype(F32)).astype(BF16)
            both = jnp.concatenate([upper, lower], axis=0)
            acc_ref[...] += dot_nt(onehot, both)
            return carry

        lax.fori_loop(0, BLOCK // group, one_group, 0)

        @pl.when(block == blocks - 1)
        def _():
            lane_row = lax.broadcasted_iota(jnp.int32, (codes, lanes), 1) % group
            total = jnp.zeros((codes, lanes), F32)
            for r in range(group):
                total = total + jnp.where(
                    lane_row == r, acc_ref[r * codes : (r + 1) * codes, :], 0.0
                )
            tab_ref[...] = total

    prob = pl.BlockSpec((heads, 1, BLOCK, span), lambda i, w: (0, i, 0, 0))
    tab = pl.pallas_call(
        body,
        grid_spec=pltpu.PrefetchScalarGridSpec(
            num_scalar_prefetch=1,
            grid=(blocks,),
            in_specs=[
                prob,
                prob,
                pl.BlockSpec((2, 1, BLOCK, rows), lambda i, w: (0, w[0], i, 0)),
            ],
            out_specs=pl.BlockSpec((codes, lanes), lambda i, w: (0, 0)),
            scratch_shapes=[pltpu.VMEM((group * codes, lanes), F32)],
        ),
        out_shape=jax.ShapeDtypeStruct((codes, lanes), F32),
        cost_estimate=NO_COST,
        name="table_sums",
    )(which, *scores, buckets)
    total = tab.reshape(2, nb, 2, 2, heads, group).sum(axis=(2, 5))
    return total[:, :, 0], total[:, :, 1]


def input_back(grads_a, grads_b, weight_a, weight_b, grad_sum, features, inputs):
    width = weight_a.shape[2]

    def body(g_a, g_b, w_a, w_b, sum_ref, f_ref, x_ref, in_ref, lay_ref, prod_ref, col_ref):
        total = sum_ref[...]
        for g_ref, w_ref in ((g_a, w_a), (g_b, w_b)):
            for c in range(3):
                total = total + dot_nt(g_ref[:, c * width : (c + 1) * width], w_ref[c])
        in_ref[...] = total
        lay_ref[...] = dot(f_ref[...], total.astype(BF16))
        prod_ref[...] = dot_tn(x_ref[...], g_a[...])
        col_ref[...] = jnp.sum(g_a[...].astype(F32), axis=0, keepdims=True)

    model = inputs.shape[1]
    return pl.pallas_call(
        body,
        out_shape=[
            jax.ShapeDtypeStruct(grad_sum.shape, F32),
            jax.ShapeDtypeStruct((features.shape[0], model), F32),
            jax.ShapeDtypeStruct((model, 3 * width), F32),
            jax.ShapeDtypeStruct((1, 3 * width), F32),
        ],
        cost_estimate=NO_COST,
        name="input_back",
    )(grads_a, grads_b, weight_a, weight_b, grad_sum, features, inputs)


def pair_back(inputs, grads, product, columns):
    model = inputs.shape[1]
    wide = grads.shape[1]

    def body(x_ref, g_ref, prod_ref, col_ref, a_ref, b_ref, sum_ref):
        total = (prod_ref[...] + dot_tn(x_ref[...], g_ref[...])).astype(BF16)
        a_ref[...] = total[: model // 2]
        b_ref[...] = total[model // 2 :]
        sum_ref[...] = col_ref[...] + jnp.sum(g_ref[...].astype(F32), axis=0, keepdims=True)

    half = jax.ShapeDtypeStruct((model // 2, wide), BF16)
    return pl.pallas_call(
        body,
        out_shape=[half, half, jax.ShapeDtypeStruct((1, wide), F32)],
        cost_estimate=NO_COST,
        name="pair_back",
    )(inputs, grads, product, columns)


def swap(value):
    size = lax.axis_size("tensor")
    return lax.ppermute(value, "tensor", [(i, (i + 1) % size) for i in range(size)])


def ring_bits(turned):
    size = lax.axis_size("dp")
    bits = [1 << k for k in range(size.bit_length() - 1)]
    return bits[1::-1] + bits[2:] if turned else bits


def ring_steps(bits):
    return [(True, bit) for bit in bits] + [(False, bit) for bit in reversed(bits)]


def side_of(bit):
    return (lax.axis_index("dp") >> (bit.bit_length() - 1)) & 1


def begin(step, value):
    scatter, bit = step
    if not scatter:
        return value, value
    side = side_of(bit)
    half = value.shape[0] // 2
    part = lambda where: lax.dynamic_slice_in_dim(
        value, where * half, half, 0, allow_negative_indices=False
    )
    return part(side), part(1 - side)


def finish(step, kept, send):
    scatter, bit = step
    size = lax.axis_size("dp")
    received = lax.ppermute(send, "dp", [(i, i ^ bit) for i in range(size)])
    if scatter:
        return kept + received
    low = side_of(bit) == 0
    return jnp.concatenate([jnp.where(low, kept, received), jnp.where(low, received, kept)])


def ring_run(steps, value):
    for step in steps:
        value = finish(step, *begin(step, value))
    return value


def update(clip_factor, grads, state):
    share = state[0].shape[1] // BLOCK
    start = lax.axis_index("dp").astype(jnp.int32) * share
    wide, wide_info, thin, thin_info = [], [], [], []
    base = 0
    row = 0
    for grad in grads:
        rows = grad.size // BLOCK
        if grad.ndim == 2 and grad.shape[1] % BLOCK == 0 and grad.shape[0] > 16:
            lanes = grad.shape[1] // BLOCK
            grad = jnp.pad(grad, ((0, -grad.shape[0] % 8), (0, 0)))
            slab = min(grad.shape[0], -(-(share // lanes + 18) // 8) * 8)
            wide.append(grad)
            wide_info.append((base, lanes, grad.shape[0], slab))
        else:
            thin.append(jnp.pad(grad.reshape(rows, BLOCK), ((0, -rows % 8), (0, 0))))
            thin_info.append((base, row, rows))
            row += rows + -rows % 8
        base += rows
    thin_all = jnp.concatenate(thin)
    margin = -(-max(info[1] * info[3] for info in wide_info) // 8) * 8 + 8

    def slab_start(first, info):
        base, lanes, rows, slab = info
        wanted = jnp.maximum(first - base, 0) // (lanes * 8) * 8
        return pl.multiple_of(jnp.minimum(wanted, rows - slab), 8)

    def body(start_ref, clip_ref, *refs):
        wide_refs = refs[: len(wide)]
        thin_ref = refs[len(wide)]
        master, one, two, ema = refs[len(wide) + 1 : len(wide) + 5]
        new_master, new_one, new_two, new_ema, copy, own = refs[len(wide) + 5 :]
        first = start_ref[0]
        own[margin : margin + share, :] = jnp.zeros((share, BLOCK), F32)
        for ref, info in zip(wide_refs, wide_info):
            base, lanes, rows, slab = info

            @pl.when((first < base + rows * lanes) & (first + share > base))
            def _():
                place = margin + base + slab_start(first, info) * lanes - first
                for k in range(lanes):
                    own[pl.ds(place + k, slab, stride=lanes), :] = ref[
                        :, k * BLOCK : (k + 1) * BLOCK
                    ]

        for base, row, rows in thin_info:

            @pl.when((first < base + rows) & (first + share > base))
            def _():
                own[pl.ds(margin + base - first, rows), :] = thin_ref[row : row + rows, :]

        scale = clip_ref[0]

        def advance(row, rows):
            many = -(-rows // 8) * 8
            grad = own[pl.ds(pl.multiple_of(margin + row, 8), many), :].reshape(1, many * BLOCK)
            grad = grad[:, : rows * BLOCK] * scale
            place = (slice(None), pl.ds(pl.multiple_of(row * BLOCK, 8 * BLOCK), rows * BLOCK))
            moment = beta_one * one[place] + (1.0 - beta_one) * grad
            second = beta_two * two[place] + (1.0 - beta_two) * grad * grad
            new_one[place] = moment
            new_two[place] = second
            step_size = (
                moment
                / (1.0 - beta_one**STEP)
                / (jnp.sqrt(second / (1.0 - beta_two**STEP)) + adam_eps)
            )
            weight = master[place]
            weight = weight - learn_rate * (step_size + decay_rate * weight)
            new_master[place] = weight
            new_ema[place] = average_rate * ema[place] + (1.0 - average_rate) * weight
            copy[place] = weight.astype(BF16)

        def many_rows(number, carry):
            advance(number * CHUNK, CHUNK)
            return carry

        lax.fori_loop(0, share // CHUNK, many_rows, 0)
        if share % CHUNK:
            advance(share // CHUNK * CHUNK, share % CHUNK)

    plain = pl.BlockSpec((1, share * BLOCK), lambda i, s: (0, 0))
    specs = [pl.BlockSpec(memory_space=pltpu.SMEM)]
    for grad, info in zip(wide, wide_info):
        specs.append(
            pl.BlockSpec(
                (pl.Element(info[3]), pl.Element(grad.shape[1])),
                lambda i, s, info=info: (slab_start(s[0], info), 0),
            )
        )
    specs.append(pl.BlockSpec(thin_all.shape, lambda i, s: (0, 0)))
    flat = jax.ShapeDtypeStruct((1, share * BLOCK), F32)
    return pl.pallas_call(
        body,
        grid_spec=pltpu.PrefetchScalarGridSpec(
            num_scalar_prefetch=1,
            grid=(1,),
            in_specs=specs + [plain] * 4,
            out_specs=[plain] * 5,
            scratch_shapes=[pltpu.VMEM((2 * margin + share + 8, BLOCK), F32)],
        ),
        out_shape=[flat] * 4 + [jax.ShapeDtypeStruct((1, share * BLOCK), BF16)],
        name="update",
    )(
        start.reshape(1),
        clip_factor.reshape(1),
        *wide,
        thin_all,
        *state,
    )


def per_device(
    hidden_in,
    cotangent,
    box_coords,
    doc_ids,
    buckets,
    layout_weight,
    norm_gains,
    norm_shifts,
    branch_biases,
    qkv_weight,
    query_value_bias,
    output_weight,
    ffn_in_weight,
    ffn_in_bias,
    ffn_out_weight,
    relative_table,
    master_flat,
    moment_one,
    moment_two,
    ema_flat,
):
    turn = lax.axis_index("tensor")
    window = turn.astype(jnp.int32).reshape(1)
    gains = norm_gains.astype(F32)
    norm_offsets = norm_shifts.astype(F32)
    biases = branch_biases.astype(F32)

    small_own = jnp.concatenate(
        [query_value_bias.reshape(-1), ffn_in_bias, relative_table.reshape(-1)]
    )
    qkv_other = swap(qkv_weight)
    small_other = swap(small_own)
    output_other = swap(output_weight)
    ffn_in_other = swap(ffn_in_weight)
    ffn_out_other = swap(ffn_out_weight)
    cuts = (query_value_bias.size, query_value_bias.size + ffn_in_bias.size)
    qv_bias_other = small_other[: cuts[0]].reshape(query_value_bias.shape)
    ffn_bias_other = small_other[cuts[0] : cuts[1]]
    table_other = small_other[cuts[1] :].reshape(relative_table.shape)

    features = box_features(box_coords).astype(BF16)
    embedded = hidden_in.astype(F32) + dot_tn(features, layout_weight)
    inputs = embedded.astype(BF16)
    inputs_swap = swap(inputs)

    def project(weight, bias):
        shift = jnp.stack([bias[0], jnp.zeros_like(bias[0]), bias[1]]).astype(F32)
        return jnp.concatenate(
            [(dot(inputs, weight[c]) + shift[c]).astype(BF16) for c in range(3)], axis=1
        )

    qkv_a = project(qkv_weight, query_value_bias)
    context_a, probs_a = attend(window, qkv_a, doc_ids, buckets, relative_table)
    qkv_b = project(qkv_other, qv_bias_other)
    context_b, probs_b = attend(window, qkv_b, doc_ids, buckets, table_other)
    context_swap = swap(context_b)
    attn_out = dot(context_a, output_weight) + dot(context_b, output_other) + biases[0]
    normed_one, inv_std_one = normalize(embedded + attn_out)
    mid_norm = normed_one * gains[0] + norm_offsets[0]
    mid_low = mid_norm.astype(BF16)
    mid_swap = swap(mid_low)

    def expand(weight, bias):
        pre = dot(mid_low, weight) + bias.astype(F32)
        share = 0.5 + 0.5 * lax.erf(pre * math.sqrt(0.5))
        slope = share + pre * (math.sqrt(0.5 / math.pi) * jnp.exp(-0.5 * pre * pre))
        return (pre * share).astype(BF16), slope

    hidden_a, slope_a = expand(ffn_in_weight, ffn_in_bias)
    hidden_b, slope_b = expand(ffn_in_other, ffn_bias_other)
    hidden_swap = swap(hidden_b)
    branch = dot(hidden_a, ffn_out_weight) + dot(hidden_b, ffn_out_other) + biases[1]
    normed_two, inv_std_two = normalize(mid_norm + branch)
    hidden_out = (normed_two * gains[1] + norm_offsets[1]).astype(BF16)
    grad_out = cotangent.astype(F32)
    gain_two = jnp.sum(grad_out * normed_two, axis=0)
    shift_two = jnp.sum(grad_out, axis=0)
    grad_sum_two = norm_back(grad_out, normed_two, inv_std_two, gains[1])
    bias_two = jnp.sum(grad_sum_two, axis=0)
    grad_branch = grad_sum_two.astype(BF16)
    grad_branch_swap = swap(grad_branch)

    grad_pre_b = (slope_b * dot_nt(grad_branch, ffn_out_other)).astype(BF16)
    grad_pre_swap = swap(grad_pre_b)
    grad_pre_a = (slope_a * dot_nt(grad_branch, ffn_out_weight)).astype(BF16)
    ffn_out_low = (
        dot_tn(hidden_a, grad_branch) + dot_tn(hidden_swap, grad_branch_swap)
    ).astype(BF16)
    ffn_in_low = (dot_tn(mid_low, grad_pre_a) + dot_tn(mid_swap, grad_pre_swap)).astype(BF16)
    grad_mid = (
        grad_sum_two + dot_nt(grad_pre_a, ffn_in_weight) + dot_nt(grad_pre_b, ffn_in_other)
    )
    gain_one = jnp.sum(grad_mid * normed_one, axis=0)
    shift_one = jnp.sum(grad_mid, axis=0)
    grad_sum_one = norm_back(grad_mid, normed_one, inv_std_one, gains[0])
    bias_one = jnp.sum(grad_sum_one, axis=0)
    grad_attn = grad_sum_one.astype(BF16)
    grad_attn_swap = swap(grad_attn)
    output_grad = dot_tn(context_a, grad_attn) + dot_tn(context_swap, grad_attn_swap)
    grad_context_a = dot_nt(grad_attn, output_weight).astype(BF16)
    grad_context_b = dot_nt(grad_attn, output_other).astype(BF16)

    barrier = lax.optimization_barrier
    steps_a, steps_b = ring_steps(ring_bits(False)), ring_steps(ring_bits(True))
    out_keep, out_send = begin(
        steps_a[0], jnp.concatenate([ffn_out_low, output_grad.astype(BF16)])
    )
    in_keep, in_send = begin(steps_b[0], ffn_in_low)
    (grad_context_a, grad_context_b), out_send, in_send = barrier(
        ((grad_context_a, grad_context_b), out_send, in_send)
    )
    out_sum = finish(steps_a[0], out_keep, out_send)
    in_sum = finish(steps_b[0], in_keep, in_send)
    grads_a, grads_b, scores_a, scores_b = attend_back(
        window, (qkv_a, qkv_b), (grad_context_a, grad_context_b), (probs_a, probs_b)
    )
    grads_swap = swap(grads_b)

    out_keep, out_send = begin(steps_a[1], out_sum)
    in_keep, in_send = begin(steps_b[1], in_sum)
    scores_a, scores_b, out_send, in_send = barrier((scores_a, scores_b, out_send, in_send))
    out_sum = finish(steps_a[1], out_keep, out_send)
    in_sum = finish(steps_b[1], in_keep, in_send)
    table_a, table_b = table_sums(window, (scores_a, scores_b), buckets, NB)

    out_keep, out_send = begin(steps_a[2], out_sum)
    in_keep, in_send = begin(steps_b[2], in_sum)
    (
        table_a, table_b, grads_a, grads_b, grads_swap, grad_pre_a, grad_pre_swap, out_send, in_send
    ) = barrier(
        (
            table_a, table_b, grads_a, grads_b, grads_swap, grad_pre_a, grad_pre_swap, out_send, in_send
        )
    )
    out_sum = finish(steps_a[2], out_keep, out_send)
    in_sum = finish(steps_b[2], in_keep, in_send)
    width = qkv_weight.shape[2]
    input_grad, layout_part, product, columns = input_back(
        grads_a, grads_b, qkv_weight, qkv_other, grad_sum_one, features, inputs
    )
    pack_a, pack_b, qv_sums = pair_back(inputs_swap, grads_swap, product, columns)
    sums = [out_sum, in_sum, pack_a, pack_b]
    plans = [steps_a[3:], steps_b[3:], steps_a, steps_b]
    rounds = len(plans[0])
    for number in range(rounds):
        opened = [begin(plan[number], value) for plan, value in zip(plans, sums)]
        sends = [send for _, send in opened]
        if number == 1:
            (
                sends, layout_part, qv_sums, table_a, table_b, grad_pre_a, grad_pre_swap
            ) = barrier(
                (sends, layout_part, qv_sums, table_a, table_b, grad_pre_a, grad_pre_swap)
            )
        else:
            sends = barrier(sends)
        sums = [
            finish(plan[number], kept, send)
            for plan, (kept, _), send in zip(plans, opened, sends)
        ]
    sums[2:] = [ring_run(plan[rounds:-1], value) for plan, value in zip(plans[2:], sums[2:])]
    out_all, ffn_in_low, pack_a, pack_b = barrier(sums)
    pack_a = ring_run(steps_a[-1:], pack_a)
    pack_b = ring_run(steps_b[-1:], pack_b)

    qv_bias_grad = jnp.stack([qv_sums[0, :width], qv_sums[0, 2 * width :]])
    ffn_bias_grad = jnp.sum(grad_pre_a.astype(F32), axis=0) + jnp.sum(
        grad_pre_swap.astype(F32), axis=0
    )
    table_grad = table_a + swap(table_b)
    shared = jnp.concatenate(
        [
            layout_part,
            jnp.stack([gain_one, gain_two, shift_one, shift_two, bias_one, bias_two]),
        ]
    )
    cut = shared.shape[0] // lax.axis_size("tensor")
    first_turn = turn == 0
    own_shared = jnp.where(first_turn, shared[:cut], shared[cut:])
    own_shared = own_shared + swap(
        jnp.where(first_turn, shared[cut:], shared[:cut]).astype(BF16)
    ).astype(F32)

    model = layout_part.shape[1]
    small = jnp.concatenate(
        [ffn_bias_grad, qv_bias_grad.reshape(-1), table_grad.reshape(-1)]
    ).astype(BF16)
    small = jnp.pad(small, (0, -small.size % (16 * model))).reshape(-1, model)
    own_rows = own_shared.shape[0] + -own_shared.shape[0] % 16
    unit = 8 * lax.axis_size("dp")
    fill = -(own_rows + small.shape[0]) % unit
    pack_c = jnp.concatenate(
        [
            jnp.pad(own_shared.astype(BF16), ((0, own_rows - own_shared.shape[0]), (0, 0))),
            jnp.pad(small, ((0, fill), (0, 0))),
        ]
    )

    pack_c = ring_run(steps_b, pack_c)

    square = sum(
        jnp.sum(jnp.square(member.astype(F32)))
        for member in (out_all, ffn_in_low, pack_a, pack_b, pack_c)
    )
    ffn_out_grad = out_all[: ffn_out_low.shape[0]].astype(F32)
    output_grad = out_all[ffn_out_low.shape[0] :].astype(F32)
    ffn_in_grad = ffn_in_low.astype(F32)
    qkv_grad = jnp.stack(
        [
            jnp.concatenate([part[:, c * width : (c + 1) * width] for part in (pack_a, pack_b)])
            for c in range(3)
        ]
    ).astype(F32)
    own_low = pack_c[:cut]
    small = pack_c[own_rows:].reshape(-1).astype(F32)
    place = 0
    smalls = []
    for member in (ffn_bias_grad, qv_bias_grad, table_grad):
        smalls.append(small[place : place + member.size].reshape(member.shape))
        place += member.size
    ffn_bias_grad, qv_bias_grad, table_grad = smalls
    other_low = swap(own_low)
    shared = jnp.where(
        first_turn,
        jnp.concatenate([own_low, other_low]),
        jnp.concatenate([other_low, own_low]),
    ).astype(F32)
    layout_grad = shared[: layout_part.shape[0]]
    gains_grad, shifts_grad, biases_grad = jnp.split(shared[layout_part.shape[0] :], 3)

    grad_norm = jnp.sqrt(square + swap(square))
    clip_factor = clip_limit / jnp.maximum(grad_norm, clip_limit)
    updated = update(
        clip_factor,
        (
            ffn_in_grad,
            ffn_bias_grad,
            ffn_out_grad,
            qkv_grad.reshape(-1, width),
            qv_bias_grad,
            output_grad,
            table_grad,
            own_low.astype(F32),
        ),
        (master_flat, moment_one, moment_two, ema_flat),
    )
    return (
        hidden_out,
        input_grad,
        layout_grad,
        gains_grad,
        shifts_grad,
        biases_grad,
        qkv_grad,
        qv_bias_grad,
        output_grad,
        ffn_in_grad,
        ffn_bias_grad,
        ffn_out_grad,
        table_grad,
        grad_norm,
    ) + tuple(updated)


def solution(mesh):
    return jax.shard_map(
        per_device,
        mesh=mesh,
        in_specs=(
            P(("dp", "tensor"), None),
            P(("dp", "tensor"), None),
            P(None, ("dp", "tensor")),
            P("dp", None),
            P(None, "dp", None, None),
            P(),
            P(),
            P(),
            P(),
            P(None, None, "tensor"),
            P(None, "tensor"),
            P("tensor", None),
            P(None, "tensor"),
            P("tensor"),
            P("tensor", None),
            P(None, None, "tensor"),
            P("tensor", "dp"),
            P("tensor", "dp"),
            P("tensor", "dp"),
            P("tensor", "dp"),
        ),
        out_specs=(
            P(("dp", "tensor"), None),
            P(("dp", "tensor"), None),
            P(),
            P(),
            P(),
            P(),
            P(None, None, "tensor"),
            P(None, "tensor"),
            P("tensor", None),
            P(None, "tensor"),
            P("tensor"),
            P("tensor", None),
            P(None, None, "tensor"),
            P(),
            P("tensor", "dp"),
            P("tensor", "dp"),
            P("tensor", "dp"),
            P("tensor", "dp"),
            P("tensor", "dp"),
        ),
        check_vma=False,
    )
```

```python
import math

import jax
import jax.numpy as jnp
from jax import lax
from jax.experimental import pallas as pl
from jax.experimental.pallas import tpu as pltpu
from jax.sharding import PartitionSpec as P

NB = 32
FEAT = 256
STEP = 10
BLOCK = 128
CHUNK = 32
ATTEND_FLOPS = 1 << 33
BACK_FLOPS = 1 << 35
NO_COST = pl.CostEstimate(flops=1, transcendentals=0, bytes_accessed=1)


norm_eps = 1e-05
learn_rate = 0.02
beta_one = 0.9
beta_two = 0.999
adam_eps = 1e-08
decay_rate = 0.01
average_rate = 0.5
clip_limit = 1.0
mask_fill = -1e30

F32 = jnp.float32
BF16 = jnp.bfloat16
NT = (((1,), (1,)), ((), ()))
TN = (((0,), (0,)), ((), ()))


def dot(left, right):
    return jnp.dot(left, right, preferred_element_type=F32)


def dot_nt(left, right):
    return lax.dot_general(left, right, NT, preferred_element_type=F32)


def dot_tn(left, right):
    return lax.dot_general(left, right, TN, preferred_element_type=F32)


def box_features(coords):
    count = FEAT // 8
    freqs = jnp.exp(-math.log(10000.0) * jnp.arange(count, dtype=F32) / count)
    angles = coords.astype(F32)[:, None, :] * freqs[None, :, None]
    waves = jnp.stack([jnp.sin(angles), jnp.cos(angles)], axis=1)
    return waves.reshape(FEAT, coords.shape[1])


def normalize(value):
    centre = value - jnp.mean(value, axis=-1, keepdims=True)
    inv_std = lax.rsqrt(jnp.mean(centre * centre, axis=-1, keepdims=True) + norm_eps)
    return (centre * inv_std, inv_std)


def norm_back(grad_out, normed, inv_std, gain):
    scaled = grad_out * gain
    return inv_std * (
        scaled
        - jnp.mean(scaled, axis=-1, keepdims=True)
        - normed * jnp.mean(scaled * normed, axis=-1, keepdims=True)
    )


def attend(which, qkv, docs, buckets, table):
    rows, width = qkv.shape[0], qkv.shape[1] // 3
    nb, heads = table.shape[1:]
    pairs = heads // 2
    half = width // heads
    span = 3 * BLOCK
    blocks = rows // BLOCK
    scale = 1.0 / math.sqrt(half)
    lookup = jnp.pad(
        jnp.concatenate([table[0], table[1]], axis=0).astype(F32).T,
        ((0, 0), (0, BLOCK - 2 * nb)),
    ).reshape(heads, 1, BLOCK)
    doc_row = docs[:, None, :]
    doc_col = docs[:, :, None]

    def body(which_ref, qkv_ref, dr_ref, dc_ref, b_ref, t_ref, ctx_ref, p_ref):
        block = pl.program_id(0)
        start = pl.multiple_of(jnp.clip(block - 1, 0, blocks - 3) * BLOCK, BLOCK)
        own_rows = pl.ds(pl.multiple_of(block * BLOCK, BLOCK), BLOCK)
        key_rows = pl.ds(start, span)
        same = dc_ref[0] == dr_ref[0, :, key_rows]
        first = b_ref[0, 0, :, key_rows]
        second = b_ref[1, 0, :, key_rows] + nb
        low_lane = lax.broadcasted_iota(jnp.int32, (BLOCK, 2 * half), 1) < half

        def shifted(p, c):
            return pl.ds(pl.multiple_of(c * width + p * 2 * half, 2 * half), 2 * half)

        def one_pair(p, carry):
            cols = shifted(p, 0)
            q2 = qkv_ref[own_rows, cols]
            k2 = qkv_ref[key_rows, shifted(p, 1)]
            v2 = qkv_ref[key_rows, shifted(p, 2)]
            outs = []
            for e in range(2):
                qm = jnp.where(low_lane == (e == 0), q2, jnp.zeros_like(q2))
                raw = dot_nt(qm, k2)
                trow = jnp.broadcast_to(t_ref[2 * p + e], (BLOCK, BLOCK))
                bias = jnp.concatenate(
                    [
                        jnp.take_along_axis(
                            trow, first[:, c : c + BLOCK], axis=1, mode="promise_in_bounds"
                        )
                        + jnp.take_along_axis(
                            trow, second[:, c : c + BLOCK], axis=1, mode="promise_in_bounds"
                        )
                        for c in range(0, span, BLOCK)
                    ],
                    axis=1,
                )
                scores = jnp.where(same, raw * scale + bias, mask_fill)
                top = jnp.max(scores, axis=1, keepdims=True)
                weights = jnp.exp(scores - top)
                probs = weights * (1.0 / jnp.sum(weights, axis=1, keepdims=True))
                p_ref[2 * p + e, 0] = probs
                outs.append(dot(probs.astype(BF16), v2))
            ctx_ref[:, cols] = jnp.where(low_lane, outs[0], outs[1]).astype(BF16)
            return carry

        lax.fori_loop(0, pairs, one_pair, 0, unroll=True)

    return pl.pallas_call(
        body,
        grid_spec=pltpu.PrefetchScalarGridSpec(
            num_scalar_prefetch=1,
            grid=(blocks,),
            in_specs=[
                pl.BlockSpec((rows, 3 * width), lambda i, w: (0, 0)),
                pl.BlockSpec((1, 1, rows), lambda i, w: (w[0], 0, 0)),
                pl.BlockSpec((1, BLOCK, 1), lambda i, w: (w[0], i, 0)),
                pl.BlockSpec((2, 1, BLOCK, rows), lambda i, w: (0, w[0], i, 0)),
                pl.BlockSpec((heads, 1, BLOCK), lambda i, w: (0, 0, 0)),
            ],
            out_specs=[
                pl.BlockSpec((BLOCK, width), lambda i, w: (i, 0)),
                pl.BlockSpec((heads, 1, BLOCK, span), lambda i, w: (0, i, 0, 0)),
            ],
        ),
        out_shape=[
            jax.ShapeDtypeStruct((rows, width), BF16),
            jax.ShapeDtypeStruct((heads, blocks, BLOCK, span), F32),
        ],
        cost_estimate=pl.CostEstimate(flops=ATTEND_FLOPS, transcendentals=0, bytes_accessed=1 << 23),
        name="attend",
    )(which, qkv, doc_row, doc_col, buckets, lookup)


def attend_back(which, qkvs, grads, probs):
    rows, width = qkvs[0].shape[0], qkvs[0].shape[1] // 3
    heads, blocks, _, span = probs[0].shape
    pairs = heads // 2
    half = width // heads
    scale = 1.0 / math.sqrt(half)

    def body(qkv_a, qkv_b, g_a, g_b, p_a, p_b, d_a, d_b, s_a, s_b, acc_a, acc_b):
        block = pl.program_id(0)
        start = pl.multiple_of(jnp.clip(block - 1, 0, blocks - 3) * BLOCK, BLOCK)
        own_rows = pl.ds(pl.multiple_of(block * BLOCK, BLOCK), BLOCK)
        key_rows = pl.ds(start, span)
        low_lane = lax.broadcasted_iota(jnp.int32, (BLOCK, 2 * half), 1) < half

        @pl.when(block == 0)
        def _():
            acc_a[...] = jnp.zeros_like(acc_a)
            acc_b[...] = jnp.zeros_like(acc_b)

        for qkv_ref, g_ref, p_ref, d_ref, s_ref, sums in (
            (qkv_a, g_a, p_a, d_a, s_a, acc_a),
            (qkv_b, g_b, p_b, d_b, s_b, acc_b),
        ):

            def shifted(p, c):
                return pl.ds(pl.multiple_of(c * width + p * 2 * half, 2 * half), 2 * half)

            def one_pair(p, carry):
                cols = shifted(p, 0)
                q2 = qkv_ref[own_rows, cols]
                g2 = g_ref[:, cols]
                k2 = qkv_ref[key_rows, shifted(p, 1)]
                v2 = qkv_ref[key_rows, shifted(p, 2)]
                dqs = []
                dk = sums[0, key_rows, cols]
                dv = sums[1, key_rows, cols]
                for e in range(2):
                    mine = low_lane == (e == 0)
                    qm = jnp.where(mine, q2, jnp.zeros_like(q2))
                    gm = jnp.where(mine, g2, jnp.zeros_like(g2))
                    pr = p_ref[2 * p + e, 0]
                    gp = dot_nt(gm, v2)
                    gs = pr * (gp - jnp.sum(pr * gp, axis=1, keepdims=True))
                    s_ref[2 * p + e, 0] = gs
                    raw = (gs * scale).astype(BF16)
                    dqs.append(dot(raw, k2))
                    dk = dk + dot_tn(raw, qm)
                    dv = dv + dot_tn(pr.astype(BF16), gm)
                d_ref[own_rows, cols] = jnp.where(low_lane, dqs[0], dqs[1]).astype(BF16)
                sums[0, key_rows, cols] = dk
                sums[1, key_rows, cols] = dv
                return carry

            lax.fori_loop(0, pairs, one_pair, 0, unroll=True)

        @pl.when(block == blocks - 1)
        def _():
            for d_ref, sums in ((d_a, acc_a), (d_b, acc_b)):
                d_ref[:, width : 2 * width] = sums[0].astype(BF16)
                d_ref[:, 2 * width :] = sums[1].astype(BF16)

    whole = pl.BlockSpec((rows, 3 * width), lambda i: (0, 0))
    part = pl.BlockSpec((BLOCK, width), lambda i: (i, 0))
    prob = pl.BlockSpec((heads, 1, BLOCK, span), lambda i: (0, i, 0, 0))
    shape = jax.ShapeDtypeStruct((rows, 3 * width), BF16)
    score = jax.ShapeDtypeStruct(probs[0].shape, F32)
    return pl.pallas_call(
        body,
        grid=(blocks,),
        in_specs=[whole, whole, part, part, prob, prob],
        out_specs=[whole, whole, prob, prob],
        scratch_shapes=[
            pltpu.VMEM((2, rows, width), F32),
            pltpu.VMEM((2, rows, width), F32),
        ],
        out_shape=[shape, shape, score, score],
        input_output_aliases={4: 2, 5: 3},
        cost_estimate=pl.CostEstimate(
            flops=BACK_FLOPS, transcendentals=0, bytes_accessed=1 << 24
        ),
        name="attend_back",
    )(*qkvs, *grads, *probs)


def table_sums(which, scores, buckets):
    heads, blocks, _, span = scores[0].shape
    nb = NB
    rows = blocks * BLOCK
    group = 8
    codes = 2 * nb
    lanes = 2 * 2 * heads * group

    def body(which_ref, s_a, s_b, b_ref, tab_ref, acc_ref):
        block = pl.program_id(0)
        start = pl.multiple_of(jnp.clip(block - 1, 0, blocks - 3) * BLOCK, BLOCK)
        key_rows = pl.ds(start, span)

        @pl.when(block == 0)
        def _():
            acc_ref[...] = jnp.zeros_like(acc_ref)

        code_ids = lax.broadcasted_iota(jnp.int32, (nb, span), 0)

        def one_group(g, carry):
            r8 = pl.ds(pl.multiple_of(g * group, group), group)
            b0 = b_ref[0, 0, r8, key_rows]
            b1 = b_ref[1, 0, r8, key_rows]
            pieces = []
            for r in range(group):
                for b in (b0, b1):
                    row = jnp.broadcast_to(b[r : r + 1], (nb, span))
                    pieces.append(jnp.where(row == code_ids, 1.0, 0.0).astype(BF16))
            onehot = jnp.concatenate(pieces, axis=0)
            gg = jnp.concatenate(
                [ref[:, 0, r8, :].reshape(heads * group, span) for ref in (s_a, s_b)], axis=0
            )
            upper = gg.astype(BF16)
            lower = (gg - upper.astype(F32)).astype(BF16)
            both = jnp.concatenate([upper, lower], axis=0)
            acc_ref[...] += dot_nt(onehot, both)
            return carry

        lax.fori_loop(0, BLOCK // group, one_group, 0)

        @pl.when(block == blocks - 1)
        def _():
            lane_row = lax.broadcasted_iota(jnp.int32, (codes, lanes), 1) % group
            total = jnp.zeros((codes, lanes), F32)
            for r in range(group):
                total = total + jnp.where(
                    lane_row == r, acc_ref[r * codes : (r + 1) * codes, :], 0.0
                )
            tab_ref[...] = total

    prob = pl.BlockSpec((heads, 1, BLOCK, span), lambda i, w: (0, i, 0, 0))
    return pl.pallas_call(
        body,
        grid_spec=pltpu.PrefetchScalarGridSpec(
            num_scalar_prefetch=1,
            grid=(blocks,),
            in_specs=[
                prob,
                prob,
                pl.BlockSpec((2, 1, BLOCK, rows), lambda i, w: (0, w[0], i, 0)),
            ],
            out_specs=pl.BlockSpec((codes, lanes), lambda i, w: (0, 0)),
            scratch_shapes=[pltpu.VMEM((group * codes, lanes), F32)],
        ),
        out_shape=jax.ShapeDtypeStruct((codes, lanes), F32),
        cost_estimate=NO_COST,
        name="table_sums",
    )(which, *scores, buckets)


def split_tables(tables, nb):
    heads = tables.shape[1] // 32
    total = tables.reshape(2, nb, 2, 2, heads, 8).sum(axis=(2, 5))
    return total[:, :, 0], total[:, :, 1]


def input_back(grads_a, grads_b, weight_a, weight_b, grad_sum, features, inputs):
    width = weight_a.shape[2]

    def body(g_a, g_b, w_a, w_b, sum_ref, f_ref, x_ref, in_ref, lay_ref, prod_ref, col_ref):
        total = sum_ref[...]
        for g_ref, w_ref in ((g_a, w_a), (g_b, w_b)):
            for c in range(3):
                total = total + dot_nt(g_ref[:, c * width : (c + 1) * width], w_ref[c])
        in_ref[...] = total
        lay_ref[...] = dot(f_ref[...], total.astype(BF16))
        prod_ref[...] = dot_tn(x_ref[...], g_a[...])
        col_ref[...] = jnp.sum(g_a[...].astype(F32), axis=0, keepdims=True)

    model = inputs.shape[1]
    return pl.pallas_call(
        body,
        out_shape=[
            jax.ShapeDtypeStruct(grad_sum.shape, F32),
            jax.ShapeDtypeStruct((features.shape[0], model), F32),
            jax.ShapeDtypeStruct((model, 3 * width), F32),
            jax.ShapeDtypeStruct((1, 3 * width), F32),
        ],
        cost_estimate=NO_COST,
        name="input_back",
    )(grads_a, grads_b, weight_a, weight_b, grad_sum, features, inputs)


def pair_back(inputs, grads, product, columns):
    model = inputs.shape[1]
    wide = grads.shape[1]

    def body(x_ref, g_ref, prod_ref, col_ref, a_ref, b_ref, sum_ref):
        total = (prod_ref[...] + dot_tn(x_ref[...], g_ref[...])).astype(BF16)
        a_ref[...] = total[: model // 2]
        b_ref[...] = total[model // 2 :]
        sum_ref[...] = col_ref[...] + jnp.sum(g_ref[...].astype(F32), axis=0, keepdims=True)

    half = jax.ShapeDtypeStruct((model // 2, wide), BF16)
    return pl.pallas_call(
        body,
        out_shape=[half, half, jax.ShapeDtypeStruct((1, wide), F32)],
        cost_estimate=NO_COST,
        name="pair_back",
    )(inputs, grads, product, columns)


def swap(value):
    size = lax.axis_size("tensor")
    return lax.ppermute(value, "tensor", [(i, (i + 1) % size) for i in range(size)])


def ring_bits(turned):
    size = lax.axis_size("dp")
    bits = [1 << k for k in range(size.bit_length() - 1)]
    return bits[1::-1] + bits[2:] if turned else bits


def ring_steps(bits):
    return [(True, bit) for bit in bits] + [(False, bit) for bit in reversed(bits)]


def side_of(bit):
    return (lax.axis_index("dp") >> (bit.bit_length() - 1)) & 1


def begin(step, value):
    scatter, bit = step
    if not scatter:
        return value, value
    side = side_of(bit)
    half = value.shape[0] // 2
    part = lambda where: lax.dynamic_slice_in_dim(
        value, where * half, half, 0, allow_negative_indices=False
    )
    return part(side), part(1 - side)


def finish(step, kept, send):
    scatter, bit = step
    size = lax.axis_size("dp")
    received = lax.ppermute(send, "dp", [(i, i ^ bit) for i in range(size)])
    if scatter:
        return kept + received
    low = side_of(bit) == 0
    return jnp.concatenate([jnp.where(low, kept, received), jnp.where(low, received, kept)])


def ring_run(steps, value):
    for step in steps:
        value = finish(step, *begin(step, value))
    return value


def update(clip_factor, grads, state):
    share = state[0].shape[1] // BLOCK
    start = lax.axis_index("dp").astype(jnp.int32) * share
    wide, wide_info, thin, thin_info = [], [], [], []
    base = 0
    row = 0
    for grad in grads:
        rows = grad.size // BLOCK
        if grad.ndim == 2 and grad.shape[1] % BLOCK == 0 and grad.shape[0] > 16:
            lanes = grad.shape[1] // BLOCK
            grad = jnp.pad(grad, ((0, -grad.shape[0] % 8), (0, 0)))
            slab = min(grad.shape[0], -(-(share // lanes + 18) // 8) * 8)
            wide.append(grad)
            wide_info.append((base, lanes, grad.shape[0], slab))
        else:
            thin.append(jnp.pad(grad.reshape(rows, BLOCK), ((0, -rows % 8), (0, 0))))
            thin_info.append((base, row, rows))
            row += rows + -rows % 8
        base += rows
    thin_all = jnp.concatenate(thin)
    margin = -(-max(info[1] * info[3] for info in wide_info) // 8) * 8 + 8

    def slab_start(first, info):
        base, lanes, rows, slab = info
        wanted = jnp.maximum(first - base, 0) // (lanes * 8) * 8
        return pl.multiple_of(jnp.minimum(wanted, rows - slab), 8)

    def body(start_ref, clip_ref, *refs):
        wide_refs = refs[: len(wide)]
        thin_ref = refs[len(wide)]
        master, one, two, ema = refs[len(wide) + 1 : len(wide) + 5]
        new_master, new_one, new_two, new_ema, copy, own = refs[len(wide) + 5 :]
        first = start_ref[0]
        own[margin : margin + share, :] = jnp.zeros((share, BLOCK), F32)
        for ref, info in zip(wide_refs, wide_info):
            base, lanes, rows, slab = info

            @pl.when((first < base + rows * lanes) & (first + share > base))
            def _():
                place = margin + base + slab_start(first, info) * lanes - first
                for k in range(lanes):
                    own[pl.ds(place + k, slab, stride=lanes), :] = ref[
                        :, k * BLOCK : (k + 1) * BLOCK
                    ]

        for base, row, rows in thin_info:

            @pl.when((first < base + rows) & (first + share > base))
            def _():
                own[pl.ds(margin + base - first, rows), :] = thin_ref[row : row + rows, :]

        scale = clip_ref[0]

        def advance(row, rows):
            many = -(-rows // 8) * 8
            grad = own[pl.ds(pl.multiple_of(margin + row, 8), many), :].reshape(1, many * BLOCK)
            grad = grad[:, : rows * BLOCK] * scale
            place = (slice(None), pl.ds(pl.multiple_of(row * BLOCK, 8 * BLOCK), rows * BLOCK))
            moment = beta_one * one[place] + (1.0 - beta_one) * grad
            second = beta_two * two[place] + (1.0 - beta_two) * grad * grad
            new_one[place] = moment
            new_two[place] = second
            step_size = (
                moment
                / (1.0 - beta_one**STEP)
                / (jnp.sqrt(second / (1.0 - beta_two**STEP)) + adam_eps)
            )
            weight = master[place]
            weight = weight - learn_rate * (step_size + decay_rate * weight)
            new_master[place] = weight
            new_ema[place] = average_rate * ema[place] + (1.0 - average_rate) * weight
            copy[place] = weight.astype(BF16)

        def many_rows(number, carry):
            advance(number * CHUNK, CHUNK)
            return carry

        lax.fori_loop(0, share // CHUNK, many_rows, 0)
        if share % CHUNK:
            advance(share // CHUNK * CHUNK, share % CHUNK)

    plain = pl.BlockSpec((1, share * BLOCK), lambda i, s: (0, 0))
    specs = [pl.BlockSpec(memory_space=pltpu.SMEM)]
    for grad, info in zip(wide, wide_info):
        specs.append(
            pl.BlockSpec(
                (pl.Element(info[3]), pl.Element(grad.shape[1])),
                lambda i, s, info=info: (slab_start(s[0], info), 0),
            )
        )
    specs.append(pl.BlockSpec(thin_all.shape, lambda i, s: (0, 0)))
    flat = jax.ShapeDtypeStruct((1, share * BLOCK), F32)
    return pl.pallas_call(
        body,
        grid_spec=pltpu.PrefetchScalarGridSpec(
            num_scalar_prefetch=1,
            grid=(1,),
            in_specs=specs + [plain] * 4,
            out_specs=[plain] * 5,
            scratch_shapes=[pltpu.VMEM((2 * margin + share + 8, BLOCK), F32)],
        ),
        out_shape=[flat] * 4 + [jax.ShapeDtypeStruct((1, share * BLOCK), BF16)],
        name="update",
    )(
        start.reshape(1),
        clip_factor.reshape(1),
        *wide,
        thin_all,
        *state,
    )


def per_device(
    hidden_in,
    cotangent,
    box_coords,
    doc_ids,
    buckets,
    layout_weight,
    norm_gains,
    norm_shifts,
    branch_biases,
    qkv_weight,
    query_value_bias,
    output_weight,
    ffn_in_weight,
    ffn_in_bias,
    ffn_out_weight,
    relative_table,
    master_flat,
    moment_one,
    moment_two,
    ema_flat,
):
    turn = lax.axis_index("tensor")
    window = turn.astype(jnp.int32).reshape(1)
    gains = norm_gains.astype(F32)
    norm_offsets = norm_shifts.astype(F32)
    biases = branch_biases.astype(F32)

    small_own = jnp.concatenate(
        [query_value_bias.reshape(-1), ffn_in_bias, relative_table.reshape(-1)]
    )
    qkv_other = swap(qkv_weight)
    small_other = swap(small_own)
    output_other = swap(output_weight)
    ffn_in_other = swap(ffn_in_weight)
    ffn_out_other = swap(ffn_out_weight)
    cuts = (query_value_bias.size, query_value_bias.size + ffn_in_bias.size)
    qv_bias_other = small_other[: cuts[0]].reshape(query_value_bias.shape)
    ffn_bias_other = small_other[cuts[0] : cuts[1]]
    table_other = small_other[cuts[1] :].reshape(relative_table.shape)

    features = box_features(box_coords).astype(BF16)
    embedded = hidden_in.astype(F32) + dot_tn(features, layout_weight)
    inputs = embedded.astype(BF16)
    inputs_swap = swap(inputs)

    def project(weight, bias):
        shift = jnp.stack([bias[0], jnp.zeros_like(bias[0]), bias[1]]).astype(F32)
        return jnp.concatenate(
            [(dot(inputs, weight[c]) + shift[c]).astype(BF16) for c in range(3)], axis=1
        )

    qkv_a = project(qkv_weight, query_value_bias)
    context_a, probs_a = attend(window, qkv_a, doc_ids, buckets, relative_table)
    qkv_b = project(qkv_other, qv_bias_other)
    context_b, probs_b = attend(window, qkv_b, doc_ids, buckets, table_other)
    context_swap = swap(context_b)
    attn_out = dot(context_a, output_weight) + dot(context_b, output_other) + biases[0]
    normed_one, inv_std_one = normalize(embedded + attn_out)
    mid_norm = normed_one * gains[0] + norm_offsets[0]
    mid_low = mid_norm.astype(BF16)
    mid_swap = swap(mid_low)

    def expand(weight, bias):
        pre = dot(mid_low, weight) + bias.astype(F32)
        share = 0.5 + 0.5 * lax.erf(pre * math.sqrt(0.5))
        slope = share + pre * (math.sqrt(0.5 / math.pi) * jnp.exp(-0.5 * pre * pre))
        return (pre * share).astype(BF16), slope

    hidden_a, slope_a = expand(ffn_in_weight, ffn_in_bias)
    hidden_b, slope_b = expand(ffn_in_other, ffn_bias_other)
    hidden_swap = swap(hidden_b)
    branch = dot(hidden_a, ffn_out_weight) + dot(hidden_b, ffn_out_other) + biases[1]
    normed_two, inv_std_two = normalize(mid_norm + branch)
    hidden_out = (normed_two * gains[1] + norm_offsets[1]).astype(BF16)
    grad_out = cotangent.astype(F32)
    gain_two = jnp.sum(grad_out * normed_two, axis=0)
    shift_two = jnp.sum(grad_out, axis=0)
    grad_sum_two = norm_back(grad_out, normed_two, inv_std_two, gains[1])
    bias_two = jnp.sum(grad_sum_two, axis=0)
    grad_branch = grad_sum_two.astype(BF16)
    grad_branch_swap = swap(grad_branch)

    grad_pre_b = (slope_b * dot_nt(grad_branch, ffn_out_other)).astype(BF16)
    grad_pre_swap = swap(grad_pre_b)
    grad_pre_a = (slope_a * dot_nt(grad_branch, ffn_out_weight)).astype(BF16)
    ffn_out_low = (
        dot_tn(hidden_a, grad_branch) + dot_tn(hidden_swap, grad_branch_swap)
    ).astype(BF16)
    ffn_in_low = (dot_tn(mid_low, grad_pre_a) + dot_tn(mid_swap, grad_pre_swap)).astype(BF16)
    grad_mid = (
        grad_sum_two + dot_nt(grad_pre_a, ffn_in_weight) + dot_nt(grad_pre_b, ffn_in_other)
    )
    gain_one = jnp.sum(grad_mid * normed_one, axis=0)
    shift_one = jnp.sum(grad_mid, axis=0)
    grad_sum_one = norm_back(grad_mid, normed_one, inv_std_one, gains[0])
    bias_one = jnp.sum(grad_sum_one, axis=0)
    grad_attn = grad_sum_one.astype(BF16)
    grad_attn_swap = swap(grad_attn)
    output_grad = dot_tn(context_a, grad_attn) + dot_tn(context_swap, grad_attn_swap)
    grad_context_a = dot_nt(grad_attn, output_weight).astype(BF16)
    grad_context_b = dot_nt(grad_attn, output_other).astype(BF16)

    barrier = lax.optimization_barrier
    steps_a, steps_b = ring_steps(ring_bits(False)), ring_steps(ring_bits(True))
    out_keep, out_send = begin(
        steps_a[0], jnp.concatenate([ffn_out_low, output_grad.astype(BF16)])
    )
    in_keep, in_send = begin(steps_b[0], ffn_in_low)
    (grad_context_a, grad_context_b), out_send, in_send = barrier(
        ((grad_context_a, grad_context_b), out_send, in_send)
    )
    out_sum = finish(steps_a[0], out_keep, out_send)
    in_sum = finish(steps_b[0], in_keep, in_send)
    grads_a, grads_b, scores_a, scores_b = attend_back(
        window, (qkv_a, qkv_b), (grad_context_a, grad_context_b), (probs_a, probs_b)
    )
    grads_swap = swap(grads_b)

    out_keep, out_send = begin(steps_a[1], out_sum)
    in_keep, in_send = begin(steps_b[1], in_sum)
    grads_a, grads_b, out_send, in_send = barrier((grads_a, grads_b, out_send, in_send))
    out_sum = finish(steps_a[1], out_keep, out_send)
    in_sum = finish(steps_b[1], in_keep, in_send)
    width = qkv_weight.shape[2]
    input_grad, layout_part, product, columns = input_back(
        grads_a, grads_b, qkv_weight, qkv_other, grad_sum_one, features, inputs
    )
    pack_a, pack_b, qv_sums = pair_back(inputs_swap, grads_swap, product, columns)

    plans = {
        "out": (0, steps_a[2:]),
        "in": (0, steps_b[2:]),
        "a": (0, steps_a),
        "b": (0, steps_b),
        "c": (2, steps_b),
    }
    sums = {"out": out_sum, "in": in_sum, "a": pack_a, "b": pack_b}
    last = len(steps_a) - 1
    for number in range(last + 3):
        if number == 2:
            qv_bias_grad = jnp.stack([qv_sums[0, :width], qv_sums[0, 2 * width :]])
            ffn_bias_grad = jnp.sum(grad_pre_a.astype(F32), axis=0) + jnp.sum(
                grad_pre_swap.astype(F32), axis=0
            )
            table_a, table_b = split_tables(tables, NB)
            table_grad = table_a + swap(table_b)
            shared = jnp.concatenate(
                [
                    layout_part,
                    jnp.stack([gain_one, gain_two, shift_one, shift_two, bias_one, bias_two]),
                ]
            )
            cut = shared.shape[0] // lax.axis_size("tensor")
            first_turn = turn == 0
            own_shared = jnp.where(first_turn, shared[:cut], shared[cut:])
            own_shared = own_shared + swap(
                jnp.where(first_turn, shared[cut:], shared[:cut]).astype(BF16)
            ).astype(F32)
            model = layout_part.shape[1]
            small = jnp.concatenate(
                [ffn_bias_grad, qv_bias_grad.reshape(-1), table_grad.reshape(-1)]
            ).astype(BF16)
            small = jnp.pad(small, (0, -small.size % (16 * model))).reshape(-1, model)
            own_rows = own_shared.shape[0] + -own_shared.shape[0] % 16
            unit = 8 * lax.axis_size("dp")
            fill = -(own_rows + small.shape[0]) % unit
            pack_c = jnp.concatenate(
                [
                    jnp.pad(own_shared.astype(BF16), ((0, own_rows - own_shared.shape[0]), (0, 0))),
                    jnp.pad(small, ((0, fill), (0, 0))),
                ]
            )
            sums["c"] = pack_c
        opened = {
            name: begin(steps[number - first], sums[name])
            for name, (first, steps) in plans.items()
            if first <= number < first + len(steps)
        }
        sends = {name: send for name, (_, send) in opened.items()}
        if number == 0:
            sends, scores_a, scores_b = barrier((sends, scores_a, scores_b))
            tables = table_sums(window, (scores_a, scores_b), buckets)
            kepts, tables = barrier(({name: kept for name, (kept, _) in opened.items()}, tables))
            opened = {name: (kept, None) for name, kept in kepts.items()}
        elif number == 1:
            sends, tables, layout_part, qv_sums, grad_pre_a, grad_pre_swap = barrier(
                (sends, tables, layout_part, qv_sums, grad_pre_a, grad_pre_swap)
            )
        elif number == last - 1:
            sends, sums["out"], sums["in"] = barrier((sends, sums["out"], sums["in"]))
        elif number == last + 2:
            sends, sums["a"], sums["b"] = barrier((sends, sums["a"], sums["b"]))
        else:
            sends = barrier(sends)
        for name, (kept, _) in opened.items():
            first, steps = plans[name]
            sums[name] = finish(steps[number - first], kept, sends[name])
    out_all, ffn_in_low, pack_a, pack_b, pack_c = (sums[name] for name in "out in a b c".split())

    square = sum(
        jnp.sum(jnp.square(member.astype(F32)))
        for member in (out_all, ffn_in_low, pack_a, pack_b, pack_c)
    )
    ffn_out_grad = out_all[: ffn_out_low.shape[0]].astype(F32)
    output_grad = out_all[ffn_out_low.shape[0] :].astype(F32)
    ffn_in_grad = ffn_in_low.astype(F32)
    qkv_grad = jnp.stack(
        [
            jnp.concatenate([part[:, c * width : (c + 1) * width] for part in (pack_a, pack_b)])
            for c in range(3)
        ]
    ).astype(F32)
    own_low = pack_c[:cut]
    few = -(-(ffn_bias_grad.size + qv_bias_grad.size + table_grad.size) // model)
    small = pack_c[own_rows : own_rows + few].astype(F32).reshape(-1)
    place = 0
    smalls = []
    for member in (ffn_bias_grad, qv_bias_grad, table_grad):
        smalls.append(small[place : place + member.size].reshape(member.shape))
        place += member.size
    ffn_bias_grad, qv_bias_grad, table_grad = smalls
    other_low = swap(own_low)
    shared = jnp.where(
        first_turn,
        jnp.concatenate([own_low, other_low]),
        jnp.concatenate([other_low, own_low]),
    ).astype(F32)
    layout_grad = shared[: layout_part.shape[0]]
    gains_grad, shifts_grad, biases_grad = jnp.split(shared[layout_part.shape[0] :], 3)

    grad_norm = jnp.sqrt(square + swap(square))
    clip_factor = clip_limit / jnp.maximum(grad_norm, clip_limit)
    updated = update(
        clip_factor,
        (
            ffn_in_grad,
            ffn_bias_grad,
            ffn_out_grad,
            qkv_grad.reshape(-1, width),
            qv_bias_grad,
            output_grad,
            table_grad,
            own_low.astype(F32),
        ),
        (master_flat, moment_one, moment_two, ema_flat),
    )
    return (
        hidden_out,
        input_grad,
        layout_grad,
        gains_grad,
        shifts_grad,
        biases_grad,
        qkv_grad,
        qv_bias_grad,
        output_grad,
        ffn_in_grad,
        ffn_bias_grad,
        ffn_out_grad,
        table_grad,
        grad_norm,
    ) + tuple(updated)


def solution(mesh):
    return jax.shard_map(
        per_device,
        mesh=mesh,
        in_specs=(
            P(("dp", "tensor"), None),
            P(("dp", "tensor"), None),
            P(None, ("dp", "tensor")),
            P("dp", None),
            P(None, "dp", None, None),
            P(),
            P(),
            P(),
            P(),
            P(None, None, "tensor"),
            P(None, "tensor"),
            P("tensor", None),
            P(None, "tensor"),
            P("tensor"),
            P("tensor", None),
            P(None, None, "tensor"),
            P("tensor", "dp"),
            P("tensor", "dp"),
            P("tensor", "dp"),
            P("tensor", "dp"),
        ),
        out_specs=(
            P(("dp", "tensor"), None),
            P(("dp", "tensor"), None),
            P(),
            P(),
            P(),
            P(),
            P(None, None, "tensor"),
            P(None, "tensor"),
            P("tensor", None),
            P(None, "tensor"),
            P("tensor"),
            P("tensor", None),
            P(None, None, "tensor"),
            P(),
            P("tensor", "dp"),
            P("tensor", "dp"),
            P("tensor", "dp"),
            P("tensor", "dp"),
            P("tensor", "dp"),
        ),
        check_vma=False,
    )
```

```python
import math

import jax
import jax.numpy as jnp
from jax import lax
from jax.experimental import pallas as pl
from jax.experimental.pallas import tpu as pltpu
from jax.sharding import PartitionSpec as P

NB = 32
FEAT = 256
STEP = 10
BLOCK = 128
CHUNK = 32
ATTEND_FLOPS = 1 << 33
BACK_FLOPS = 1 << 35
NO_COST = pl.CostEstimate(flops=1, transcendentals=0, bytes_accessed=1)


norm_eps = 1e-05
learn_rate = 0.02
beta_one = 0.9
beta_two = 0.999
adam_eps = 1e-08
decay_rate = 0.01
average_rate = 0.5
clip_limit = 1.0
mask_fill = -1e30

F32 = jnp.float32
BF16 = jnp.bfloat16
NT = (((1,), (1,)), ((), ()))
TN = (((0,), (0,)), ((), ()))


def dot(left, right):
    return jnp.dot(left, right, preferred_element_type=F32)


def dot_nt(left, right):
    return lax.dot_general(left, right, NT, preferred_element_type=F32)


def dot_tn(left, right):
    return lax.dot_general(left, right, TN, preferred_element_type=F32)


def box_features(coords):
    count = FEAT // 8
    freqs = jnp.exp(-math.log(10000.0) * jnp.arange(count, dtype=F32) / count)
    angles = coords.astype(F32)[:, None, :] * freqs[None, :, None]
    waves = jnp.stack([jnp.sin(angles), jnp.cos(angles)], axis=1)
    return waves.reshape(FEAT, coords.shape[1])


def normalize(value):
    centre = value - jnp.mean(value, axis=-1, keepdims=True)
    inv_std = lax.rsqrt(jnp.mean(centre * centre, axis=-1, keepdims=True) + norm_eps)
    return (centre * inv_std, inv_std)


def norm_back(grad_out, normed, inv_std, gain):
    scaled = grad_out * gain
    return inv_std * (
        scaled
        - jnp.mean(scaled, axis=-1, keepdims=True)
        - normed * jnp.mean(scaled * normed, axis=-1, keepdims=True)
    )


def attend(which, inputs, weight, bias, docs, buckets, table):
    rows, model = inputs.shape
    width = weight.shape[2]
    nb, heads = table.shape[1:]
    pairs = heads // 2
    half = width // heads
    span = 3 * BLOCK
    blocks = rows // BLOCK
    scale = 1.0 / math.sqrt(half)
    lookup = jnp.pad(
        jnp.concatenate([table[0], table[1]], axis=0).astype(F32).T,
        ((0, 0), (0, BLOCK - 2 * nb)),
    ).reshape(heads, 1, BLOCK)
    doc_row = docs[:, None, :]
    doc_col = docs[:, :, None]

    def body(
        which_ref, x_ref, w_ref, bias_ref, dr_ref, dc_ref, b_ref, t_ref, qkv_ref, ctx_ref, p_ref
    ):
        block = pl.program_id(0)

        @pl.when(block == 0)
        def _():
            for c in range(3):
                made = dot(x_ref[...], w_ref[c])
                if c != 1:
                    made = made + bias_ref[c // 2 : c // 2 + 1, :].astype(F32)
                qkv_ref[:, c * width : (c + 1) * width] = made.astype(BF16)

        start = pl.multiple_of(jnp.clip(block - 1, 0, blocks - 3) * BLOCK, BLOCK)
        own_rows = pl.ds(pl.multiple_of(block * BLOCK, BLOCK), BLOCK)
        key_rows = pl.ds(start, span)
        same = dc_ref[0] == dr_ref[0, :, key_rows]
        first = b_ref[0, 0, :, key_rows]
        second = b_ref[1, 0, :, key_rows] + nb
        low_lane = lax.broadcasted_iota(jnp.int32, (BLOCK, 2 * half), 1) < half

        def shifted(p, c):
            return pl.ds(pl.multiple_of(c * width + p * 2 * half, 2 * half), 2 * half)

        def one_pair(p, carry):
            cols = shifted(p, 0)
            q2 = qkv_ref[own_rows, cols]
            k2 = qkv_ref[key_rows, shifted(p, 1)]
            v2 = qkv_ref[key_rows, shifted(p, 2)]
            outs = []
            for e in range(2):
                qm = jnp.where(low_lane == (e == 0), q2, jnp.zeros_like(q2))
                raw = dot_nt(qm, k2)
                trow = jnp.broadcast_to(t_ref[2 * p + e], (BLOCK, BLOCK))
                bias = jnp.concatenate(
                    [
                        jnp.take_along_axis(
                            trow, first[:, c : c + BLOCK], axis=1, mode="promise_in_bounds"
                        )
                        + jnp.take_along_axis(
                            trow, second[:, c : c + BLOCK], axis=1, mode="promise_in_bounds"
                        )
                        for c in range(0, span, BLOCK)
                    ],
                    axis=1,
                )
                scores = jnp.where(same, raw * scale + bias, mask_fill)
                top = jnp.max(scores, axis=1, keepdims=True)
                weights = jnp.exp(scores - top)
                probs = weights * (1.0 / jnp.sum(weights, axis=1, keepdims=True))
                p_ref[2 * p + e, 0] = probs
                outs.append(dot(probs.astype(BF16), v2))
            ctx_ref[:, cols] = jnp.where(low_lane, outs[0], outs[1]).astype(BF16)
            return carry

        lax.fori_loop(0, pairs, one_pair, 0, unroll=True)

    return pl.pallas_call(
        body,
        grid_spec=pltpu.PrefetchScalarGridSpec(
            num_scalar_prefetch=1,
            grid=(blocks,),
            in_specs=[
                pl.BlockSpec((rows, model), lambda i, w: (0, 0)),
                pl.BlockSpec((3, model, width), lambda i, w: (0, 0, 0)),
                pl.BlockSpec((2, width), lambda i, w: (0, 0)),
                pl.BlockSpec((1, 1, rows), lambda i, w: (w[0], 0, 0)),
                pl.BlockSpec((1, BLOCK, 1), lambda i, w: (w[0], i, 0)),
                pl.BlockSpec((2, 1, BLOCK, rows), lambda i, w: (0, w[0], i, 0)),
                pl.BlockSpec((heads, 1, BLOCK), lambda i, w: (0, 0, 0)),
            ],
            out_specs=[
                pl.BlockSpec((rows, 3 * width), lambda i, w: (0, 0)),
                pl.BlockSpec((BLOCK, width), lambda i, w: (i, 0)),
                pl.BlockSpec((heads, 1, BLOCK, span), lambda i, w: (0, i, 0, 0)),
            ],
        ),
        out_shape=[
            jax.ShapeDtypeStruct((rows, 3 * width), BF16),
            jax.ShapeDtypeStruct((rows, width), BF16),
            jax.ShapeDtypeStruct((heads, blocks, BLOCK, span), F32),
        ],
        cost_estimate=pl.CostEstimate(flops=ATTEND_FLOPS, transcendentals=0, bytes_accessed=1 << 23),
        name="attend",
    )(which, inputs, weight, bias, doc_row, doc_col, buckets, lookup)


def attend_back(which, qkvs, grads, probs):
    rows, width = qkvs[0].shape[0], qkvs[0].shape[1] // 3
    heads, blocks, _, span = probs[0].shape
    pairs = heads // 2
    half = width // heads
    scale = 1.0 / math.sqrt(half)

    def body(qkv_a, qkv_b, g_a, g_b, p_a, p_b, d_a, d_b, s_a, s_b, acc_a, acc_b):
        block = pl.program_id(0)
        start = pl.multiple_of(jnp.clip(block - 1, 0, blocks - 3) * BLOCK, BLOCK)
        own_rows = pl.ds(pl.multiple_of(block * BLOCK, BLOCK), BLOCK)
        key_rows = pl.ds(start, span)
        low_lane = lax.broadcasted_iota(jnp.int32, (BLOCK, 2 * half), 1) < half

        @pl.when(block == 0)
        def _():
            acc_a[...] = jnp.zeros_like(acc_a)
            acc_b[...] = jnp.zeros_like(acc_b)

        for qkv_ref, g_ref, p_ref, d_ref, s_ref, sums in (
            (qkv_a, g_a, p_a, d_a, s_a, acc_a),
            (qkv_b, g_b, p_b, d_b, s_b, acc_b),
        ):

            def shifted(p, c):
                return pl.ds(pl.multiple_of(c * width + p * 2 * half, 2 * half), 2 * half)

            def one_pair(p, carry):
                cols = shifted(p, 0)
                q2 = qkv_ref[own_rows, cols]
                g2 = g_ref[:, cols]
                k2 = qkv_ref[key_rows, shifted(p, 1)]
                v2 = qkv_ref[key_rows, shifted(p, 2)]
                dqs = []
                dk = sums[0, key_rows, cols]
                dv = sums[1, key_rows, cols]
                for e in range(2):
                    mine = low_lane == (e == 0)
                    qm = jnp.where(mine, q2, jnp.zeros_like(q2))
                    gm = jnp.where(mine, g2, jnp.zeros_like(g2))
                    pr = p_ref[2 * p + e, 0]
                    gp = dot_nt(gm, v2)
                    gs = pr * (gp - jnp.sum(pr * gp, axis=1, keepdims=True))
                    s_ref[2 * p + e, 0] = gs
                    raw = (gs * scale).astype(BF16)
                    dqs.append(dot(raw, k2))
                    dk = dk + dot_tn(raw, qm)
                    dv = dv + dot_tn(pr.astype(BF16), gm)
                d_ref[own_rows, cols] = jnp.where(low_lane, dqs[0], dqs[1]).astype(BF16)
                sums[0, key_rows, cols] = dk
                sums[1, key_rows, cols] = dv
                return carry

            lax.fori_loop(0, pairs, one_pair, 0, unroll=True)

        @pl.when(block == blocks - 1)
        def _():
            for d_ref, sums in ((d_a, acc_a), (d_b, acc_b)):
                d_ref[:, width : 2 * width] = sums[0].astype(BF16)
                d_ref[:, 2 * width :] = sums[1].astype(BF16)

    whole = pl.BlockSpec((rows, 3 * width), lambda i: (0, 0))
    part = pl.BlockSpec((BLOCK, width), lambda i: (i, 0))
    prob = pl.BlockSpec((heads, 1, BLOCK, span), lambda i: (0, i, 0, 0))
    shape = jax.ShapeDtypeStruct((rows, 3 * width), BF16)
    score = jax.ShapeDtypeStruct(probs[0].shape, F32)
    return pl.pallas_call(
        body,
        grid=(blocks,),
        in_specs=[whole, whole, part, part, prob, prob],
        out_specs=[whole, whole, prob, prob],
        scratch_shapes=[
            pltpu.VMEM((2, rows, width), F32),
            pltpu.VMEM((2, rows, width), F32),
        ],
        out_shape=[shape, shape, score, score],
        input_output_aliases={4: 2, 5: 3},
        cost_estimate=pl.CostEstimate(
            flops=BACK_FLOPS, transcendentals=0, bytes_accessed=1 << 24
        ),
        name="attend_back",
    )(*qkvs, *grads, *probs)


def table_sums(which, scores, buckets):
    heads, blocks, _, span = scores[0].shape
    nb = NB
    rows = blocks * BLOCK
    group = 8
    codes = 2 * nb
    lanes = 2 * 2 * heads * group

    def body(which_ref, s_a, s_b, b_ref, tab_ref, acc_ref):
        block = pl.program_id(0)
        start = pl.multiple_of(jnp.clip(block - 1, 0, blocks - 3) * BLOCK, BLOCK)
        key_rows = pl.ds(start, span)

        @pl.when(block == 0)
        def _():
            acc_ref[...] = jnp.zeros_like(acc_ref)

        code_ids = lax.broadcasted_iota(jnp.int32, (nb, span), 0).astype(F32).astype(BF16)
        one, zero = jnp.ones((), BF16), jnp.zeros((), BF16)

        def one_side(r8):
            b0 = b_ref[0, 0, r8, key_rows].astype(F32)
            b1 = b_ref[1, 0, r8, key_rows].astype(F32)
            pieces = []
            for r in range(group):
                for b in (b0, b1):
                    row = jnp.broadcast_to(b[r : r + 1], (nb, span)).astype(BF16)
                    pieces.append(jnp.where(row == code_ids, one, zero))
            gg = jnp.concatenate(
                [ref[:, 0, r8, :].reshape(heads * group, span) for ref in (s_a, s_b)], axis=0
            )
            upper = gg.astype(BF16)
            lower = (gg - upper.astype(F32)).astype(BF16)
            return jnp.concatenate(pieces, axis=0), jnp.concatenate([upper, lower], axis=0)

        def two_groups(g, carry):
            sides = [
                one_side(pl.ds(pl.multiple_of((2 * g + k) * group, group), group))
                for k in range(2)
            ]
            onehot, both = (jnp.concatenate(parts, axis=1) for parts in zip(*sides))
            acc_ref[...] += dot_nt(onehot, both)
            return carry

        lax.fori_loop(0, BLOCK // group // 2, two_groups, 0)

        @pl.when(block == blocks - 1)
        def _():
            lane_row = lax.broadcasted_iota(jnp.int32, (codes, lanes), 1) % group
            total = jnp.zeros((codes, lanes), F32)
            for r in range(group):
                total = total + jnp.where(
                    lane_row == r, acc_ref[r * codes : (r + 1) * codes, :], 0.0
                )
            tab_ref[...] = total

    prob = pl.BlockSpec((heads, 1, BLOCK, span), lambda i, w: (0, i, 0, 0))
    return pl.pallas_call(
        body,
        grid_spec=pltpu.PrefetchScalarGridSpec(
            num_scalar_prefetch=1,
            grid=(blocks,),
            in_specs=[
                prob,
                prob,
                pl.BlockSpec((2, 1, BLOCK, rows), lambda i, w: (0, w[0], i, 0)),
            ],
            out_specs=pl.BlockSpec((codes, lanes), lambda i, w: (0, 0)),
            scratch_shapes=[pltpu.VMEM((group * codes, lanes), F32)],
        ),
        out_shape=jax.ShapeDtypeStruct((codes, lanes), F32),
        cost_estimate=NO_COST,
        name="table_sums",
    )(which, *scores, buckets)


def split_tables(tables, nb):
    heads = tables.shape[1] // 32
    total = tables.reshape(2, nb, 2, 2, heads, 8).sum(axis=(2, 5))
    return total[:, :, 0], total[:, :, 1]


def input_back(grads_a, grads_b, weight_a, weight_b, grad_sum, features, inputs):
    width = weight_a.shape[2]

    def body(g_a, g_b, w_a, w_b, sum_ref, f_ref, x_ref, in_ref, lay_ref, prod_ref, col_ref):
        total = sum_ref[...]
        for g_ref, w_ref in ((g_a, w_a), (g_b, w_b)):
            for c in range(3):
                total = total + dot_nt(g_ref[:, c * width : (c + 1) * width], w_ref[c])
        in_ref[...] = total
        lay_ref[...] = dot(f_ref[...], total.astype(BF16))
        prod_ref[...] = dot_tn(x_ref[...], g_a[...])
        col_ref[...] = jnp.sum(g_a[...].astype(F32), axis=0, keepdims=True)

    model = inputs.shape[1]
    return pl.pallas_call(
        body,
        out_shape=[
            jax.ShapeDtypeStruct(grad_sum.shape, F32),
            jax.ShapeDtypeStruct((features.shape[0], model), F32),
            jax.ShapeDtypeStruct((model, 3 * width), F32),
            jax.ShapeDtypeStruct((1, 3 * width), F32),
        ],
        cost_estimate=NO_COST,
        name="input_back",
    )(grads_a, grads_b, weight_a, weight_b, grad_sum, features, inputs)


def pair_back(inputs, grads, product, columns):
    model = inputs.shape[1]
    wide = grads.shape[1]

    def body(x_ref, g_ref, prod_ref, col_ref, a_ref, b_ref, sum_ref):
        total = (prod_ref[...] + dot_tn(x_ref[...], g_ref[...])).astype(BF16)
        a_ref[...] = total[: model // 2]
        b_ref[...] = total[model // 2 :]
        sum_ref[...] = col_ref[...] + jnp.sum(g_ref[...].astype(F32), axis=0, keepdims=True)

    half = jax.ShapeDtypeStruct((model // 2, wide), BF16)
    return pl.pallas_call(
        body,
        out_shape=[half, half, jax.ShapeDtypeStruct((1, wide), F32)],
        cost_estimate=NO_COST,
        name="pair_back",
    )(inputs, grads, product, columns)


def swap(value):
    size = lax.axis_size("tensor")
    return lax.ppermute(value, "tensor", [(i, (i + 1) % size) for i in range(size)])


def ring_bits(turned):
    size = lax.axis_size("dp")
    bits = [1 << k for k in range(size.bit_length() - 1)]
    return bits[1::-1] + bits[2:] if turned else bits


def ring_steps(bits):
    return [(True, bit) for bit in bits] + [(False, bit) for bit in reversed(bits)]


def side_of(bit):
    return (lax.axis_index("dp") >> (bit.bit_length() - 1)) & 1


def begin(step, value):
    scatter, bit = step
    if not scatter:
        return value, value
    side = side_of(bit)
    half = value.shape[0] // 2
    part = lambda where: lax.dynamic_slice_in_dim(
        value, where * half, half, 0, allow_negative_indices=False
    )
    return part(side), part(1 - side)


def finish(step, kept, send):
    scatter, bit = step
    size = lax.axis_size("dp")
    received = lax.ppermute(send, "dp", [(i, i ^ bit) for i in range(size)])
    if scatter:
        return kept + received
    low = side_of(bit) == 0
    return jnp.concatenate([jnp.where(low, kept, received), jnp.where(low, received, kept)])


def ring_run(steps, value):
    for step in steps:
        value = finish(step, *begin(step, value))
    return value


def update(clip_factor, grads, state):
    share = state[0].shape[1] // BLOCK
    start = lax.axis_index("dp").astype(jnp.int32) * share
    wide, wide_info, thin, thin_info = [], [], [], []
    base = 0
    row = 0
    for grad in grads:
        rows = grad.size // BLOCK
        if grad.ndim == 2 and grad.shape[1] % BLOCK == 0 and grad.shape[0] > 16:
            lanes = grad.shape[1] // BLOCK
            grad = jnp.pad(grad, ((0, -grad.shape[0] % 8), (0, 0)))
            slab = min(grad.shape[0], -(-(share // lanes + 18) // 8) * 8)
            wide.append(grad)
            wide_info.append((base, lanes, grad.shape[0], slab))
        else:
            thin.append(jnp.pad(grad.reshape(rows, BLOCK), ((0, -rows % 8), (0, 0))))
            thin_info.append((base, row, rows))
            row += rows + -rows % 8
        base += rows
    thin_all = jnp.concatenate(thin)
    margin = -(-max(info[1] * info[3] for info in wide_info) // 8) * 8 + 8

    def slab_start(first, info):
        base, lanes, rows, slab = info
        wanted = jnp.maximum(first - base, 0) // (lanes * 8) * 8
        return pl.multiple_of(jnp.minimum(wanted, rows - slab), 8)

    def body(start_ref, clip_ref, *refs):
        wide_refs = refs[: len(wide)]
        thin_ref = refs[len(wide)]
        master, one, two, ema = refs[len(wide) + 1 : len(wide) + 5]
        new_master, new_one, new_two, new_ema, copy, own = refs[len(wide) + 5 :]
        first = start_ref[0]
        own[margin : margin + share, :] = jnp.zeros((share, BLOCK), F32)
        for ref, info in zip(wide_refs, wide_info):
            base, lanes, rows, slab = info

            @pl.when((first < base + rows * lanes) & (first + share > base))
            def _():
                place = margin + base + slab_start(first, info) * lanes - first
                for k in range(lanes):
                    own[pl.ds(place + k, slab, stride=lanes), :] = ref[
                        :, k * BLOCK : (k + 1) * BLOCK
                    ]

        for base, row, rows in thin_info:

            @pl.when((first < base + rows) & (first + share > base))
            def _():
                own[pl.ds(margin + base - first, rows), :] = thin_ref[row : row + rows, :]

        scale = clip_ref[0]

        def advance(row, rows):
            many = -(-rows // 8) * 8
            grad = own[pl.ds(pl.multiple_of(margin + row, 8), many), :].reshape(1, many * BLOCK)
            grad = grad[:, : rows * BLOCK] * scale
            place = (slice(None), pl.ds(pl.multiple_of(row * BLOCK, 8 * BLOCK), rows * BLOCK))
            moment = beta_one * one[place] + (1.0 - beta_one) * grad
            second = beta_two * two[place] + (1.0 - beta_two) * grad * grad
            new_one[place] = moment
            new_two[place] = second
            step_size = (
                moment
                / (1.0 - beta_one**STEP)
                / (jnp.sqrt(second / (1.0 - beta_two**STEP)) + adam_eps)
            )
            weight = master[place]
            weight = weight - learn_rate * (step_size + decay_rate * weight)
            new_master[place] = weight
            new_ema[place] = average_rate * ema[place] + (1.0 - average_rate) * weight
            copy[place] = weight.astype(BF16)

        def many_rows(number, carry):
            advance(number * CHUNK, CHUNK)
            return carry

        lax.fori_loop(0, share // CHUNK, many_rows, 0)
        if share % CHUNK:
            advance(share // CHUNK * CHUNK, share % CHUNK)

    plain = pl.BlockSpec((1, share * BLOCK), lambda i, s: (0, 0))
    specs = [pl.BlockSpec(memory_space=pltpu.SMEM)]
    for grad, info in zip(wide, wide_info):
        specs.append(
            pl.BlockSpec(
                (pl.Element(info[3]), pl.Element(grad.shape[1])),
                lambda i, s, info=info: (slab_start(s[0], info), 0),
            )
        )
    specs.append(pl.BlockSpec(thin_all.shape, lambda i, s: (0, 0)))
    flat = jax.ShapeDtypeStruct((1, share * BLOCK), F32)
    return pl.pallas_call(
        body,
        grid_spec=pltpu.PrefetchScalarGridSpec(
            num_scalar_prefetch=1,
            grid=(1,),
            in_specs=specs + [plain] * 4,
            out_specs=[plain] * 5,
            scratch_shapes=[pltpu.VMEM((2 * margin + share + 8, BLOCK), F32)],
        ),
        out_shape=[flat] * 4 + [jax.ShapeDtypeStruct((1, share * BLOCK), BF16)],
        name="update",
    )(
        start.reshape(1),
        clip_factor.reshape(1),
        *wide,
        thin_all,
        *state,
    )


def per_device(
    hidden_in,
    cotangent,
    box_coords,
    doc_ids,
    buckets,
    layout_weight,
    norm_gains,
    norm_shifts,
    branch_biases,
    qkv_weight,
    query_value_bias,
    output_weight,
    ffn_in_weight,
    ffn_in_bias,
    ffn_out_weight,
    relative_table,
    master_flat,
    moment_one,
    moment_two,
    ema_flat,
):
    turn = lax.axis_index("tensor")
    window = turn.astype(jnp.int32).reshape(1)
    gains = norm_gains.astype(F32)
    norm_offsets = norm_shifts.astype(F32)
    biases = branch_biases.astype(F32)

    small_own = jnp.concatenate(
        [query_value_bias.reshape(-1), ffn_in_bias, relative_table.reshape(-1)]
    )
    qkv_other = swap(qkv_weight)
    small_other = swap(small_own)
    output_other = swap(output_weight)
    ffn_in_other = swap(ffn_in_weight)
    ffn_out_other = swap(ffn_out_weight)
    cuts = (query_value_bias.size, query_value_bias.size + ffn_in_bias.size)
    qv_bias_other = small_other[: cuts[0]].reshape(query_value_bias.shape)
    ffn_bias_other = small_other[cuts[0] : cuts[1]]
    table_other = small_other[cuts[1] :].reshape(relative_table.shape)

    features = box_features(box_coords).astype(BF16)
    embedded = hidden_in.astype(F32) + dot_tn(features, layout_weight)
    inputs = embedded.astype(BF16)
    inputs_swap = swap(inputs)

    qkv_a, context_a, probs_a = attend(
        window, inputs, qkv_weight, query_value_bias, doc_ids, buckets, relative_table
    )
    qkv_b, context_b, probs_b = attend(
        window, inputs, qkv_other, qv_bias_other, doc_ids, buckets, table_other
    )
    context_swap = swap(context_b)
    attn_out = dot(context_a, output_weight) + dot(context_b, output_other) + biases[0]
    normed_one, inv_std_one = normalize(embedded + attn_out)
    mid_norm = normed_one * gains[0] + norm_offsets[0]
    mid_low = mid_norm.astype(BF16)
    mid_swap = swap(mid_low)

    def expand(weight, bias):
        pre = dot(mid_low, weight) + bias.astype(F32)
        share = 0.5 + 0.5 * lax.erf(pre * math.sqrt(0.5))
        slope = share + pre * (math.sqrt(0.5 / math.pi) * jnp.exp(-0.5 * pre * pre))
        return (pre * share).astype(BF16), slope

    hidden_a, slope_a = expand(ffn_in_weight, ffn_in_bias)
    hidden_b, slope_b = expand(ffn_in_other, ffn_bias_other)
    hidden_swap = swap(hidden_b)
    branch = dot(hidden_a, ffn_out_weight) + dot(hidden_b, ffn_out_other) + biases[1]
    normed_two, inv_std_two = normalize(mid_norm + branch)
    hidden_out = (normed_two * gains[1] + norm_offsets[1]).astype(BF16)
    grad_out = cotangent.astype(F32)
    gain_two = jnp.sum(grad_out * normed_two, axis=0)
    shift_two = jnp.sum(grad_out, axis=0)
    grad_sum_two = norm_back(grad_out, normed_two, inv_std_two, gains[1])
    bias_two = jnp.sum(grad_sum_two, axis=0)
    grad_branch = grad_sum_two.astype(BF16)
    grad_branch_swap = swap(grad_branch)

    grad_pre_b = (slope_b * dot_nt(grad_branch, ffn_out_other)).astype(BF16)
    grad_pre_swap = swap(grad_pre_b)
    grad_pre_a = (slope_a * dot_nt(grad_branch, ffn_out_weight)).astype(BF16)
    ffn_out_low = (
        dot_tn(hidden_a, grad_branch) + dot_tn(hidden_swap, grad_branch_swap)
    ).astype(BF16)
    ffn_in_low = (dot_tn(mid_low, grad_pre_a) + dot_tn(mid_swap, grad_pre_swap)).astype(BF16)
    grad_mid = (
        grad_sum_two + dot_nt(grad_pre_a, ffn_in_weight) + dot_nt(grad_pre_b, ffn_in_other)
    )
    gain_one = jnp.sum(grad_mid * normed_one, axis=0)
    shift_one = jnp.sum(grad_mid, axis=0)
    grad_sum_one = norm_back(grad_mid, normed_one, inv_std_one, gains[0])
    bias_one = jnp.sum(grad_sum_one, axis=0)
    grad_attn = grad_sum_one.astype(BF16)
    grad_attn_swap = swap(grad_attn)
    output_grad = dot_tn(context_a, grad_attn) + dot_tn(context_swap, grad_attn_swap)
    grad_context_a = dot_nt(grad_attn, output_weight).astype(BF16)
    grad_context_b = dot_nt(grad_attn, output_other).astype(BF16)

    barrier = lax.optimization_barrier
    steps_a, steps_b = ring_steps(ring_bits(False)), ring_steps(ring_bits(True))
    out_keep, out_send = begin(
        steps_a[0], jnp.concatenate([ffn_out_low, output_grad.astype(BF16)])
    )
    in_keep, in_send = begin(steps_b[0], ffn_in_low)
    (grad_context_a, grad_context_b), out_send, in_send = barrier(
        ((grad_context_a, grad_context_b), out_send, in_send)
    )
    grads_a, grads_b, scores_a, scores_b = attend_back(
        window, (qkv_a, qkv_b), (grad_context_a, grad_context_b), (probs_a, probs_b)
    )
    grads_swap = swap(grads_b)
    width = qkv_weight.shape[2]
    early = input_back(grads_a, grads_b, qkv_weight, qkv_other, grad_sum_one, features, inputs)
    early, out_keep, in_keep = barrier((early, out_keep, in_keep))
    input_grad, layout_part, product, columns = early
    out_sum = finish(steps_a[0], out_keep, out_send)
    in_sum = finish(steps_b[0], in_keep, in_send)

    out_keep, out_send = begin(steps_a[1], out_sum)
    in_keep, in_send = begin(steps_b[1], in_sum)
    product, scores_a, scores_b, out_send, in_send = barrier(
        (product, scores_a, scores_b, out_send, in_send)
    )
    late = pair_back(inputs_swap, grads_swap, product, columns)
    tables = table_sums(window, (scores_a, scores_b), buckets)
    late, tables, out_keep, in_keep = barrier((late, tables, out_keep, in_keep))
    pack_a, pack_b, qv_sums = late
    out_sum = finish(steps_a[1], out_keep, out_send)
    in_sum = finish(steps_b[1], in_keep, in_send)

    plans = {
        "out": (0, steps_a[2:]),
        "in": (0, steps_b[2:]),
        "a": (0, steps_a),
        "b": (0, steps_b),
        "c": (2, steps_b),
    }
    sums = {"out": out_sum, "in": in_sum, "a": pack_a, "b": pack_b}
    last = len(steps_a) - 1
    for number in range(last + 3):
        if number == 2:
            qv_bias_grad = jnp.stack([qv_sums[0, :width], qv_sums[0, 2 * width :]])
            ffn_bias_grad = jnp.sum(grad_pre_a.astype(F32), axis=0) + jnp.sum(
                grad_pre_swap.astype(F32), axis=0
            )
            table_a, table_b = split_tables(tables, NB)
            table_grad = table_a + swap(table_b)
            shared = jnp.concatenate(
                [
                    layout_part,
                    jnp.stack([gain_one, gain_two, shift_one, shift_two, bias_one, bias_two]),
                ]
            )
            cut = shared.shape[0] // lax.axis_size("tensor")
            first_turn = turn == 0
            own_shared = jnp.where(first_turn, shared[:cut], shared[cut:])
            own_shared = own_shared + swap(
                jnp.where(first_turn, shared[cut:], shared[:cut]).astype(BF16)
            ).astype(F32)
            model = layout_part.shape[1]
            small = jnp.concatenate(
                [ffn_bias_grad, qv_bias_grad.reshape(-1), table_grad.reshape(-1)]
            ).astype(BF16)
            small = jnp.pad(small, (0, -small.size % (16 * model))).reshape(-1, model)
            own_rows = own_shared.shape[0] + -own_shared.shape[0] % 16
            unit = 8 * lax.axis_size("dp")
            fill = -(own_rows + small.shape[0]) % unit
            pack_c = jnp.concatenate(
                [
                    jnp.pad(own_shared.astype(BF16), ((0, own_rows - own_shared.shape[0]), (0, 0))),
                    jnp.pad(small, ((0, fill), (0, 0))),
                ]
            )
            sums["c"] = pack_c
        opened = {
            name: begin(steps[number - first], sums[name])
            for name, (first, steps) in plans.items()
            if first <= number < first + len(steps)
        }
        sends = {name: send for name, (_, send) in opened.items()}
        if number == 1:
            sends, tables, layout_part, qv_sums, grad_pre_a, grad_pre_swap = barrier(
                (sends, tables, layout_part, qv_sums, grad_pre_a, grad_pre_swap)
            )
        elif number == last - 1:
            sends, sums["out"], sums["in"] = barrier((sends, sums["out"], sums["in"]))
        elif number == last + 2:
            sends, sums["a"], sums["b"] = barrier((sends, sums["a"], sums["b"]))
        else:
            sends = barrier(sends)
        for name, (kept, _) in opened.items():
            first, steps = plans[name]
            sums[name] = finish(steps[number - first], kept, sends[name])
    out_all, ffn_in_low, pack_a, pack_b, pack_c = (sums[name] for name in ("out", "in", "a", "b", "c"))

    square = sum(
        jnp.sum(jnp.square(member.astype(F32)))
        for member in (out_all, ffn_in_low, pack_a, pack_b, pack_c)
    )
    ffn_out_grad = out_all[: ffn_out_low.shape[0]].astype(F32)
    output_grad = out_all[ffn_out_low.shape[0] :].astype(F32)
    ffn_in_grad = ffn_in_low.astype(F32)
    qkv_grad = jnp.stack(
        [
            jnp.concatenate([part[:, c * width : (c + 1) * width] for part in (pack_a, pack_b)])
            for c in range(3)
        ]
    ).astype(F32)
    own_low = pack_c[:cut]
    few = -(-(ffn_bias_grad.size + qv_bias_grad.size + table_grad.size) // model)
    small = pack_c[own_rows : own_rows + few].astype(F32).reshape(-1)
    place = 0
    smalls = []
    for member in (ffn_bias_grad, qv_bias_grad, table_grad):
        smalls.append(small[place : place + member.size].reshape(member.shape))
        place += member.size
    ffn_bias_grad, qv_bias_grad, table_grad = smalls
    other_low = swap(own_low)
    shared = jnp.where(
        first_turn,
        jnp.concatenate([own_low, other_low]),
        jnp.concatenate([other_low, own_low]),
    ).astype(F32)
    layout_grad = shared[: layout_part.shape[0]]
    gains_grad, shifts_grad, biases_grad = jnp.split(shared[layout_part.shape[0] :], 3)

    grad_norm = jnp.sqrt(square + swap(square))
    clip_factor = clip_limit / jnp.maximum(grad_norm, clip_limit)
    updated = update(
        clip_factor,
        (
            ffn_in_grad,
            ffn_bias_grad,
            ffn_out_grad,
            qkv_grad.reshape(-1, width),
            qv_bias_grad,
            output_grad,
            table_grad,
            own_low.astype(F32),
        ),
        (master_flat, moment_one, moment_two, ema_flat),
    )
    return (
        hidden_out,
        input_grad,
        layout_grad,
        gains_grad,
        shifts_grad,
        biases_grad,
        qkv_grad,
        qv_bias_grad,
        output_grad,
        ffn_in_grad,
        ffn_bias_grad,
        ffn_out_grad,
        table_grad,
        grad_norm,
    ) + tuple(updated)


def solution(mesh):
    return jax.shard_map(
        per_device,
        mesh=mesh,
        in_specs=(
            P(("dp", "tensor"), None),
            P(("dp", "tensor"), None),
            P(None, ("dp", "tensor")),
            P("dp", None),
            P(None, "dp", None, None),
            P(),
            P(),
            P(),
            P(),
            P(None, None, "tensor"),
            P(None, "tensor"),
            P("tensor", None),
            P(None, "tensor"),
            P("tensor"),
            P("tensor", None),
            P(None, None, "tensor"),
            P("tensor", "dp"),
            P("tensor", "dp"),
            P("tensor", "dp"),
            P("tensor", "dp"),
        ),
        out_specs=(
            P(("dp", "tensor"), None),
            P(("dp", "tensor"), None),
            P(),
            P(),
            P(),
            P(),
            P(None, None, "tensor"),
            P(None, "tensor"),
            P("tensor", None),
            P(None, "tensor"),
            P("tensor"),
            P("tensor", None),
            P(None, None, "tensor"),
            P(),
            P("tensor", "dp"),
            P("tensor", "dp"),
            P("tensor", "dp"),
            P("tensor", "dp"),
            P("tensor", "dp"),
        ),
        check_vma=False,
    )
```

```python
import math

import jax
import jax.numpy as jnp
from jax import lax
from jax.experimental import pallas as pl
from jax.experimental.pallas import tpu as pltpu
from jax.sharding import PartitionSpec as P

NB = 32
FEAT = 256
STEP = 10
BLOCK = 128
CHUNK = 32
ATTEND_FLOPS = 1 << 33
BACK_FLOPS = 1 << 35
NO_COST = pl.CostEstimate(flops=1, transcendentals=0, bytes_accessed=1)


norm_eps = 1e-05
learn_rate = 0.02
beta_one = 0.9
beta_two = 0.999
adam_eps = 1e-08
decay_rate = 0.01
average_rate = 0.5
clip_limit = 1.0
mask_fill = -1e30

F32 = jnp.float32
BF16 = jnp.bfloat16
NT = (((1,), (1,)), ((), ()))
TN = (((0,), (0,)), ((), ()))


def dot(left, right):
    return jnp.dot(left, right, preferred_element_type=F32)


def dot_nt(left, right):
    return lax.dot_general(left, right, NT, preferred_element_type=F32)


def dot_tn(left, right):
    return lax.dot_general(left, right, TN, preferred_element_type=F32)


def box_features(coords):
    count = FEAT // 8
    freqs = jnp.exp(-math.log(10000.0) * jnp.arange(count, dtype=F32) / count)
    angles = coords.astype(F32)[:, None, :] * freqs[None, :, None]
    waves = jnp.stack([jnp.sin(angles), jnp.cos(angles)], axis=1)
    return waves.reshape(FEAT, coords.shape[1])


def normalize(value):
    centre = value - jnp.mean(value, axis=-1, keepdims=True)
    inv_std = lax.rsqrt(jnp.mean(centre * centre, axis=-1, keepdims=True) + norm_eps)
    return (centre * inv_std, inv_std)


def norm_back(grad_out, normed, inv_std, gain):
    scaled = grad_out * gain
    return inv_std * (
        scaled
        - jnp.mean(scaled, axis=-1, keepdims=True)
        - normed * jnp.mean(scaled * normed, axis=-1, keepdims=True)
    )


def attend(which, inputs, weight, bias, docs, buckets, table):
    rows, model = inputs.shape
    width = weight.shape[2]
    heads, _, nb = table.shape
    pairs = heads // 2
    half = width // heads
    span = 3 * BLOCK
    blocks = rows // BLOCK
    scale = 1.0 / math.sqrt(half)
    def body(
        which_ref, x_ref, w_ref, bias_ref, doc_ref, b_ref, t_ref, qkv_ref, ctx_ref, p_ref
    ):
        block = pl.program_id(0)

        @pl.when(block == 0)
        def _():
            for c in range(3):
                made = dot(x_ref[...], w_ref[c])
                if c != 1:
                    made = made + bias_ref[c // 2 : c // 2 + 1, :].astype(F32)
                qkv_ref[:, c * width : (c + 1) * width] = made.astype(BF16)

        start = pl.multiple_of(jnp.clip(block - 1, 0, blocks - 3) * BLOCK, BLOCK)
        own_rows = pl.ds(pl.multiple_of(block * BLOCK, BLOCK), BLOCK)
        key_rows = pl.ds(start, span)
        windows = docs.shape[0]

        def docs_at(lanes, count):
            here = doc_ref[:, lanes].astype(F32)
            mine = lax.broadcasted_iota(jnp.int32, (windows, count), 0) == which_ref[0]
            return jnp.sum(jnp.where(mine, here, 0.0), axis=0, keepdims=True)

        diagonal = lax.broadcasted_iota(jnp.int32, (BLOCK, BLOCK), 0) == (
            lax.broadcasted_iota(jnp.int32, (BLOCK, BLOCK), 1)
        )
        docs_here = jnp.broadcast_to(docs_at(own_rows, BLOCK), (BLOCK, BLOCK))
        column = jnp.sum(jnp.where(diagonal, docs_here, 0.0), axis=1, keepdims=True)
        same = column == docs_at(key_rows, span)
        first = b_ref[0, 0, :, key_rows]
        second = b_ref[1, 0, :, key_rows]
        low_lane = lax.broadcasted_iota(jnp.int32, (BLOCK, 2 * half), 1) < half

        def shifted(p, c):
            return pl.ds(pl.multiple_of(c * width + p * 2 * half, 2 * half), 2 * half)

        def one_pair(p, carry):
            cols = shifted(p, 0)
            q2 = qkv_ref[own_rows, cols]
            k2 = qkv_ref[key_rows, shifted(p, 1)]
            v2 = qkv_ref[key_rows, shifted(p, 2)]
            outs = []
            for e in range(2):
                qm = jnp.where(low_lane == (e == 0), q2, jnp.zeros_like(q2))
                raw = dot_nt(qm, k2)
                rows_xy = jnp.concatenate(
                    [t_ref[2 * p + e].astype(F32), jnp.zeros((2, BLOCK - nb), F32)], axis=1
                )
                row_x = jnp.broadcast_to(rows_xy[0:1], (BLOCK, BLOCK))
                row_y = jnp.broadcast_to(rows_xy[1:2], (BLOCK, BLOCK))
                bias = jnp.concatenate(
                    [
                        jnp.take_along_axis(
                            row_x, first[:, c : c + BLOCK], axis=1, mode="promise_in_bounds"
                        )
                        + jnp.take_along_axis(
                            row_y, second[:, c : c + BLOCK], axis=1, mode="promise_in_bounds"
                        )
                        for c in range(0, span, BLOCK)
                    ],
                    axis=1,
                )
                scores = jnp.where(same, raw * scale + bias, mask_fill)
                top = jnp.max(scores, axis=1, keepdims=True)
                weights = jnp.exp(scores - top)
                probs = weights * (1.0 / jnp.sum(weights, axis=1, keepdims=True))
                p_ref[2 * p + e, 0] = probs
                outs.append(dot(probs.astype(BF16), v2))
            ctx_ref[:, cols] = jnp.where(low_lane, outs[0], outs[1]).astype(BF16)
            return carry

        lax.fori_loop(0, pairs, one_pair, 0, unroll=True)

    return pl.pallas_call(
        body,
        grid_spec=pltpu.PrefetchScalarGridSpec(
            num_scalar_prefetch=1,
            grid=(blocks,),
            in_specs=[
                pl.BlockSpec((rows, model), lambda i, w: (0, 0)),
                pl.BlockSpec((3, model, width), lambda i, w: (0, 0, 0)),
                pl.BlockSpec((2, width), lambda i, w: (0, 0)),
                pl.BlockSpec(docs.shape, lambda i, w: (0, 0)),
                pl.BlockSpec((2, 1, BLOCK, rows), lambda i, w: (0, w[0], i, 0)),
                pl.BlockSpec(table.shape, lambda i, w: (0, 0, 0)),
            ],
            out_specs=[
                pl.BlockSpec((rows, 3 * width), lambda i, w: (0, 0)),
                pl.BlockSpec((BLOCK, width), lambda i, w: (i, 0)),
                pl.BlockSpec((heads, 1, BLOCK, span), lambda i, w: (0, i, 0, 0)),
            ],
        ),
        out_shape=[
            jax.ShapeDtypeStruct((rows, 3 * width), BF16),
            jax.ShapeDtypeStruct((rows, width), BF16),
            jax.ShapeDtypeStruct((heads, blocks, BLOCK, span), F32),
        ],
        cost_estimate=pl.CostEstimate(flops=ATTEND_FLOPS, transcendentals=0, bytes_accessed=1 << 23),
        name="attend",
    )(which, inputs, weight, bias, docs, buckets, table)


def attend_back(which, qkvs, grads, probs):
    rows, width = qkvs[0].shape[0], qkvs[0].shape[1] // 3
    heads, blocks, _, span = probs[0].shape
    pairs = heads // 2
    half = width // heads
    scale = 1.0 / math.sqrt(half)

    def body(qkv_a, qkv_b, g_a, g_b, p_a, p_b, d_a, d_b, s_a, s_b, acc_a, acc_b):
        block = pl.program_id(0)
        start = pl.multiple_of(jnp.clip(block - 1, 0, blocks - 3) * BLOCK, BLOCK)
        own_rows = pl.ds(pl.multiple_of(block * BLOCK, BLOCK), BLOCK)
        key_rows = pl.ds(start, span)
        low_lane = lax.broadcasted_iota(jnp.int32, (BLOCK, 2 * half), 1) < half

        @pl.when(block == 0)
        def _():
            acc_a[...] = jnp.zeros_like(acc_a)
            acc_b[...] = jnp.zeros_like(acc_b)

        for qkv_ref, g_ref, p_ref, d_ref, s_ref, sums in (
            (qkv_a, g_a, p_a, d_a, s_a, acc_a),
            (qkv_b, g_b, p_b, d_b, s_b, acc_b),
        ):

            def shifted(p, c):
                return pl.ds(pl.multiple_of(c * width + p * 2 * half, 2 * half), 2 * half)

            def one_pair(p, carry):
                cols = shifted(p, 0)
                q2 = qkv_ref[own_rows, cols]
                g2 = g_ref[:, cols]
                k2 = qkv_ref[key_rows, shifted(p, 1)]
                v2 = qkv_ref[key_rows, shifted(p, 2)]
                dqs = []
                dk = sums[0, key_rows, cols]
                dv = sums[1, key_rows, cols]
                for e in range(2):
                    mine = low_lane == (e == 0)
                    qm = jnp.where(mine, q2, jnp.zeros_like(q2))
                    gm = jnp.where(mine, g2, jnp.zeros_like(g2))
                    pr = p_ref[2 * p + e, 0]
                    gp = dot_nt(gm, v2)
                    gs = pr * (gp - jnp.sum(pr * gp, axis=1, keepdims=True))
                    s_ref[2 * p + e, 0] = gs
                    raw = (gs * scale).astype(BF16)
                    dqs.append(dot(raw, k2))
                    dk = dk + dot_tn(raw, qm)
                    dv = dv + dot_tn(pr.astype(BF16), gm)
                d_ref[own_rows, cols] = jnp.where(low_lane, dqs[0], dqs[1]).astype(BF16)
                sums[0, key_rows, cols] = dk
                sums[1, key_rows, cols] = dv
                return carry

            lax.fori_loop(0, pairs, one_pair, 0, unroll=True)

        @pl.when(block == blocks - 1)
        def _():
            for d_ref, sums in ((d_a, acc_a), (d_b, acc_b)):
                d_ref[:, width : 2 * width] = sums[0].astype(BF16)
                d_ref[:, 2 * width :] = sums[1].astype(BF16)

    whole = pl.BlockSpec((rows, 3 * width), lambda i: (0, 0))
    part = pl.BlockSpec((BLOCK, width), lambda i: (i, 0))
    prob = pl.BlockSpec((heads, 1, BLOCK, span), lambda i: (0, i, 0, 0))
    shape = jax.ShapeDtypeStruct((rows, 3 * width), BF16)
    score = jax.ShapeDtypeStruct(probs[0].shape, F32)
    return pl.pallas_call(
        body,
        grid=(blocks,),
        in_specs=[whole, whole, part, part, prob, prob],
        out_specs=[whole, whole, prob, prob],
        scratch_shapes=[
            pltpu.VMEM((2, rows, width), F32),
            pltpu.VMEM((2, rows, width), F32),
        ],
        out_shape=[shape, shape, score, score],
        input_output_aliases={4: 2, 5: 3},
        cost_estimate=pl.CostEstimate(
            flops=BACK_FLOPS, transcendentals=0, bytes_accessed=1 << 24
        ),
        name="attend_back",
    )(*qkvs, *grads, *probs)


def table_sums(which, scores, buckets):
    heads, blocks, _, span = scores[0].shape
    nb = NB
    rows = blocks * BLOCK
    group = 8
    codes = 2 * nb
    lanes = 2 * 2 * heads * group

    def body(which_ref, s_a, s_b, b_ref, tab_ref, acc_ref):
        block = pl.program_id(0)
        start = pl.multiple_of(jnp.clip(block - 1, 0, blocks - 3) * BLOCK, BLOCK)
        key_rows = pl.ds(start, span)

        @pl.when(block == 0)
        def _():
            acc_ref[...] = jnp.zeros_like(acc_ref)

        code_ids = lax.broadcasted_iota(jnp.int32, (nb, span), 0).astype(F32).astype(BF16)
        one, zero = jnp.ones((), BF16), jnp.zeros((), BF16)

        def one_side(r8):
            b0 = b_ref[0, 0, r8, key_rows].astype(F32)
            b1 = b_ref[1, 0, r8, key_rows].astype(F32)
            pieces = []
            for r in range(group):
                for b in (b0, b1):
                    row = jnp.broadcast_to(b[r : r + 1], (nb, span)).astype(BF16)
                    pieces.append(jnp.where(row == code_ids, one, zero))
            gg = jnp.concatenate(
                [ref[:, 0, r8, :].reshape(heads * group, span) for ref in (s_a, s_b)], axis=0
            )
            upper = gg.astype(BF16)
            lower = (gg - upper.astype(F32)).astype(BF16)
            return jnp.concatenate(pieces, axis=0), jnp.concatenate([upper, lower], axis=0)

        def two_groups(g, carry):
            sides = [
                one_side(pl.ds(pl.multiple_of((2 * g + k) * group, group), group))
                for k in range(2)
            ]
            onehot, both = (jnp.concatenate(parts, axis=1) for parts in zip(*sides))
            acc_ref[...] += dot_nt(onehot, both)
            return carry

        lax.fori_loop(0, BLOCK // group // 2, two_groups, 0)

        @pl.when(block == blocks - 1)
        def _():
            lane_row = lax.broadcasted_iota(jnp.int32, (codes, lanes), 1) % group
            total = jnp.zeros((codes, lanes), F32)
            for r in range(group):
                total = total + jnp.where(
                    lane_row == r, acc_ref[r * codes : (r + 1) * codes, :], 0.0
                )
            tab_ref[...] = total

    prob = pl.BlockSpec((heads, 1, BLOCK, span), lambda i, w: (0, i, 0, 0))
    return pl.pallas_call(
        body,
        grid_spec=pltpu.PrefetchScalarGridSpec(
            num_scalar_prefetch=1,
            grid=(blocks,),
            in_specs=[
                prob,
                prob,
                pl.BlockSpec((2, 1, BLOCK, rows), lambda i, w: (0, w[0], i, 0)),
            ],
            out_specs=pl.BlockSpec((codes, lanes), lambda i, w: (0, 0)),
            scratch_shapes=[pltpu.VMEM((group * codes, lanes), F32)],
        ),
        out_shape=jax.ShapeDtypeStruct((codes, lanes), F32),
        cost_estimate=NO_COST,
        name="table_sums",
    )(which, *scores, buckets)


def input_back(grads_a, grads_b, weight_a, weight_b, grad_sum, features, inputs):
    width = weight_a.shape[2]

    def body(g_a, g_b, w_a, w_b, sum_ref, f_ref, x_ref, in_ref, lay_ref, prod_ref, col_ref):
        total = sum_ref[...]
        for g_ref, w_ref in ((g_a, w_a), (g_b, w_b)):
            for c in range(3):
                total = total + dot_nt(g_ref[:, c * width : (c + 1) * width], w_ref[c])
        in_ref[...] = total
        lay_ref[...] = dot(f_ref[...], total.astype(BF16))
        prod_ref[...] = dot_tn(x_ref[...], g_a[...])
        col_ref[...] = jnp.sum(g_a[...].astype(F32), axis=0, keepdims=True)

    model = inputs.shape[1]
    return pl.pallas_call(
        body,
        out_shape=[
            jax.ShapeDtypeStruct(grad_sum.shape, F32),
            jax.ShapeDtypeStruct((features.shape[0], model), F32),
            jax.ShapeDtypeStruct((model, 3 * width), F32),
            jax.ShapeDtypeStruct((1, 3 * width), F32),
        ],
        cost_estimate=NO_COST,
        name="input_back",
    )(grads_a, grads_b, weight_a, weight_b, grad_sum, features, inputs)


def pair_back(inputs, grads, product, columns):
    model = inputs.shape[1]
    wide = grads.shape[1]

    def body(x_ref, g_ref, prod_ref, col_ref, a_ref, b_ref, sum_ref):
        total = (prod_ref[...] + dot_tn(x_ref[...], g_ref[...])).astype(BF16)
        a_ref[...] = total[: model // 2]
        b_ref[...] = total[model // 2 :]
        sum_ref[...] = col_ref[...] + jnp.sum(g_ref[...].astype(F32), axis=0, keepdims=True)

    half = jax.ShapeDtypeStruct((model // 2, wide), BF16)
    return pl.pallas_call(
        body,
        out_shape=[half, half, jax.ShapeDtypeStruct((1, wide), F32)],
        cost_estimate=NO_COST,
        name="pair_back",
    )(inputs, grads, product, columns)


def small_parts(turn, layout, stats, tables, columns, pre_a, pre_b, cut):
    rows, model = layout.shape
    width = model // 2
    tall = -(-(cut + 1) // 16) * 16
    used = cut + 2 + pre_a.shape[1] // model
    unit = 8 * lax.axis_size("dp")
    full_rows = -(-used // unit) * unit

    def body(turn_ref, lay_ref, *refs):
        stat_refs, refs = refs[:6], refs[6:]
        tab_ref, col_ref, a_ref, b_ref, own_ref, other_ref, low, high = refs
        lanes = tab_ref.shape[1] // 2
        heads = lanes // 16
        codes = tab_ref.shape[0]
        table = tab_ref[:, 0:lanes] + tab_ref[:, lanes : 2 * lanes]
        table = jnp.concatenate([table, jnp.zeros((codes, BLOCK - lanes), F32)], axis=1)
        for step in (1, 2, 4):
            table = table + pltpu.roll(table, BLOCK - step, 1)
        code = lax.broadcasted_iota(jnp.int32, (codes, BLOCK), 0)
        lane = lax.broadcasted_iota(jnp.int32, (codes, BLOCK), 1)

        def table_row(side, ref):
            for c in range(0, codes * heads, BLOCK):
                index = side * heads * 8 + (lane + c) % heads * 8
                value = jnp.take_along_axis(table, index, axis=1, mode="promise_in_bounds")
                value = jnp.where((lane + c) // heads == code, value, 0.0)
                ref[cut : cut + 1, c : c + BLOCK] = jnp.sum(value, axis=0, keepdims=True)

        low[...] = jnp.zeros_like(low)
        high[...] = jnp.zeros_like(high)
        low[0:cut, :] = lay_ref[0:cut, :]
        high[0 : rows - cut, :] = lay_ref[cut:rows, :]
        for k, ref in enumerate(stat_refs):
            high[rows - cut + k : rows - cut + k + 1, :] = ref[...]
        first = jnp.full(low.shape, turn_ref[0], jnp.int32) == 0
        own_ref[...] = jnp.zeros_like(own_ref)
        own_ref[0:tall, :] = jnp.where(first, low[...], high[...])
        table_row(0, own_ref)
        own_ref[cut + 1 : cut + 2, 0:width] = col_ref[:, 0:width]
        own_ref[cut + 1 : cut + 2, width:model] = col_ref[:, 2 * width : 3 * width]
        total = jnp.sum(a_ref[...].astype(F32), axis=0, keepdims=True) + jnp.sum(
            b_ref[...].astype(F32), axis=0, keepdims=True
        )
        for k in range(used - cut - 2):
            own_ref[cut + 2 + k : cut + 3 + k, :] = total[:, k * model : (k + 1) * model]
        low[...] = jnp.where(first, high[...], low[...])
        table_row(1, low)
        other_ref[...] = low[...].astype(BF16)

    def full(value):
        return pl.BlockSpec(value.shape, lambda i, w: (0,) * value.ndim)

    operands = (layout, *stats, tables, columns, pre_a, pre_b)
    outs = [
        jax.ShapeDtypeStruct((full_rows, model), F32),
        jax.ShapeDtypeStruct((tall, model), BF16),
    ]
    return pl.pallas_call(
        body,
        grid_spec=pltpu.PrefetchScalarGridSpec(
            num_scalar_prefetch=1,
            grid=(1,),
            in_specs=[full(value) for value in operands],
            out_specs=[full(value) for value in outs],
            scratch_shapes=[pltpu.VMEM((tall, model), F32)] * 2,
        ),
        out_shape=outs,
        cost_estimate=NO_COST,
        name="small_parts",
    )(turn, *operands)


def swap(value):
    size = lax.axis_size("tensor")
    return lax.ppermute(value, "tensor", [(i, (i + 1) % size) for i in range(size)])


def ring_bits(turned):
    size = lax.axis_size("dp")
    bits = [1 << k for k in range(size.bit_length() - 1)]
    return bits[1::-1] + bits[2:] if turned else bits


def ring_steps(bits):
    return [(True, bit) for bit in bits] + [(False, bit) for bit in reversed(bits)]


def side_of(bit):
    return (lax.axis_index("dp") >> (bit.bit_length() - 1)) & 1


def begin(step, value):
    scatter, bit = step
    if not scatter:
        return value, value
    side = side_of(bit)
    half = value.shape[0] // 2
    part = lambda where: lax.dynamic_slice_in_dim(
        value, where * half, half, 0, allow_negative_indices=False
    )
    return part(side), part(1 - side)


def finish(step, kept, send):
    scatter, bit = step
    size = lax.axis_size("dp")
    received = lax.ppermute(send, "dp", [(i, i ^ bit) for i in range(size)])
    if scatter:
        return kept + received
    low = side_of(bit) == 0
    return jnp.concatenate([jnp.where(low, kept, received), jnp.where(low, received, kept)])


def ring_run(steps, value):
    for step in steps:
        value = finish(step, *begin(step, value))
    return value


def update(clip_factor, grads, state):
    share = state[0].shape[1] // BLOCK
    start = lax.axis_index("dp").astype(jnp.int32) * share
    wide, wide_info, thin, thin_info = [], [], [], []
    base = 0
    row = 0
    for grad in grads:
        rows = grad.size // BLOCK
        if grad.ndim == 2 and grad.shape[1] % BLOCK == 0 and grad.shape[0] > 16:
            lanes = grad.shape[1] // BLOCK
            grad = jnp.pad(grad, ((0, -grad.shape[0] % 8), (0, 0)))
            slab = min(grad.shape[0], -(-(share // lanes + 18) // 8) * 8)
            wide.append(grad)
            wide_info.append((base, lanes, grad.shape[0], slab))
        else:
            thin.append(jnp.pad(grad.reshape(rows, BLOCK), ((0, -rows % 8), (0, 0))))
            thin_info.append((base, row, rows))
            row += rows + -rows % 8
        base += rows
    thin_all = jnp.concatenate(thin)
    margin = -(-max(info[1] * info[3] for info in wide_info) // 8) * 8 + 8

    def slab_start(first, info):
        base, lanes, rows, slab = info
        wanted = jnp.maximum(first - base, 0) // (lanes * 8) * 8
        return pl.multiple_of(jnp.minimum(wanted, rows - slab), 8)

    def body(start_ref, clip_ref, *refs):
        wide_refs = refs[: len(wide)]
        thin_ref = refs[len(wide)]
        master, one, two, ema = refs[len(wide) + 1 : len(wide) + 5]
        new_master, new_one, new_two, new_ema, copy, own = refs[len(wide) + 5 :]
        first = start_ref[0]
        own[margin : margin + share, :] = jnp.zeros((share, BLOCK), F32)
        for ref, info in zip(wide_refs, wide_info):
            base, lanes, rows, slab = info

            @pl.when((first < base + rows * lanes) & (first + share > base))
            def _():
                place = margin + base + slab_start(first, info) * lanes - first
                for k in range(lanes):
                    own[pl.ds(place + k, slab, stride=lanes), :] = ref[
                        :, k * BLOCK : (k + 1) * BLOCK
                    ]

        for base, row, rows in thin_info:

            @pl.when((first < base + rows) & (first + share > base))
            def _():
                own[pl.ds(margin + base - first, rows), :] = thin_ref[row : row + rows, :]

        scale = clip_ref[0]

        def advance(row, rows):
            many = -(-rows // 8) * 8
            grad = own[pl.ds(pl.multiple_of(margin + row, 8), many), :].reshape(1, many * BLOCK)
            grad = grad[:, : rows * BLOCK] * scale
            place = (slice(None), pl.ds(pl.multiple_of(row * BLOCK, 8 * BLOCK), rows * BLOCK))
            moment = beta_one * one[place] + (1.0 - beta_one) * grad
            second = beta_two * two[place] + (1.0 - beta_two) * grad * grad
            new_one[place] = moment
            new_two[place] = second
            step_size = (
                moment
                / (1.0 - beta_one**STEP)
                / (jnp.sqrt(second / (1.0 - beta_two**STEP)) + adam_eps)
            )
            weight = master[place]
            weight = weight - learn_rate * (step_size + decay_rate * weight)
            new_master[place] = weight
            new_ema[place] = average_rate * ema[place] + (1.0 - average_rate) * weight
            copy[place] = weight.astype(BF16)

        def many_rows(number, carry):
            advance(number * CHUNK, CHUNK)
            return carry

        lax.fori_loop(0, share // CHUNK, many_rows, 0)
        if share % CHUNK:
            advance(share // CHUNK * CHUNK, share % CHUNK)

    plain = pl.BlockSpec((1, share * BLOCK), lambda i, s: (0, 0))
    specs = [pl.BlockSpec(memory_space=pltpu.SMEM)]
    for grad, info in zip(wide, wide_info):
        specs.append(
            pl.BlockSpec(
                (pl.Element(info[3]), pl.Element(grad.shape[1])),
                lambda i, s, info=info: (slab_start(s[0], info), 0),
            )
        )
    specs.append(pl.BlockSpec(thin_all.shape, lambda i, s: (0, 0)))
    flat = jax.ShapeDtypeStruct((1, share * BLOCK), F32)
    return pl.pallas_call(
        body,
        grid_spec=pltpu.PrefetchScalarGridSpec(
            num_scalar_prefetch=1,
            grid=(1,),
            in_specs=specs + [plain] * 4,
            out_specs=[plain] * 5,
            scratch_shapes=[pltpu.VMEM((2 * margin + share + 8, BLOCK), F32)],
        ),
        out_shape=[flat] * 4 + [jax.ShapeDtypeStruct((1, share * BLOCK), BF16)],
        name="update",
    )(
        start.reshape(1),
        clip_factor.reshape(1),
        *wide,
        thin_all,
        *state,
    )


def per_device(
    hidden_in,
    cotangent,
    box_coords,
    doc_ids,
    buckets,
    layout_weight,
    norm_gains,
    norm_shifts,
    branch_biases,
    qkv_weight,
    query_value_bias,
    output_weight,
    ffn_in_weight,
    ffn_in_bias,
    ffn_out_weight,
    relative_table,
    master_flat,
    moment_one,
    moment_two,
    ema_flat,
):
    turn = lax.axis_index("tensor")
    window = turn.astype(jnp.int32).reshape(1)
    gains = norm_gains.astype(F32)
    norm_offsets = norm_shifts.astype(F32)
    biases = branch_biases.astype(F32)

    table_own = jnp.transpose(relative_table, (2, 0, 1))
    qkv_other = swap(qkv_weight)
    qv_bias_other = swap(query_value_bias)
    table_other = swap(table_own)
    output_other = swap(output_weight)
    ffn_in_other = swap(ffn_in_weight)
    ffn_bias_other = swap(ffn_in_bias)
    ffn_out_other = swap(ffn_out_weight)

    features = box_features(box_coords).astype(BF16)
    embedded = hidden_in.astype(F32) + dot_tn(features, layout_weight)
    inputs = embedded.astype(BF16)
    inputs_swap = swap(inputs)

    qkv_a, context_a, probs_a = attend(
        window, inputs, qkv_weight, query_value_bias, doc_ids, buckets, table_own
    )
    qkv_b, context_b, probs_b = attend(
        window, inputs, qkv_other, qv_bias_other, doc_ids, buckets, table_other
    )
    context_swap = swap(context_b)
    attn_out = dot(context_a, output_weight) + dot(context_b, output_other) + biases[0]
    normed_one, inv_std_one = normalize(embedded + attn_out)
    mid_norm = normed_one * gains[0] + norm_offsets[0]
    mid_low = mid_norm.astype(BF16)
    mid_swap = swap(mid_low)

    def expand(weight, bias):
        pre = dot(mid_low, weight) + bias.astype(F32)
        share = 0.5 + 0.5 * lax.erf(pre * math.sqrt(0.5))
        slope = share + pre * (math.sqrt(0.5 / math.pi) * jnp.exp(-0.5 * pre * pre))
        return (pre * share).astype(BF16), slope

    hidden_a, slope_a = expand(ffn_in_weight, ffn_in_bias)
    hidden_b, slope_b = expand(ffn_in_other, ffn_bias_other)
    hidden_swap = swap(hidden_b)
    branch = dot(hidden_a, ffn_out_weight) + dot(hidden_b, ffn_out_other) + biases[1]
    normed_two, inv_std_two = normalize(mid_norm + branch)
    hidden_out = (normed_two * gains[1] + norm_offsets[1]).astype(BF16)
    grad_out = cotangent.astype(F32)
    gain_two = jnp.sum(grad_out * normed_two, axis=0, keepdims=True)
    shift_two = jnp.sum(grad_out, axis=0, keepdims=True)
    grad_sum_two = norm_back(grad_out, normed_two, inv_std_two, gains[1])
    bias_two = jnp.sum(grad_sum_two, axis=0, keepdims=True)
    grad_branch = grad_sum_two.astype(BF16)
    grad_branch_swap = swap(grad_branch)

    grad_pre_b = (slope_b * dot_nt(grad_branch, ffn_out_other)).astype(BF16)
    grad_pre_swap = swap(grad_pre_b)
    grad_pre_a = (slope_a * dot_nt(grad_branch, ffn_out_weight)).astype(BF16)
    ffn_out_low = (
        dot_tn(hidden_a, grad_branch) + dot_tn(hidden_swap, grad_branch_swap)
    ).astype(BF16)
    ffn_in_low = (dot_tn(mid_low, grad_pre_a) + dot_tn(mid_swap, grad_pre_swap)).astype(BF16)
    grad_mid = (
        grad_sum_two + dot_nt(grad_pre_a, ffn_in_weight) + dot_nt(grad_pre_b, ffn_in_other)
    )
    gain_one = jnp.sum(grad_mid * normed_one, axis=0, keepdims=True)
    shift_one = jnp.sum(grad_mid, axis=0, keepdims=True)
    grad_sum_one = norm_back(grad_mid, normed_one, inv_std_one, gains[0])
    bias_one = jnp.sum(grad_sum_one, axis=0, keepdims=True)
    grad_attn = grad_sum_one.astype(BF16)
    grad_attn_swap = swap(grad_attn)
    output_grad = dot_tn(context_a, grad_attn) + dot_tn(context_swap, grad_attn_swap)
    grad_context_a = dot_nt(grad_attn, output_weight).astype(BF16)
    grad_context_b = dot_nt(grad_attn, output_other).astype(BF16)

    barrier = lax.optimization_barrier
    steps_a, steps_b = ring_steps(ring_bits(False)), ring_steps(ring_bits(True))
    out_keep, out_send = begin(
        steps_a[0], jnp.concatenate([ffn_out_low, output_grad.astype(BF16)])
    )
    in_keep, in_send = begin(steps_b[0], ffn_in_low)
    (grad_context_a, grad_context_b), out_send, in_send = barrier(
        ((grad_context_a, grad_context_b), out_send, in_send)
    )
    grads_a, grads_b, scores_a, scores_b = attend_back(
        window, (qkv_a, qkv_b), (grad_context_a, grad_context_b), (probs_a, probs_b)
    )
    grads_swap = swap(grads_b)
    width = qkv_weight.shape[2]
    early = input_back(grads_a, grads_b, qkv_weight, qkv_other, grad_sum_one, features, inputs)
    early, out_keep, in_keep = barrier((early, out_keep, in_keep))
    input_grad, layout_part, product, columns = early
    out_sum = finish(steps_a[0], out_keep, out_send)
    in_sum = finish(steps_b[0], in_keep, in_send)

    out_keep, out_send = begin(steps_a[1], out_sum)
    in_keep, in_send = begin(steps_b[1], in_sum)
    product, scores_a, scores_b, out_send, in_send = barrier(
        (product, scores_a, scores_b, out_send, in_send)
    )
    late = pair_back(inputs_swap, grads_swap, product, columns)
    tables = table_sums(window, (scores_a, scores_b), buckets)
    late, tables, out_keep, in_keep = barrier((late, tables, out_keep, in_keep))
    pack_a, pack_b, qv_sums = late
    out_sum = finish(steps_a[1], out_keep, out_send)
    in_sum = finish(steps_b[1], in_keep, in_send)

    plans = {
        "out": (0, steps_a[2:]),
        "in": (0, steps_b[2:]),
        "a": (0, steps_a),
        "b": (0, steps_b),
        "c": (2, steps_b),
    }
    sums = {"out": out_sum, "in": in_sum, "a": pack_a, "b": pack_b}
    last = len(steps_a) - 1
    for number in range(last + 3):
        if number == 2:
            other = swap(other_shared).astype(F32)
            pack_c = own_shared + jnp.pad(
                other, ((0, own_shared.shape[0] - other.shape[0]), (0, 0))
            )
            pack_c = pack_c.astype(BF16)
            sums["c"] = pack_c
        opened = {
            name: begin(steps[number - first], sums[name])
            for name, (first, steps) in plans.items()
            if first <= number < first + len(steps)
        }
        sends = {name: send for name, (_, send) in opened.items()}
        if number == 1:
            sends, tables, qv_sums, layout_part = barrier((sends, tables, qv_sums, layout_part))
            cut = (layout_part.shape[0] + 6) // lax.axis_size("tensor")
            own_shared, other_shared = small_parts(
                window,
                layout_part,
                (gain_one, gain_two, shift_one, shift_two, bias_one, bias_two),
                tables,
                qv_sums,
                grad_pre_a,
                grad_pre_swap,
                cut,
            )
        elif number == last - 1:
            sends, sums["out"], sums["in"] = barrier((sends, sums["out"], sums["in"]))
        elif number == last + 2:
            sends, sums["a"], sums["b"] = barrier((sends, sums["a"], sums["b"]))
        else:
            sends = barrier(sends)
        for name, (kept, _) in opened.items():
            first, steps = plans[name]
            sums[name] = finish(steps[number - first], kept, sends[name])
    out_all, ffn_in_low, pack_a, pack_b, pack_c = (sums[name] for name in ("out", "in", "a", "b", "c"))

    square = sum(
        jnp.sum(jnp.square(member.astype(F32)))
        for member in (out_all, ffn_in_low, pack_a, pack_b, pack_c)
    )
    ffn_out_grad = out_all[: ffn_out_low.shape[0]].astype(F32)
    output_grad = out_all[ffn_out_low.shape[0] :].astype(F32)
    ffn_in_grad = ffn_in_low.astype(F32)
    qkv_grad = jnp.stack(
        [
            jnp.concatenate([part[:, c * width : (c + 1) * width] for part in (pack_a, pack_b)])
            for c in range(3)
        ]
    ).astype(F32)
    own_low = pack_c[:cut]
    small = pack_c[cut : cut + 4].astype(F32)
    table_grad = small[0, : relative_table.size].reshape(relative_table.shape)
    qv_bias_grad = small[1].reshape(query_value_bias.shape)
    ffn_bias_grad = small[2:4].reshape(-1)
    first_turn = turn == 0
    other_low = swap(own_low)
    shared = jnp.where(
        first_turn,
        jnp.concatenate([own_low, other_low]),
        jnp.concatenate([other_low, own_low]),
    ).astype(F32)
    layout_grad = shared[: layout_part.shape[0]]
    gains_grad, shifts_grad, biases_grad = jnp.split(shared[layout_part.shape[0] :], 3)

    grad_norm = jnp.sqrt(square + swap(square))
    clip_factor = clip_limit / jnp.maximum(grad_norm, clip_limit)
    updated = update(
        clip_factor,
        (
            ffn_in_grad,
            ffn_bias_grad,
            ffn_out_grad,
            qkv_grad.reshape(-1, width),
            qv_bias_grad,
            output_grad,
            table_grad,
            own_low.astype(F32),
        ),
        (master_flat, moment_one, moment_two, ema_flat),
    )
    return (
        hidden_out,
        input_grad,
        layout_grad,
        gains_grad,
        shifts_grad,
        biases_grad,
        qkv_grad,
        qv_bias_grad,
        output_grad,
        ffn_in_grad,
        ffn_bias_grad,
        ffn_out_grad,
        table_grad,
        grad_norm,
    ) + tuple(updated)


def solution(mesh):
    return jax.shard_map(
        per_device,
        mesh=mesh,
        in_specs=(
            P(("dp", "tensor"), None),
            P(("dp", "tensor"), None),
            P(None, ("dp", "tensor")),
            P("dp", None),
            P(None, "dp", None, None),
            P(),
            P(),
            P(),
            P(),
            P(None, None, "tensor"),
            P(None, "tensor"),
            P("tensor", None),
            P(None, "tensor"),
            P("tensor"),
            P("tensor", None),
            P(None, None, "tensor"),
            P("tensor", "dp"),
            P("tensor", "dp"),
            P("tensor", "dp"),
            P("tensor", "dp"),
        ),
        out_specs=(
            P(("dp", "tensor"), None),
            P(("dp", "tensor"), None),
            P(),
            P(),
            P(),
            P(),
            P(None, None, "tensor"),
            P(None, "tensor"),
            P("tensor", None),
            P(None, "tensor"),
            P("tensor"),
            P("tensor", None),
            P(None, None, "tensor"),
            P(),
            P("tensor", "dp"),
            P("tensor", "dp"),
            P("tensor", "dp"),
            P("tensor", "dp"),
            P("tensor", "dp"),
        ),
        check_vma=False,
    )
```

```python
import math

import jax
import jax.numpy as jnp
from jax import lax
from jax.experimental import pallas as pl
from jax.experimental.pallas import tpu as pltpu
from jax.sharding import PartitionSpec as P

NB = 32
FEAT = 256
STEP = 10
BLOCK = 128
CHUNK = 32
ATTEND_FLOPS = 1 << 33
BACK_FLOPS = 1 << 35
NO_COST = pl.CostEstimate(flops=1, transcendentals=0, bytes_accessed=1)


norm_eps = 1e-05
learn_rate = 0.02
beta_one = 0.9
beta_two = 0.999
adam_eps = 1e-08
decay_rate = 0.01
average_rate = 0.5
clip_limit = 1.0
mask_fill = -1e30

F32 = jnp.float32
BF16 = jnp.bfloat16
NT = (((1,), (1,)), ((), ()))
TN = (((0,), (0,)), ((), ()))


def dot(left, right):
    return jnp.dot(left, right, preferred_element_type=F32)


def dot_nt(left, right):
    return lax.dot_general(left, right, NT, preferred_element_type=F32)


def dot_tn(left, right):
    return lax.dot_general(left, right, TN, preferred_element_type=F32)


def box_features(coords):
    count = FEAT // 8
    freqs = jnp.exp(-math.log(10000.0) * jnp.arange(count, dtype=F32) / count)
    angles = coords.astype(F32)[:, None, :] * freqs[None, :, None]
    waves = jnp.stack([jnp.sin(angles), jnp.cos(angles)], axis=1)
    return waves.reshape(FEAT, coords.shape[1])


def normalize(value):
    centre = value - jnp.mean(value, axis=-1, keepdims=True)
    inv_std = lax.rsqrt(jnp.mean(centre * centre, axis=-1, keepdims=True) + norm_eps)
    return (centre * inv_std, inv_std)


def norm_back(grad_out, normed, inv_std, gain):
    scaled = grad_out * gain
    return inv_std * (
        scaled
        - jnp.mean(scaled, axis=-1, keepdims=True)
        - normed * jnp.mean(scaled * normed, axis=-1, keepdims=True)
    )


def attend(which, inputs, weight, bias, docs, buckets, table):
    rows, model = inputs.shape
    width = weight.shape[2]
    heads, _, nb = table.shape
    pairs = heads // 2
    half = width // heads
    span = 3 * BLOCK
    blocks = rows // BLOCK
    scale = 1.0 / math.sqrt(half)
    def body(
        which_ref, x_ref, w_ref, bias_ref, doc_ref, b_ref, t_ref, qkv_ref, ctx_ref, p_ref
    ):
        block = pl.program_id(0)

        @pl.when(block == 0)
        def _():
            for c in range(3):
                made = dot(x_ref[...], w_ref[c])
                if c != 1:
                    made = made + bias_ref[c // 2 : c // 2 + 1, :].astype(F32)
                qkv_ref[:, c * width : (c + 1) * width] = made.astype(BF16)

        start = pl.multiple_of(jnp.clip(block - 1, 0, blocks - 3) * BLOCK, BLOCK)
        own_rows = pl.ds(pl.multiple_of(block * BLOCK, BLOCK), BLOCK)
        key_rows = pl.ds(start, span)
        windows = docs.shape[0]

        def docs_at(lanes, count):
            here = doc_ref[:, lanes].astype(F32)
            mine = lax.broadcasted_iota(jnp.int32, (windows, count), 0) == which_ref[0]
            return jnp.sum(jnp.where(mine, here, 0.0), axis=0, keepdims=True)

        diagonal = lax.broadcasted_iota(jnp.int32, (BLOCK, BLOCK), 0) == (
            lax.broadcasted_iota(jnp.int32, (BLOCK, BLOCK), 1)
        )
        docs_here = jnp.broadcast_to(docs_at(own_rows, BLOCK), (BLOCK, BLOCK))
        column = jnp.sum(jnp.where(diagonal, docs_here, 0.0), axis=1, keepdims=True)
        same = column == docs_at(key_rows, span)
        first = b_ref[0, 0, :, key_rows]
        second = b_ref[1, 0, :, key_rows]
        low_lane = lax.broadcasted_iota(jnp.int32, (BLOCK, 2 * half), 1) < half

        def shifted(p, c):
            return pl.ds(pl.multiple_of(c * width + p * 2 * half, 2 * half), 2 * half)

        def one_pair(p, carry):
            cols = shifted(p, 0)
            q2 = qkv_ref[own_rows, cols]
            k2 = qkv_ref[key_rows, shifted(p, 1)]
            v2 = qkv_ref[key_rows, shifted(p, 2)]
            outs = []
            for e in range(2):
                qm = jnp.where(low_lane == (e == 0), q2, jnp.zeros_like(q2))
                raw = dot_nt(qm, k2)
                rows_xy = jnp.concatenate(
                    [t_ref[2 * p + e].astype(F32), jnp.zeros((2, BLOCK - nb), F32)], axis=1
                )
                row_x = jnp.broadcast_to(rows_xy[0:1], (BLOCK, BLOCK))
                row_y = jnp.broadcast_to(rows_xy[1:2], (BLOCK, BLOCK))
                bias = jnp.concatenate(
                    [
                        jnp.take_along_axis(
                            row_x, first[:, c : c + BLOCK], axis=1, mode="promise_in_bounds"
                        )
                        + jnp.take_along_axis(
                            row_y, second[:, c : c + BLOCK], axis=1, mode="promise_in_bounds"
                        )
                        for c in range(0, span, BLOCK)
                    ],
                    axis=1,
                )
                scores = jnp.where(same, raw * scale + bias, mask_fill)
                top = jnp.max(scores, axis=1, keepdims=True)
                weights = jnp.exp(scores - top)
                probs = weights * (1.0 / jnp.sum(weights, axis=1, keepdims=True))
                p_ref[2 * p + e, 0] = probs
                outs.append(dot(probs.astype(BF16), v2))
            ctx_ref[:, cols] = jnp.where(low_lane, outs[0], outs[1]).astype(BF16)
            return carry

        lax.fori_loop(0, pairs, one_pair, 0, unroll=True)

    return pl.pallas_call(
        body,
        grid_spec=pltpu.PrefetchScalarGridSpec(
            num_scalar_prefetch=1,
            grid=(blocks,),
            in_specs=[
                pl.BlockSpec((rows, model), lambda i, w: (0, 0)),
                pl.BlockSpec((3, model, width), lambda i, w: (0, 0, 0)),
                pl.BlockSpec((2, width), lambda i, w: (0, 0)),
                pl.BlockSpec(docs.shape, lambda i, w: (0, 0)),
                pl.BlockSpec((2, 1, BLOCK, rows), lambda i, w: (0, w[0], i, 0)),
                pl.BlockSpec(table.shape, lambda i, w: (0, 0, 0)),
            ],
            out_specs=[
                pl.BlockSpec((rows, 3 * width), lambda i, w: (0, 0)),
                pl.BlockSpec((BLOCK, width), lambda i, w: (i, 0)),
                pl.BlockSpec((heads, 1, BLOCK, span), lambda i, w: (0, i, 0, 0)),
            ],
        ),
        out_shape=[
            jax.ShapeDtypeStruct((rows, 3 * width), BF16),
            jax.ShapeDtypeStruct((rows, width), BF16),
            jax.ShapeDtypeStruct((heads, blocks, BLOCK, span), F32),
        ],
        cost_estimate=pl.CostEstimate(flops=ATTEND_FLOPS, transcendentals=0, bytes_accessed=1 << 23),
        name="attend",
    )(which, inputs, weight, bias, docs, buckets, table)


def attend_back(which, qkvs, grads, probs):
    rows, width = qkvs[0].shape[0], qkvs[0].shape[1] // 3
    heads, blocks, _, span = probs[0].shape
    pairs = heads // 2
    half = width // heads
    scale = 1.0 / math.sqrt(half)

    def body(qkv_a, qkv_b, g_a, g_b, p_a, p_b, d_a, d_b, s_a, s_b, acc_a, acc_b):
        block = pl.program_id(0)
        start = pl.multiple_of(jnp.clip(block - 1, 0, blocks - 3) * BLOCK, BLOCK)
        own_rows = pl.ds(pl.multiple_of(block * BLOCK, BLOCK), BLOCK)
        key_rows = pl.ds(start, span)
        low_lane = lax.broadcasted_iota(jnp.int32, (BLOCK, 2 * half), 1) < half

        @pl.when(block == 0)
        def _():
            acc_a[...] = jnp.zeros_like(acc_a)
            acc_b[...] = jnp.zeros_like(acc_b)

        for qkv_ref, g_ref, p_ref, d_ref, s_ref, sums in (
            (qkv_a, g_a, p_a, d_a, s_a, acc_a),
            (qkv_b, g_b, p_b, d_b, s_b, acc_b),
        ):

            def shifted(p, c):
                return pl.ds(pl.multiple_of(c * width + p * 2 * half, 2 * half), 2 * half)

            def one_pair(p, carry):
                cols = shifted(p, 0)
                q2 = qkv_ref[own_rows, cols]
                g2 = g_ref[:, cols]
                k2 = qkv_ref[key_rows, shifted(p, 1)]
                v2 = qkv_ref[key_rows, shifted(p, 2)]
                dqs = []
                dk = sums[0, key_rows, cols]
                dv = sums[1, key_rows, cols]
                for e in range(2):
                    mine = low_lane == (e == 0)
                    qm = jnp.where(mine, q2, jnp.zeros_like(q2))
                    gm = jnp.where(mine, g2, jnp.zeros_like(g2))
                    pr = p_ref[2 * p + e, 0]
                    gp = dot_nt(gm, v2)
                    gs = pr * (gp - jnp.sum(pr * gp, axis=1, keepdims=True))
                    s_ref[2 * p + e, 0] = gs
                    raw = (gs * scale).astype(BF16)
                    dqs.append(dot(raw, k2))
                    dk = dk + dot_tn(raw, qm)
                    dv = dv + dot_tn(pr.astype(BF16), gm)
                d_ref[own_rows, cols] = jnp.where(low_lane, dqs[0], dqs[1]).astype(BF16)
                sums[0, key_rows, cols] = dk
                sums[1, key_rows, cols] = dv
                return carry

            lax.fori_loop(0, pairs, one_pair, 0, unroll=True)

        @pl.when(block == blocks - 1)
        def _():
            for d_ref, sums in ((d_a, acc_a), (d_b, acc_b)):
                d_ref[:, width : 2 * width] = sums[0].astype(BF16)
                d_ref[:, 2 * width :] = sums[1].astype(BF16)

    whole = pl.BlockSpec((rows, 3 * width), lambda i: (0, 0))
    part = pl.BlockSpec((BLOCK, width), lambda i: (i, 0))
    prob = pl.BlockSpec((heads, 1, BLOCK, span), lambda i: (0, i, 0, 0))
    shape = jax.ShapeDtypeStruct((rows, 3 * width), BF16)
    score = jax.ShapeDtypeStruct(probs[0].shape, F32)
    return pl.pallas_call(
        body,
        grid=(blocks,),
        in_specs=[whole, whole, part, part, prob, prob],
        out_specs=[whole, whole, prob, prob],
        scratch_shapes=[
            pltpu.VMEM((2, rows, width), F32),
            pltpu.VMEM((2, rows, width), F32),
        ],
        out_shape=[shape, shape, score, score],
        input_output_aliases={4: 2, 5: 3},
        cost_estimate=pl.CostEstimate(
            flops=BACK_FLOPS, transcendentals=0, bytes_accessed=1 << 24
        ),
        name="attend_back",
    )(*qkvs, *grads, *probs)


def table_sums(which, scores, buckets):
    heads, blocks, _, span = scores[0].shape
    nb = NB
    rows = blocks * BLOCK
    group = 8
    codes = 2 * nb
    lanes = 2 * 2 * heads * group

    def body(which_ref, s_a, s_b, b_ref, tab_ref, acc_ref):
        block = pl.program_id(0)
        start = pl.multiple_of(jnp.clip(block - 1, 0, blocks - 3) * BLOCK, BLOCK)
        key_rows = pl.ds(start, span)

        @pl.when(block == 0)
        def _():
            acc_ref[...] = jnp.zeros_like(acc_ref)

        code_ids = lax.broadcasted_iota(jnp.int32, (nb, span), 0).astype(F32).astype(BF16)
        one, zero = jnp.ones((), BF16), jnp.zeros((), BF16)

        def one_side(r8):
            b0 = b_ref[0, 0, r8, key_rows].astype(F32)
            b1 = b_ref[1, 0, r8, key_rows].astype(F32)
            pieces = []
            for r in range(group):
                for b in (b0, b1):
                    row = jnp.broadcast_to(b[r : r + 1], (nb, span)).astype(BF16)
                    pieces.append(jnp.where(row == code_ids, one, zero))
            gg = jnp.concatenate(
                [ref[:, 0, r8, :].reshape(heads * group, span) for ref in (s_a, s_b)], axis=0
            )
            upper = gg.astype(BF16)
            lower = (gg - upper.astype(F32)).astype(BF16)
            return jnp.concatenate(pieces, axis=0), jnp.concatenate([upper, lower], axis=0)

        def two_groups(g, carry):
            sides = [
                one_side(pl.ds(pl.multiple_of((2 * g + k) * group, group), group))
                for k in range(2)
            ]
            onehot, both = (jnp.concatenate(parts, axis=1) for parts in zip(*sides))
            acc_ref[...] += dot_nt(onehot, both)
            return carry

        lax.fori_loop(0, BLOCK // group // 2, two_groups, 0)

        @pl.when(block == blocks - 1)
        def _():
            lane_row = lax.broadcasted_iota(jnp.int32, (codes, lanes), 1) % group
            total = jnp.zeros((codes, lanes), F32)
            for r in range(group):
                total = total + jnp.where(
                    lane_row == r, acc_ref[r * codes : (r + 1) * codes, :], 0.0
                )
            tab_ref[...] = total

    prob = pl.BlockSpec((heads, 1, BLOCK, span), lambda i, w: (0, i, 0, 0))
    return pl.pallas_call(
        body,
        grid_spec=pltpu.PrefetchScalarGridSpec(
            num_scalar_prefetch=1,
            grid=(blocks,),
            in_specs=[
                prob,
                prob,
                pl.BlockSpec((2, 1, BLOCK, rows), lambda i, w: (0, w[0], i, 0)),
            ],
            out_specs=pl.BlockSpec((codes, lanes), lambda i, w: (0, 0)),
            scratch_shapes=[pltpu.VMEM((group * codes, lanes), F32)],
        ),
        out_shape=jax.ShapeDtypeStruct((codes, lanes), F32),
        cost_estimate=NO_COST,
        name="table_sums",
    )(which, *scores, buckets)


def input_back(grads_a, grads_b, weight_a, weight_b, grad_sum, features, inputs):
    width = weight_a.shape[2]

    def body(g_a, g_b, w_a, w_b, sum_ref, f_ref, x_ref, in_ref, lay_ref, prod_ref, col_ref):
        total = sum_ref[...]
        for g_ref, w_ref in ((g_a, w_a), (g_b, w_b)):
            for c in range(3):
                total = total + dot_nt(g_ref[:, c * width : (c + 1) * width], w_ref[c])
        in_ref[...] = total
        lay_ref[...] = dot(f_ref[...], total.astype(BF16))
        prod_ref[...] = dot_tn(x_ref[...], g_a[...])
        col_ref[...] = jnp.sum(g_a[...].astype(F32), axis=0, keepdims=True)

    model = inputs.shape[1]
    return pl.pallas_call(
        body,
        out_shape=[
            jax.ShapeDtypeStruct(grad_sum.shape, F32),
            jax.ShapeDtypeStruct((features.shape[0], model), F32),
            jax.ShapeDtypeStruct((model, 3 * width), F32),
            jax.ShapeDtypeStruct((1, 3 * width), F32),
        ],
        cost_estimate=NO_COST,
        name="input_back",
    )(grads_a, grads_b, weight_a, weight_b, grad_sum, features, inputs)


def pair_back(sides, inputs, grads, product, columns):
    model = inputs.shape[1]
    wide = grads.shape[1]
    part = model // 4

    def body(side_ref, x_ref, g_ref, prod_ref, col_ref, *refs):
        outs, sum_ref, whole = refs[:4], refs[4], refs[5]
        whole[...] = (prod_ref[...] + dot_tn(x_ref[...], g_ref[...])).astype(BF16)
        for k, out_ref in enumerate(outs):
            side = side_ref[k // 2] if k % 2 == 0 else 1 - side_ref[k // 2]
            first = pl.multiple_of((k // 2) * 2 * part + side * part, 16)
            out_ref[...] = whole[pl.ds(first, part), :]
        sum_ref[...] = col_ref[...] + jnp.sum(g_ref[...].astype(F32), axis=0, keepdims=True)

    def full(value):
        return pl.BlockSpec(value.shape, lambda i, w: (0,) * value.ndim)

    operands = (inputs, grads, product, columns)
    outs = [jax.ShapeDtypeStruct((part, wide), BF16)] * 4
    outs.append(jax.ShapeDtypeStruct((1, wide), F32))
    return pl.pallas_call(
        body,
        grid_spec=pltpu.PrefetchScalarGridSpec(
            num_scalar_prefetch=1,
            grid=(1,),
            in_specs=[full(value) for value in operands],
            out_specs=[full(value) for value in outs],
            scratch_shapes=[pltpu.VMEM((model, wide), BF16)],
        ),
        out_shape=outs,
        cost_estimate=NO_COST,
        name="pair_back",
    )(sides, *operands)


def small_parts(turn, layout, stats, tables, columns, pre_a, pre_b, cut):
    rows, model = layout.shape
    width = model // 2
    tall = -(-(cut + 1) // 16) * 16
    used = cut + 2 + pre_a.shape[1] // model
    unit = 8 * lax.axis_size("dp")
    full_rows = -(-used // unit) * unit

    def body(turn_ref, lay_ref, *refs):
        stat_refs, refs = refs[:6], refs[6:]
        tab_ref, col_ref, a_ref, b_ref, own_ref, other_ref, low, high = refs
        lanes = tab_ref.shape[1] // 2
        heads = lanes // 16
        codes = tab_ref.shape[0]
        table = tab_ref[:, 0:lanes] + tab_ref[:, lanes : 2 * lanes]
        table = jnp.concatenate([table, jnp.zeros((codes, BLOCK - lanes), F32)], axis=1)
        for step in (1, 2, 4):
            table = table + pltpu.roll(table, BLOCK - step, 1)
        code = lax.broadcasted_iota(jnp.int32, (codes, BLOCK), 0)
        lane = lax.broadcasted_iota(jnp.int32, (codes, BLOCK), 1)

        def table_row(side, ref):
            for c in range(0, codes * heads, BLOCK):
                index = side * heads * 8 + (lane + c) % heads * 8
                value = jnp.take_along_axis(table, index, axis=1, mode="promise_in_bounds")
                value = jnp.where((lane + c) // heads == code, value, 0.0)
                ref[cut : cut + 1, c : c + BLOCK] = jnp.sum(value, axis=0, keepdims=True)

        low[...] = jnp.zeros_like(low)
        high[...] = jnp.zeros_like(high)
        low[0:cut, :] = lay_ref[0:cut, :]
        high[0 : rows - cut, :] = lay_ref[cut:rows, :]
        for k, ref in enumerate(stat_refs):
            high[rows - cut + k : rows - cut + k + 1, :] = ref[...].reshape(1, model)
        first = jnp.full(low.shape, turn_ref[0], jnp.int32) == 0
        own_ref[...] = jnp.zeros_like(own_ref)
        own_ref[0:tall, :] = jnp.where(first, low[...], high[...])
        table_row(0, own_ref)
        own_ref[cut + 1 : cut + 2, 0:width] = col_ref[:, 0:width]
        own_ref[cut + 1 : cut + 2, width:model] = col_ref[:, 2 * width : 3 * width]
        total = jnp.sum(a_ref[...].astype(F32), axis=0, keepdims=True) + jnp.sum(
            b_ref[...].astype(F32), axis=0, keepdims=True
        )
        for k in range(used - cut - 2):
            own_ref[cut + 2 + k : cut + 3 + k, :] = total[:, k * model : (k + 1) * model]
        low[...] = jnp.where(first, high[...], low[...])
        table_row(1, low)
        other_ref[...] = low[...].astype(BF16)

    def full(value):
        return pl.BlockSpec(value.shape, lambda i, w: (0,) * value.ndim)

    operands = (layout, *stats, tables, columns, pre_a, pre_b)
    outs = [
        jax.ShapeDtypeStruct((full_rows, model), F32),
        jax.ShapeDtypeStruct((tall, model), BF16),
    ]
    return pl.pallas_call(
        body,
        grid_spec=pltpu.PrefetchScalarGridSpec(
            num_scalar_prefetch=1,
            grid=(1,),
            in_specs=[full(value) for value in operands],
            out_specs=[full(value) for value in outs],
            scratch_shapes=[pltpu.VMEM((tall, model), F32)] * 2,
        ),
        out_shape=outs,
        cost_estimate=NO_COST,
        name="small_parts",
    )(turn, *operands)


def swap(value):
    size = lax.axis_size("tensor")
    return lax.ppermute(value, "tensor", [(i, (i + 1) % size) for i in range(size)])


def ring_bits(turned):
    size = lax.axis_size("dp")
    bits = [1 << k for k in range(size.bit_length() - 1)]
    return bits[1::-1] + bits[2:] if turned else bits


def ring_steps(bits):
    return [(True, bit) for bit in bits] + [(False, bit) for bit in reversed(bits)]


def side_of(bit):
    return (lax.axis_index("dp") >> (bit.bit_length() - 1)) & 1


def begin(step, value):
    scatter, bit = step
    if not scatter:
        return value, value
    side = side_of(bit)
    half = value.shape[0] // 2
    part = lambda where: lax.dynamic_slice_in_dim(
        value, where * half, half, 0, allow_negative_indices=False
    )
    return part(side), part(1 - side)


def finish(step, kept, send):
    scatter, bit = step
    size = lax.axis_size("dp")
    received = lax.ppermute(send, "dp", [(i, i ^ bit) for i in range(size)])
    if scatter:
        return kept + received
    low = side_of(bit) == 0
    return jnp.concatenate([jnp.where(low, kept, received), jnp.where(low, received, kept)])


def ring_run(steps, value):
    for step in steps:
        value = finish(step, *begin(step, value))
    return value


def update(clip_factor, grads, state):
    share = state[0].shape[1] // BLOCK
    start = lax.axis_index("dp").astype(jnp.int32) * share
    wide, wide_info, thin, thin_info = [], [], [], []
    base = 0
    row = 0
    for grad in grads:
        rows = grad.size // BLOCK
        if grad.ndim == 2 and grad.shape[1] % BLOCK == 0 and grad.shape[0] > 16:
            lanes = grad.shape[1] // BLOCK
            grad = jnp.pad(grad, ((0, -grad.shape[0] % 8), (0, 0)))
            slab = min(grad.shape[0], -(-(share // lanes + 18) // 8) * 8)
            wide.append(grad)
            wide_info.append((base, lanes, grad.shape[0], slab))
        else:
            thin.append(jnp.pad(grad.reshape(rows, BLOCK), ((0, -rows % 8), (0, 0))))
            thin_info.append((base, row, rows))
            row += rows + -rows % 8
        base += rows
    thin_all = jnp.concatenate(thin)
    margin = -(-max(info[1] * info[3] for info in wide_info) // 8) * 8 + 8

    def slab_start(first, info):
        base, lanes, rows, slab = info
        wanted = jnp.maximum(first - base, 0) // (lanes * 8) * 8
        return pl.multiple_of(jnp.minimum(wanted, rows - slab), 8)

    def body(start_ref, clip_ref, *refs):
        wide_refs = refs[: len(wide)]
        thin_ref = refs[len(wide)]
        master, one, two, ema = refs[len(wide) + 1 : len(wide) + 5]
        new_master, new_one, new_two, new_ema, copy, own = refs[len(wide) + 5 :]
        first = start_ref[0]
        own[margin : margin + share, :] = jnp.zeros((share, BLOCK), F32)
        for ref, info in zip(wide_refs, wide_info):
            base, lanes, rows, slab = info

            @pl.when((first < base + rows * lanes) & (first + share > base))
            def _():
                place = margin + base + slab_start(first, info) * lanes - first
                for k in range(lanes):
                    own[pl.ds(place + k, slab, stride=lanes), :] = ref[
                        :, k * BLOCK : (k + 1) * BLOCK
                    ]

        for base, row, rows in thin_info:

            @pl.when((first < base + rows) & (first + share > base))
            def _():
                own[pl.ds(margin + base - first, rows), :] = thin_ref[row : row + rows, :]

        scale = clip_ref[0]

        def advance(row, rows):
            many = -(-rows // 8) * 8
            grad = own[pl.ds(pl.multiple_of(margin + row, 8), many), :].reshape(1, many * BLOCK)
            grad = grad[:, : rows * BLOCK] * scale
            place = (slice(None), pl.ds(pl.multiple_of(row * BLOCK, 8 * BLOCK), rows * BLOCK))
            moment = beta_one * one[place] + (1.0 - beta_one) * grad
            second = beta_two * two[place] + (1.0 - beta_two) * grad * grad
            new_one[place] = moment
            new_two[place] = second
            step_size = (
                moment
                / (1.0 - beta_one**STEP)
                / (jnp.sqrt(second / (1.0 - beta_two**STEP)) + adam_eps)
            )
            weight = master[place]
            weight = weight - learn_rate * (step_size + decay_rate * weight)
            new_master[place] = weight
            new_ema[place] = average_rate * ema[place] + (1.0 - average_rate) * weight
            copy[place] = weight.astype(BF16)

        def many_rows(number, carry):
            advance(number * CHUNK, CHUNK)
            return carry

        lax.fori_loop(0, share // CHUNK, many_rows, 0)
        if share % CHUNK:
            advance(share // CHUNK * CHUNK, share % CHUNK)

    plain = pl.BlockSpec((1, share * BLOCK), lambda i, s: (0, 0))
    specs = [pl.BlockSpec(memory_space=pltpu.SMEM)]
    for grad, info in zip(wide, wide_info):
        specs.append(
            pl.BlockSpec(
                (pl.Element(info[3]), pl.Element(grad.shape[1])),
                lambda i, s, info=info: (slab_start(s[0], info), 0),
            )
        )
    specs.append(pl.BlockSpec(thin_all.shape, lambda i, s: (0, 0)))
    flat = jax.ShapeDtypeStruct((1, share * BLOCK), F32)
    return pl.pallas_call(
        body,
        grid_spec=pltpu.PrefetchScalarGridSpec(
            num_scalar_prefetch=1,
            grid=(1,),
            in_specs=specs + [plain] * 4,
            out_specs=[plain] * 5,
            scratch_shapes=[pltpu.VMEM((2 * margin + share + 8, BLOCK), F32)],
        ),
        out_shape=[flat] * 4 + [jax.ShapeDtypeStruct((1, share * BLOCK), BF16)],
        name="update",
    )(
        start.reshape(1),
        clip_factor.reshape(1),
        *wide,
        thin_all,
        *state,
    )


def per_device(
    hidden_in,
    cotangent,
    box_coords,
    doc_ids,
    buckets,
    layout_weight,
    norm_gains,
    norm_shifts,
    branch_biases,
    qkv_weight,
    query_value_bias,
    output_weight,
    ffn_in_weight,
    ffn_in_bias,
    ffn_out_weight,
    relative_table,
    master_flat,
    moment_one,
    moment_two,
    ema_flat,
):
    turn = lax.axis_index("tensor")
    window = turn.astype(jnp.int32).reshape(1)
    gains = norm_gains.astype(F32)
    norm_offsets = norm_shifts.astype(F32)
    biases = branch_biases.astype(F32)

    table_own = jnp.transpose(relative_table, (2, 0, 1))
    qkv_other = swap(qkv_weight)
    qv_bias_other = swap(query_value_bias)
    table_other = swap(table_own)
    output_other = swap(output_weight)
    ffn_in_other = swap(ffn_in_weight)
    ffn_bias_other = swap(ffn_in_bias)
    ffn_out_other = swap(ffn_out_weight)

    features = box_features(box_coords).astype(BF16)
    embedded = hidden_in.astype(F32) + dot_tn(features, layout_weight)
    inputs = embedded.astype(BF16)
    inputs_swap = swap(inputs)

    qkv_a, context_a, probs_a = attend(
        window, inputs, qkv_weight, query_value_bias, doc_ids, buckets, table_own
    )
    qkv_b, context_b, probs_b = attend(
        window, inputs, qkv_other, qv_bias_other, doc_ids, buckets, table_other
    )
    context_swap = swap(context_b)
    attn_out = dot(context_a, output_weight) + dot(context_b, output_other) + biases[0]
    normed_one, inv_std_one = normalize(embedded + attn_out)
    mid_norm = normed_one * gains[0] + norm_offsets[0]
    mid_low = mid_norm.astype(BF16)
    mid_swap = swap(mid_low)

    def expand(weight, bias):
        pre = dot(mid_low, weight) + bias.astype(F32)
        share = 0.5 + 0.5 * lax.erf(pre * math.sqrt(0.5))
        slope = share + pre * (math.sqrt(0.5 / math.pi) * jnp.exp(-0.5 * pre * pre))
        return (pre * share).astype(BF16), slope

    hidden_a, slope_a = expand(ffn_in_weight, ffn_in_bias)
    hidden_b, slope_b = expand(ffn_in_other, ffn_bias_other)
    hidden_swap = swap(hidden_b)
    branch = dot(hidden_a, ffn_out_weight) + dot(hidden_b, ffn_out_other) + biases[1]
    normed_two, inv_std_two = normalize(mid_norm + branch)
    hidden_out = (normed_two * gains[1] + norm_offsets[1]).astype(BF16)
    grad_out = cotangent.astype(F32)
    gain_two = jnp.sum(grad_out * normed_two, axis=0)
    shift_two = jnp.sum(grad_out, axis=0)
    grad_sum_two = norm_back(grad_out, normed_two, inv_std_two, gains[1])
    bias_two = jnp.sum(grad_sum_two, axis=0)
    grad_branch = grad_sum_two.astype(BF16)
    grad_branch_swap = swap(grad_branch)

    grad_pre_b = (slope_b * dot_nt(grad_branch, ffn_out_other)).astype(BF16)
    grad_pre_swap = swap(grad_pre_b)
    grad_pre_a = (slope_a * dot_nt(grad_branch, ffn_out_weight)).astype(BF16)
    ffn_out_low = (
        dot_tn(hidden_a, grad_branch) + dot_tn(hidden_swap, grad_branch_swap)
    ).astype(BF16)
    ffn_in_low = (dot_tn(mid_low, grad_pre_a) + dot_tn(mid_swap, grad_pre_swap)).astype(BF16)
    grad_mid = (
        grad_sum_two + dot_nt(grad_pre_a, ffn_in_weight) + dot_nt(grad_pre_b, ffn_in_other)
    )
    gain_one = jnp.sum(grad_mid * normed_one, axis=0)
    shift_one = jnp.sum(grad_mid, axis=0)
    grad_sum_one = norm_back(grad_mid, normed_one, inv_std_one, gains[0])
    bias_one = jnp.sum(grad_sum_one, axis=0)
    grad_attn = grad_sum_one.astype(BF16)
    grad_attn_swap = swap(grad_attn)
    output_grad = dot_tn(context_a, grad_attn) + dot_tn(context_swap, grad_attn_swap)
    grad_context_a = dot_nt(grad_attn, output_weight).astype(BF16)
    grad_context_b = dot_nt(grad_attn, output_other).astype(BF16)

    barrier = lax.optimization_barrier
    steps_a, steps_b = ring_steps(ring_bits(False)), ring_steps(ring_bits(True))
    out_keep, out_send = begin(
        steps_a[0], jnp.concatenate([ffn_out_low, output_grad.astype(BF16)])
    )
    in_keep, in_send = begin(steps_b[0], ffn_in_low)
    (grad_context_a, grad_context_b), out_send, in_send = barrier(
        ((grad_context_a, grad_context_b), out_send, in_send)
    )
    grads_a, grads_b, scores_a, scores_b = attend_back(
        window, (qkv_a, qkv_b), (grad_context_a, grad_context_b), (probs_a, probs_b)
    )
    grads_swap = swap(grads_b)
    width = qkv_weight.shape[2]
    early = input_back(grads_a, grads_b, qkv_weight, qkv_other, grad_sum_one, features, inputs)
    early, out_keep, in_keep = barrier((early, out_keep, in_keep))
    input_grad, layout_part, product, columns = early
    out_sum = finish(steps_a[0], out_keep, out_send)
    in_sum = finish(steps_b[0], in_keep, in_send)

    out_keep, out_send = begin(steps_a[1], out_sum)
    in_keep, in_send = begin(steps_b[1], in_sum)
    product, scores_a, scores_b, out_send, in_send = barrier(
        (product, scores_a, scores_b, out_send, in_send)
    )
    sides = jnp.stack([side_of(steps[0][1]) for steps in (steps_a, steps_b)])
    late = pair_back(sides.astype(jnp.int32), inputs_swap, grads_swap, product, columns)
    tables = table_sums(window, (scores_a, scores_b), buckets)
    late, tables, out_keep, in_keep = barrier((late, tables, out_keep, in_keep))
    a_keep, a_send, b_keep, b_send, qv_sums = late
    out_sum = finish(steps_a[1], out_keep, out_send)
    in_sum = finish(steps_b[1], in_keep, in_send)

    plans = {
        "out": (0, steps_a[2:]),
        "in": (0, steps_b[2:]),
        "a": (0, steps_a),
        "b": (0, steps_b),
        "c": (1, steps_b),
    }
    sums = {"out": out_sum, "in": in_sum}
    last = len(steps_a) - 1
    for number in range(last + 2):
        if number == 1:
            other = swap(other_shared).astype(F32)
            pack_c = own_shared + jnp.pad(
                other, ((0, own_shared.shape[0] - other.shape[0]), (0, 0))
            )
            pack_c = pack_c.astype(BF16)
            sums["c"] = pack_c
        opened = {
            name: begin(steps[number - first], sums[name])
            for name, (first, steps) in plans.items()
            if first <= number < first + len(steps) and name in sums
        }
        if number == 0:
            opened["a"], opened["b"] = (a_keep, a_send), (b_keep, b_send)
        sends = {name: send for name, (_, send) in opened.items()}
        if number == 0:
            sends, tables, qv_sums, layout_part = barrier((sends, tables, qv_sums, layout_part))
            cut = (layout_part.shape[0] + 6) // lax.axis_size("tensor")
            own_shared, other_shared = small_parts(
                window,
                layout_part,
                (gain_one, gain_two, shift_one, shift_two, bias_one, bias_two),
                tables,
                qv_sums,
                grad_pre_a,
                grad_pre_swap,
                cut,
            )
        elif number == last - 1:
            small_send = sends.pop("c")
            sends = barrier(sends)
            sends["c"], sums["out"], sums["in"] = barrier(
                (small_send, sums["out"], sums["in"])
            )
        elif number == last + 1:
            sends, sums["a"], sums["b"] = barrier((sends, sums["a"], sums["b"]))
        else:
            sends = barrier(sends)
        for name, (kept, _) in opened.items():
            first, steps = plans[name]
            sums[name] = finish(steps[number - first], kept, sends[name])
    out_all, ffn_in_low, pack_a, pack_b, pack_c = (sums[name] for name in ("out", "in", "a", "b", "c"))

    square = sum(
        jnp.sum(jnp.square(member.astype(F32)))
        for member in (out_all, ffn_in_low, pack_a, pack_b, pack_c)
    )
    ffn_out_grad = out_all[: ffn_out_low.shape[0]].astype(F32)
    output_grad = out_all[ffn_out_low.shape[0] :].astype(F32)
    ffn_in_grad = ffn_in_low.astype(F32)
    qkv_grad = jnp.stack(
        [
            jnp.concatenate([part[:, c * width : (c + 1) * width] for part in (pack_a, pack_b)])
            for c in range(3)
        ]
    ).astype(F32)
    own_low = pack_c[:cut]
    small = pack_c[cut : cut + 4].astype(F32)
    table_grad = small[0, : relative_table.size].reshape(relative_table.shape)
    qv_bias_grad = small[1].reshape(query_value_bias.shape)
    ffn_bias_grad = small[2:4].reshape(-1)
    first_turn = turn == 0
    other_low = swap(own_low)
    shared = jnp.where(
        first_turn,
        jnp.concatenate([own_low, other_low]),
        jnp.concatenate([other_low, own_low]),
    ).astype(F32)
    layout_grad = shared[: layout_part.shape[0]]
    gains_grad, shifts_grad, biases_grad = jnp.split(shared[layout_part.shape[0] :], 3)

    grad_norm = jnp.sqrt(square + swap(square))
    clip_factor = clip_limit / jnp.maximum(grad_norm, clip_limit)
    updated = update(
        clip_factor,
        (
            ffn_in_grad,
            ffn_bias_grad,
            ffn_out_grad,
            qkv_grad.reshape(-1, width),
            qv_bias_grad,
            output_grad,
            table_grad,
            own_low.astype(F32),
        ),
        (master_flat, moment_one, moment_two, ema_flat),
    )
    return (
        hidden_out,
        input_grad,
        layout_grad,
        gains_grad,
        shifts_grad,
        biases_grad,
        qkv_grad,
        qv_bias_grad,
        output_grad,
        ffn_in_grad,
        ffn_bias_grad,
        ffn_out_grad,
        table_grad,
        grad_norm,
    ) + tuple(updated)


def solution(mesh):
    return jax.shard_map(
        per_device,
        mesh=mesh,
        in_specs=(
            P(("dp", "tensor"), None),
            P(("dp", "tensor"), None),
            P(None, ("dp", "tensor")),
            P("dp", None),
            P(None, "dp", None, None),
            P(),
            P(),
            P(),
            P(),
            P(None, None, "tensor"),
            P(None, "tensor"),
            P("tensor", None),
            P(None, "tensor"),
            P("tensor"),
            P("tensor", None),
            P(None, None, "tensor"),
            P("tensor", "dp"),
            P("tensor", "dp"),
            P("tensor", "dp"),
            P("tensor", "dp"),
        ),
        out_specs=(
            P(("dp", "tensor"), None),
            P(("dp", "tensor"), None),
            P(),
            P(),
            P(),
            P(),
            P(None, None, "tensor"),
            P(None, "tensor"),
            P("tensor", None),
            P(None, "tensor"),
            P("tensor"),
            P("tensor", None),
            P(None, None, "tensor"),
            P(),
            P("tensor", "dp"),
            P("tensor", "dp"),
            P("tensor", "dp"),
            P("tensor", "dp"),
            P("tensor", "dp"),
        ),
        check_vma=False,
    )
```

```python
import math

import jax
import jax.numpy as jnp
from jax import lax
from jax.experimental import pallas as pl
from jax.experimental.pallas import tpu as pltpu
from jax.sharding import PartitionSpec as P

NB = 32
FEAT = 256
STEP = 10
BLOCK = 128
CHUNK = 32
ATTEND_FLOPS = 1 << 33
BACK_FLOPS = 1 << 35
NO_COST = pl.CostEstimate(flops=1, transcendentals=0, bytes_accessed=1)


norm_eps = 1e-05
learn_rate = 0.02
beta_one = 0.9
beta_two = 0.999
adam_eps = 1e-08
decay_rate = 0.01
average_rate = 0.5
clip_limit = 1.0
mask_fill = -1e30

F32 = jnp.float32
BF16 = jnp.bfloat16
NT = (((1,), (1,)), ((), ()))
TN = (((0,), (0,)), ((), ()))


def dot(left, right):
    return jnp.dot(left, right, preferred_element_type=F32)


def dot_nt(left, right):
    return lax.dot_general(left, right, NT, preferred_element_type=F32)


def dot_tn(left, right):
    return lax.dot_general(left, right, TN, preferred_element_type=F32)


def box_features(coords):
    count = FEAT // 8
    freqs = jnp.exp(-math.log(10000.0) * jnp.arange(count, dtype=F32) / count)
    angles = coords.astype(F32)[:, None, :] * freqs[None, :, None]
    waves = jnp.stack([jnp.sin(angles), jnp.cos(angles)], axis=1)
    return waves.reshape(FEAT, coords.shape[1])


def normalize(value):
    centre = value - jnp.mean(value, axis=-1, keepdims=True)
    inv_std = lax.rsqrt(jnp.mean(centre * centre, axis=-1, keepdims=True) + norm_eps)
    return (centre * inv_std, inv_std)


def norm_back(grad_out, normed, inv_std, gain):
    scaled = grad_out * gain
    return inv_std * (
        scaled
        - jnp.mean(scaled, axis=-1, keepdims=True)
        - normed * jnp.mean(scaled * normed, axis=-1, keepdims=True)
    )


def attend(which, inputs, weight, bias, docs, buckets, table):
    rows, model = inputs.shape
    width = weight.shape[2]
    heads, _, nb = table.shape
    pairs = heads // 2
    half = width // heads
    span = 3 * BLOCK
    blocks = rows // BLOCK
    scale = 1.0 / math.sqrt(half)
    def body(
        which_ref, x_ref, w_ref, bias_ref, doc_ref, b_ref, t_ref, qkv_ref, ctx_ref, p_ref
    ):
        block = pl.program_id(0)

        @pl.when(block == 0)
        def _():
            for c in range(3):
                made = dot(x_ref[...], w_ref[c])
                if c != 1:
                    made = made + bias_ref[c // 2 : c // 2 + 1, :].astype(F32)
                qkv_ref[:, c * width : (c + 1) * width] = made.astype(BF16)

        start = pl.multiple_of(jnp.clip(block - 1, 0, blocks - 3) * BLOCK, BLOCK)
        own_rows = pl.ds(pl.multiple_of(block * BLOCK, BLOCK), BLOCK)
        key_rows = pl.ds(start, span)
        windows = docs.shape[0]

        def docs_at(lanes, count):
            here = doc_ref[:, lanes].astype(F32)
            mine = lax.broadcasted_iota(jnp.int32, (windows, count), 0) == which_ref[0]
            return jnp.sum(jnp.where(mine, here, 0.0), axis=0, keepdims=True)

        diagonal = lax.broadcasted_iota(jnp.int32, (BLOCK, BLOCK), 0) == (
            lax.broadcasted_iota(jnp.int32, (BLOCK, BLOCK), 1)
        )
        docs_here = jnp.broadcast_to(docs_at(own_rows, BLOCK), (BLOCK, BLOCK))
        column = jnp.sum(jnp.where(diagonal, docs_here, 0.0), axis=1, keepdims=True)
        same = column == docs_at(key_rows, span)
        first = b_ref[0, 0, :, key_rows]
        second = b_ref[1, 0, :, key_rows]
        low_lane = lax.broadcasted_iota(jnp.int32, (BLOCK, 2 * half), 1) < half

        def shifted(p, c):
            return pl.ds(pl.multiple_of(c * width + p * 2 * half, 2 * half), 2 * half)

        def one_pair(p, carry):
            cols = shifted(p, 0)
            q2 = qkv_ref[own_rows, cols]
            k2 = qkv_ref[key_rows, shifted(p, 1)]
            v2 = qkv_ref[key_rows, shifted(p, 2)]
            outs = []
            for e in range(2):
                qm = jnp.where(low_lane == (e == 0), q2, jnp.zeros_like(q2))
                raw = dot_nt(qm, k2)
                rows_xy = jnp.concatenate(
                    [t_ref[2 * p + e].astype(F32), jnp.zeros((2, BLOCK - nb), F32)], axis=1
                )
                row_x = jnp.broadcast_to(rows_xy[0:1], (BLOCK, BLOCK))
                row_y = jnp.broadcast_to(rows_xy[1:2], (BLOCK, BLOCK))
                bias = jnp.concatenate(
                    [
                        jnp.take_along_axis(
                            row_x, first[:, c : c + BLOCK], axis=1, mode="promise_in_bounds"
                        )
                        + jnp.take_along_axis(
                            row_y, second[:, c : c + BLOCK], axis=1, mode="promise_in_bounds"
                        )
                        for c in range(0, span, BLOCK)
                    ],
                    axis=1,
                )
                scores = jnp.where(same, raw * scale + bias, mask_fill)
                top = jnp.max(scores, axis=1, keepdims=True)
                weights = jnp.exp(scores - top)
                probs = weights * (1.0 / jnp.sum(weights, axis=1, keepdims=True))
                p_ref[2 * p + e, 0] = probs
                outs.append(dot(probs.astype(BF16), v2))
            ctx_ref[:, cols] = jnp.where(low_lane, outs[0], outs[1]).astype(BF16)
            return carry

        lax.fori_loop(0, pairs, one_pair, 0, unroll=True)

    return pl.pallas_call(
        body,
        grid_spec=pltpu.PrefetchScalarGridSpec(
            num_scalar_prefetch=1,
            grid=(blocks,),
            in_specs=[
                pl.BlockSpec((rows, model), lambda i, w: (0, 0)),
                pl.BlockSpec((3, model, width), lambda i, w: (0, 0, 0)),
                pl.BlockSpec((2, width), lambda i, w: (0, 0)),
                pl.BlockSpec(docs.shape, lambda i, w: (0, 0)),
                pl.BlockSpec((2, 1, BLOCK, rows), lambda i, w: (0, w[0], i, 0)),
                pl.BlockSpec(table.shape, lambda i, w: (0, 0, 0)),
            ],
            out_specs=[
                pl.BlockSpec((rows, 3 * width), lambda i, w: (0, 0)),
                pl.BlockSpec((BLOCK, width), lambda i, w: (i, 0)),
                pl.BlockSpec((heads, 1, BLOCK, span), lambda i, w: (0, i, 0, 0)),
            ],
        ),
        out_shape=[
            jax.ShapeDtypeStruct((rows, 3 * width), BF16),
            jax.ShapeDtypeStruct((rows, width), BF16),
            jax.ShapeDtypeStruct((heads, blocks, BLOCK, span), F32),
        ],
        cost_estimate=pl.CostEstimate(flops=ATTEND_FLOPS, transcendentals=0, bytes_accessed=1 << 23),
        name="attend",
    )(which, inputs, weight, bias, docs, buckets, table)


def attend_back(which, qkvs, grads, probs):
    rows, width = qkvs[0].shape[0], qkvs[0].shape[1] // 3
    heads, blocks, _, span = probs[0].shape
    pairs = heads // 2
    half = width // heads
    scale = 1.0 / math.sqrt(half)

    def body(qkv_a, qkv_b, g_a, g_b, p_a, p_b, d_a, d_b, s_a, s_b, acc_a, acc_b):
        block = pl.program_id(0)
        start = pl.multiple_of(jnp.clip(block - 1, 0, blocks - 3) * BLOCK, BLOCK)
        own_rows = pl.ds(pl.multiple_of(block * BLOCK, BLOCK), BLOCK)
        key_rows = pl.ds(start, span)
        low_lane = lax.broadcasted_iota(jnp.int32, (BLOCK, 2 * half), 1) < half

        @pl.when(block == 0)
        def _():
            acc_a[...] = jnp.zeros_like(acc_a)
            acc_b[...] = jnp.zeros_like(acc_b)

        for qkv_ref, g_ref, p_ref, d_ref, s_ref, sums in (
            (qkv_a, g_a, p_a, d_a, s_a, acc_a),
            (qkv_b, g_b, p_b, d_b, s_b, acc_b),
        ):

            def shifted(p, c):
                return pl.ds(pl.multiple_of(c * width + p * 2 * half, 2 * half), 2 * half)

            def one_pair(p, carry):
                cols = shifted(p, 0)
                q2 = qkv_ref[own_rows, cols]
                g2 = g_ref[:, cols]
                k2 = qkv_ref[key_rows, shifted(p, 1)]
                v2 = qkv_ref[key_rows, shifted(p, 2)]
                dqs = []
                dk = sums[0, key_rows, cols]
                dv = sums[1, key_rows, cols]
                for e in range(2):
                    mine = low_lane == (e == 0)
                    qm = jnp.where(mine, q2, jnp.zeros_like(q2))
                    gm = jnp.where(mine, g2, jnp.zeros_like(g2))
                    pr = p_ref[2 * p + e, 0]
                    gp = dot_nt(gm, v2)
                    gs = pr * (gp - jnp.sum(pr * gp, axis=1, keepdims=True))
                    s_ref[2 * p + e, 0] = gs
                    raw = (gs * scale).astype(BF16)
                    dqs.append(dot(raw, k2))
                    dk = dk + dot_tn(raw, qm)
                    dv = dv + dot_tn(pr.astype(BF16), gm)
                d_ref[own_rows, cols] = jnp.where(low_lane, dqs[0], dqs[1]).astype(BF16)
                sums[0, key_rows, cols] = dk
                sums[1, key_rows, cols] = dv
                return carry

            lax.fori_loop(0, pairs, one_pair, 0, unroll=True)

        @pl.when(block == blocks - 1)
        def _():
            for d_ref, sums in ((d_a, acc_a), (d_b, acc_b)):
                d_ref[:, width : 2 * width] = sums[0].astype(BF16)
                d_ref[:, 2 * width :] = sums[1].astype(BF16)

    whole = pl.BlockSpec((rows, 3 * width), lambda i: (0, 0))
    part = pl.BlockSpec((BLOCK, width), lambda i: (i, 0))
    prob = pl.BlockSpec((heads, 1, BLOCK, span), lambda i: (0, i, 0, 0))
    shape = jax.ShapeDtypeStruct((rows, 3 * width), BF16)
    score = jax.ShapeDtypeStruct(probs[0].shape, F32)
    return pl.pallas_call(
        body,
        grid=(blocks,),
        in_specs=[whole, whole, part, part, prob, prob],
        out_specs=[whole, whole, prob, prob],
        scratch_shapes=[
            pltpu.VMEM((2, rows, width), F32),
            pltpu.VMEM((2, rows, width), F32),
        ],
        out_shape=[shape, shape, score, score],
        input_output_aliases={4: 2, 5: 3},
        cost_estimate=pl.CostEstimate(
            flops=BACK_FLOPS, transcendentals=0, bytes_accessed=1 << 24
        ),
        name="attend_back",
    )(*qkvs, *grads, *probs)


def table_sums(which, scores, buckets):
    heads, blocks, _, span = scores[0].shape
    nb = NB
    rows = blocks * BLOCK
    group = 8
    codes = 2 * nb
    lanes = 2 * 2 * heads * group

    def body(which_ref, s_a, s_b, b_ref, tab_ref, acc_ref):
        block = pl.program_id(0)
        start = pl.multiple_of(jnp.clip(block - 1, 0, blocks - 3) * BLOCK, BLOCK)
        key_rows = pl.ds(start, span)

        @pl.when(block == 0)
        def _():
            acc_ref[...] = jnp.zeros_like(acc_ref)

        code_ids = lax.broadcasted_iota(jnp.int32, (nb, span), 0).astype(F32).astype(BF16)
        one, zero = jnp.ones((), BF16), jnp.zeros((), BF16)

        def one_side(r8):
            b0 = b_ref[0, 0, r8, key_rows].astype(F32)
            b1 = b_ref[1, 0, r8, key_rows].astype(F32)
            pieces = []
            for r in range(group):
                for b in (b0, b1):
                    row = jnp.broadcast_to(b[r : r + 1], (nb, span)).astype(BF16)
                    pieces.append(jnp.where(row == code_ids, one, zero))
            gg = jnp.concatenate(
                [ref[:, 0, r8, :].reshape(heads * group, span) for ref in (s_a, s_b)], axis=0
            )
            upper = gg.astype(BF16)
            lower = (gg - upper.astype(F32)).astype(BF16)
            return jnp.concatenate(pieces, axis=0), jnp.concatenate([upper, lower], axis=0)

        def two_groups(g, carry):
            sides = [
                one_side(pl.ds(pl.multiple_of((2 * g + k) * group, group), group))
                for k in range(2)
            ]
            onehot, both = (jnp.concatenate(parts, axis=1) for parts in zip(*sides))
            acc_ref[...] += dot_nt(onehot, both)
            return carry

        lax.fori_loop(0, BLOCK // group // 2, two_groups, 0)

        @pl.when(block == blocks - 1)
        def _():
            lane_row = lax.broadcasted_iota(jnp.int32, (codes, lanes), 1) % group
            total = jnp.zeros((codes, lanes), F32)
            for r in range(group):
                total = total + jnp.where(
                    lane_row == r, acc_ref[r * codes : (r + 1) * codes, :], 0.0
                )
            tab_ref[...] = total

    prob = pl.BlockSpec((heads, 1, BLOCK, span), lambda i, w: (0, i, 0, 0))
    return pl.pallas_call(
        body,
        grid_spec=pltpu.PrefetchScalarGridSpec(
            num_scalar_prefetch=1,
            grid=(blocks,),
            in_specs=[
                prob,
                prob,
                pl.BlockSpec((2, 1, BLOCK, rows), lambda i, w: (0, w[0], i, 0)),
            ],
            out_specs=pl.BlockSpec((codes, lanes), lambda i, w: (0, 0)),
            scratch_shapes=[pltpu.VMEM((group * codes, lanes), F32)],
        ),
        out_shape=jax.ShapeDtypeStruct((codes, lanes), F32),
        cost_estimate=NO_COST,
        name="table_sums",
    )(which, *scores, buckets)


def input_back(grads_a, grads_b, weight_a, weight_b, grad_sum, features, inputs):
    width = weight_a.shape[2]

    def body(g_a, g_b, w_a, w_b, sum_ref, f_ref, x_ref, in_ref, lay_ref, prod_ref, col_ref):
        total = sum_ref[...]
        for g_ref, w_ref in ((g_a, w_a), (g_b, w_b)):
            for c in range(3):
                total = total + dot_nt(g_ref[:, c * width : (c + 1) * width], w_ref[c])
        in_ref[...] = total
        lay_ref[...] = dot(f_ref[...], total.astype(BF16))
        prod_ref[...] = dot_tn(x_ref[...], g_a[...])
        col_ref[...] = jnp.sum(g_a[...].astype(F32), axis=0, keepdims=True)

    model = inputs.shape[1]
    return pl.pallas_call(
        body,
        out_shape=[
            jax.ShapeDtypeStruct(grad_sum.shape, F32),
            jax.ShapeDtypeStruct((features.shape[0], model), F32),
            jax.ShapeDtypeStruct((model, 3 * width), F32),
            jax.ShapeDtypeStruct((1, 3 * width), F32),
        ],
        cost_estimate=NO_COST,
        name="input_back",
    )(grads_a, grads_b, weight_a, weight_b, grad_sum, features, inputs)


def pair_back(sides, inputs, grads, product, columns):
    model = inputs.shape[1]
    wide = grads.shape[1]
    part = model // 4

    def body(side_ref, x_ref, g_ref, prod_ref, col_ref, *refs):
        outs, sum_ref, whole = refs[:4], refs[4], refs[5]
        whole[...] = (prod_ref[...] + dot_tn(x_ref[...], g_ref[...])).astype(BF16)
        for k, out_ref in enumerate(outs):
            side = side_ref[k // 2] if k % 2 == 0 else 1 - side_ref[k // 2]
            first = pl.multiple_of((k // 2) * 2 * part + side * part, 16)
            out_ref[...] = whole[pl.ds(first, part), :]
        sum_ref[...] = col_ref[...] + jnp.sum(g_ref[...].astype(F32), axis=0, keepdims=True)

    def full(value):
        return pl.BlockSpec(value.shape, lambda i, w: (0,) * value.ndim)

    operands = (inputs, grads, product, columns)
    outs = [jax.ShapeDtypeStruct((part, wide), BF16)] * 4
    outs.append(jax.ShapeDtypeStruct((1, wide), F32))
    return pl.pallas_call(
        body,
        grid_spec=pltpu.PrefetchScalarGridSpec(
            num_scalar_prefetch=1,
            grid=(1,),
            in_specs=[full(value) for value in operands],
            out_specs=[full(value) for value in outs],
            scratch_shapes=[pltpu.VMEM((model, wide), BF16)],
        ),
        out_shape=outs,
        cost_estimate=NO_COST,
        name="pair_back",
    )(sides, *operands)


def small_parts(turn, layout, stats, tables, columns, pre_a, pre_b, cut):
    rows, model = layout.shape
    width = model // 2
    tall = -(-(cut + 1) // 16) * 16
    used = cut + 2 + pre_a.shape[1] // model
    unit = 8 * lax.axis_size("dp")
    full_rows = -(-used // unit) * unit

    def body(turn_ref, lay_ref, *refs):
        stat_refs, refs = refs[:6], refs[6:]
        tab_ref, col_ref, a_ref, b_ref, own_ref, other_ref, low, high = refs
        lanes = tab_ref.shape[1] // 2
        heads = lanes // 16
        codes = tab_ref.shape[0]
        table = tab_ref[:, 0:lanes] + tab_ref[:, lanes : 2 * lanes]
        table = jnp.concatenate([table, jnp.zeros((codes, BLOCK - lanes), F32)], axis=1)
        for step in (1, 2, 4):
            table = table + pltpu.roll(table, BLOCK - step, 1)
        code = lax.broadcasted_iota(jnp.int32, (codes, BLOCK), 0)
        lane = lax.broadcasted_iota(jnp.int32, (codes, BLOCK), 1)

        def table_row(side, ref):
            for c in range(0, codes * heads, BLOCK):
                index = side * heads * 8 + (lane + c) % heads * 8
                value = jnp.take_along_axis(table, index, axis=1, mode="promise_in_bounds")
                value = jnp.where((lane + c) // heads == code, value, 0.0)
                ref[cut : cut + 1, c : c + BLOCK] = jnp.sum(value, axis=0, keepdims=True)

        low[...] = jnp.zeros_like(low)
        high[...] = jnp.zeros_like(high)
        low[0:cut, :] = lay_ref[0:cut, :]
        high[0 : rows - cut, :] = lay_ref[cut:rows, :]
        for k, ref in enumerate(stat_refs):
            high[rows - cut + k : rows - cut + k + 1, :] = ref[...].reshape(1, model)
        first = jnp.full(low.shape, turn_ref[0], jnp.int32) == 0
        own_ref[...] = jnp.zeros_like(own_ref)
        own_ref[0:tall, :] = jnp.where(first, low[...], high[...])
        table_row(0, own_ref)
        own_ref[cut + 1 : cut + 2, 0:width] = col_ref[:, 0:width]
        own_ref[cut + 1 : cut + 2, width:model] = col_ref[:, 2 * width : 3 * width]
        total = jnp.sum(a_ref[...].astype(F32), axis=0, keepdims=True) + jnp.sum(
            b_ref[...].astype(F32), axis=0, keepdims=True
        )
        for k in range(used - cut - 2):
            own_ref[cut + 2 + k : cut + 3 + k, :] = total[:, k * model : (k + 1) * model]
        low[...] = jnp.where(first, high[...], low[...])
        table_row(1, low)
        other_ref[...] = low[...].astype(BF16)

    def full(value):
        return pl.BlockSpec(value.shape, lambda i, w: (0,) * value.ndim)

    operands = (layout, *stats, tables, columns, pre_a, pre_b)
    outs = [
        jax.ShapeDtypeStruct((full_rows, model), F32),
        jax.ShapeDtypeStruct((tall, model), BF16),
    ]
    return pl.pallas_call(
        body,
        grid_spec=pltpu.PrefetchScalarGridSpec(
            num_scalar_prefetch=1,
            grid=(1,),
            in_specs=[full(value) for value in operands],
            out_specs=[full(value) for value in outs],
            scratch_shapes=[pltpu.VMEM((tall, model), F32)] * 2,
        ),
        out_shape=outs,
        cost_estimate=NO_COST,
        name="small_parts",
    )(turn, *operands)


def settle(sides, out_pair, in_pair, out_rows):
    half, model = out_pair[0].shape
    thin, wide = in_pair[0].shape

    def body(side_ref, out_kept, out_got, in_kept, in_got, out_ref, rest_ref, in_ref, sum_ref):
        total = jnp.zeros((1, 1), F32)
        for k, (kept, got) in enumerate(((out_kept, out_got), (in_kept, in_got))):
            left, right = kept[...].astype(F32), got[...].astype(F32)
            total = total + jnp.sum(left * left + right * right).reshape(1, 1)
            first = jnp.full(left.shape, side_ref[k], jnp.int32) == 0
            low, high = jnp.where(first, left, right), jnp.where(first, right, left)
            if k == 0:
                out_ref[0:half, :] = low
                out_ref[half:out_rows, :] = high[0 : out_rows - half]
                rest_ref[...] = high[out_rows - half :]
            else:
                in_ref[0:thin, :] = low
                in_ref[thin:, :] = high
        sum_ref[...] = total

    def full(value):
        return pl.BlockSpec(value.shape, lambda i, w: (0,) * value.ndim)

    operands = (*out_pair, *in_pair)
    outs = [
        jax.ShapeDtypeStruct((out_rows, model), F32),
        jax.ShapeDtypeStruct((2 * half - out_rows, model), F32),
        jax.ShapeDtypeStruct((2 * thin, wide), F32),
        jax.ShapeDtypeStruct((1, 1), F32),
    ]
    return pl.pallas_call(
        body,
        grid_spec=pltpu.PrefetchScalarGridSpec(
            num_scalar_prefetch=1,
            grid=(1,),
            in_specs=[full(value) for value in operands],
            out_specs=[full(value) for value in outs],
        ),
        out_shape=outs,
        cost_estimate=NO_COST,
        name="settle",
    )(sides, *operands)


def swap(value):
    size = lax.axis_size("tensor")
    return lax.ppermute(value, "tensor", [(i, (i + 1) % size) for i in range(size)])


def ring_bits(turned):
    size = lax.axis_size("dp")
    bits = [1 << k for k in range(size.bit_length() - 1)]
    return bits[1::-1] + bits[2:] if turned else bits


def ring_steps(bits):
    return [(True, bit) for bit in bits] + [(False, bit) for bit in reversed(bits)]


def side_of(bit):
    return (lax.axis_index("dp") >> (bit.bit_length() - 1)) & 1


def begin(step, value):
    scatter, bit = step
    if not scatter:
        return value, value
    side = side_of(bit)
    half = value.shape[0] // 2
    part = lambda where: lax.dynamic_slice_in_dim(
        value, where * half, half, 0, allow_negative_indices=False
    )
    return part(side), part(1 - side)


def across(step, send):
    size = lax.axis_size("dp")
    return lax.ppermute(send, "dp", [(i, i ^ step[1]) for i in range(size)])


def finish(step, kept, send):
    scatter, bit = step
    received = across(step, send)
    if scatter:
        return kept + received
    low = side_of(bit) == 0
    return jnp.concatenate([jnp.where(low, kept, received), jnp.where(low, received, kept)])


def ring_run(steps, value):
    for step in steps:
        value = finish(step, *begin(step, value))
    return value


def update(clip_factor, grads, state):
    share = state[0].shape[1] // BLOCK
    start = lax.axis_index("dp").astype(jnp.int32) * share
    wide, wide_info, thin, thin_info = [], [], [], []
    base = 0
    row = 0
    for grad in grads:
        rows = grad.size // BLOCK
        if grad.ndim == 2 and grad.shape[1] % BLOCK == 0 and grad.shape[0] > 16:
            lanes = grad.shape[1] // BLOCK
            grad = jnp.pad(grad, ((0, -grad.shape[0] % 8), (0, 0)))
            slab = min(grad.shape[0], -(-(share // lanes + 18) // 8) * 8)
            wide.append(grad)
            wide_info.append((base, lanes, grad.shape[0], slab))
        else:
            thin.append(jnp.pad(grad.reshape(rows, BLOCK), ((0, -rows % 8), (0, 0))))
            thin_info.append((base, row, rows))
            row += rows + -rows % 8
        base += rows
    thin_all = jnp.concatenate(thin)
    margin = -(-max(info[1] * info[3] for info in wide_info) // 8) * 8 + 8

    def slab_start(first, info):
        base, lanes, rows, slab = info
        wanted = jnp.maximum(first - base, 0) // (lanes * 8) * 8
        return pl.multiple_of(jnp.minimum(wanted, rows - slab), 8)

    def body(start_ref, clip_ref, *refs):
        wide_refs = refs[: len(wide)]
        thin_ref = refs[len(wide)]
        master, one, two, ema = refs[len(wide) + 1 : len(wide) + 5]
        new_master, new_one, new_two, new_ema, copy, own = refs[len(wide) + 5 :]
        first = start_ref[0]
        own[margin : margin + share, :] = jnp.zeros((share, BLOCK), F32)
        for ref, info in zip(wide_refs, wide_info):
            base, lanes, rows, slab = info

            @pl.when((first < base + rows * lanes) & (first + share > base))
            def _():
                place = margin + base + slab_start(first, info) * lanes - first
                for k in range(lanes):
                    own[pl.ds(place + k, slab, stride=lanes), :] = ref[
                        :, k * BLOCK : (k + 1) * BLOCK
                    ]

        for base, row, rows in thin_info:

            @pl.when((first < base + rows) & (first + share > base))
            def _():
                own[pl.ds(margin + base - first, rows), :] = thin_ref[row : row + rows, :]

        scale = clip_ref[0]

        def advance(row, rows):
            many = -(-rows // 8) * 8
            grad = own[pl.ds(pl.multiple_of(margin + row, 8), many), :].reshape(1, many * BLOCK)
            grad = grad[:, : rows * BLOCK] * scale
            place = (slice(None), pl.ds(pl.multiple_of(row * BLOCK, 8 * BLOCK), rows * BLOCK))
            moment = beta_one * one[place] + (1.0 - beta_one) * grad
            second = beta_two * two[place] + (1.0 - beta_two) * grad * grad
            new_one[place] = moment
            new_two[place] = second
            step_size = (
                moment
                / (1.0 - beta_one**STEP)
                / (jnp.sqrt(second / (1.0 - beta_two**STEP)) + adam_eps)
            )
            weight = master[place]
            weight = weight - learn_rate * (step_size + decay_rate * weight)
            new_master[place] = weight
            new_ema[place] = average_rate * ema[place] + (1.0 - average_rate) * weight
            copy[place] = weight.astype(BF16)

        def many_rows(number, carry):
            advance(number * CHUNK, CHUNK)
            return carry

        lax.fori_loop(0, share // CHUNK, many_rows, 0)
        if share % CHUNK:
            advance(share // CHUNK * CHUNK, share % CHUNK)

    plain = pl.BlockSpec((1, share * BLOCK), lambda i, s: (0, 0))
    specs = [pl.BlockSpec(memory_space=pltpu.SMEM)]
    for grad, info in zip(wide, wide_info):
        specs.append(
            pl.BlockSpec(
                (pl.Element(info[3]), pl.Element(grad.shape[1])),
                lambda i, s, info=info: (slab_start(s[0], info), 0),
            )
        )
    specs.append(pl.BlockSpec(thin_all.shape, lambda i, s: (0, 0)))
    flat = jax.ShapeDtypeStruct((1, share * BLOCK), F32)
    return pl.pallas_call(
        body,
        grid_spec=pltpu.PrefetchScalarGridSpec(
            num_scalar_prefetch=1,
            grid=(1,),
            in_specs=specs + [plain] * 4,
            out_specs=[plain] * 5,
            scratch_shapes=[pltpu.VMEM((2 * margin + share + 8, BLOCK), F32)],
        ),
        out_shape=[flat] * 4 + [jax.ShapeDtypeStruct((1, share * BLOCK), BF16)],
        name="update",
    )(
        start.reshape(1),
        clip_factor.reshape(1),
        *wide,
        thin_all,
        *state,
    )


def per_device(
    hidden_in,
    cotangent,
    box_coords,
    doc_ids,
    buckets,
    layout_weight,
    norm_gains,
    norm_shifts,
    branch_biases,
    qkv_weight,
    query_value_bias,
    output_weight,
    ffn_in_weight,
    ffn_in_bias,
    ffn_out_weight,
    relative_table,
    master_flat,
    moment_one,
    moment_two,
    ema_flat,
):
    turn = lax.axis_index("tensor")
    window = turn.astype(jnp.int32).reshape(1)
    gains = norm_gains.astype(F32)
    norm_offsets = norm_shifts.astype(F32)
    biases = branch_biases.astype(F32)

    table_own = jnp.transpose(relative_table, (2, 0, 1))
    qkv_other = swap(qkv_weight)
    qv_bias_other = swap(query_value_bias)
    table_other = swap(table_own)
    output_other = swap(output_weight)
    ffn_in_other = swap(ffn_in_weight)
    ffn_bias_other = swap(ffn_in_bias)
    ffn_out_other = swap(ffn_out_weight)

    features = box_features(box_coords).astype(BF16)
    embedded = hidden_in.astype(F32) + dot_tn(features, layout_weight)
    inputs = embedded.astype(BF16)
    inputs_swap = swap(inputs)

    qkv_a, context_a, probs_a = attend(
        window, inputs, qkv_weight, query_value_bias, doc_ids, buckets, table_own
    )
    qkv_b, context_b, probs_b = attend(
        window, inputs, qkv_other, qv_bias_other, doc_ids, buckets, table_other
    )
    context_swap = swap(context_b)
    attn_out = dot(context_a, output_weight) + dot(context_b, output_other) + biases[0]
    normed_one, inv_std_one = normalize(embedded + attn_out)
    mid_norm = normed_one * gains[0] + norm_offsets[0]
    mid_low = mid_norm.astype(BF16)
    mid_swap = swap(mid_low)

    def expand(weight, bias):
        pre = dot(mid_low, weight) + bias.astype(F32)
        share = 0.5 + 0.5 * lax.erf(pre * math.sqrt(0.5))
        slope = share + pre * (math.sqrt(0.5 / math.pi) * jnp.exp(-0.5 * pre * pre))
        return (pre * share).astype(BF16), slope

    hidden_a, slope_a = expand(ffn_in_weight, ffn_in_bias)
    hidden_b, slope_b = expand(ffn_in_other, ffn_bias_other)
    hidden_swap = swap(hidden_b)
    branch = dot(hidden_a, ffn_out_weight) + dot(hidden_b, ffn_out_other) + biases[1]
    normed_two, inv_std_two = normalize(mid_norm + branch)
    hidden_out = (normed_two * gains[1] + norm_offsets[1]).astype(BF16)
    grad_out = cotangent.astype(F32)
    gain_two = jnp.sum(grad_out * normed_two, axis=0)
    shift_two = jnp.sum(grad_out, axis=0)
    grad_sum_two = norm_back(grad_out, normed_two, inv_std_two, gains[1])
    bias_two = jnp.sum(grad_sum_two, axis=0)
    grad_branch = grad_sum_two.astype(BF16)
    grad_branch_swap = swap(grad_branch)

    grad_pre_b = (slope_b * dot_nt(grad_branch, ffn_out_other)).astype(BF16)
    grad_pre_swap = swap(grad_pre_b)
    grad_pre_a = (slope_a * dot_nt(grad_branch, ffn_out_weight)).astype(BF16)
    ffn_out_low = (
        dot_tn(hidden_a, grad_branch) + dot_tn(hidden_swap, grad_branch_swap)
    ).astype(BF16)
    ffn_in_low = (dot_tn(mid_low, grad_pre_a) + dot_tn(mid_swap, grad_pre_swap)).astype(BF16)
    grad_mid = (
        grad_sum_two + dot_nt(grad_pre_a, ffn_in_weight) + dot_nt(grad_pre_b, ffn_in_other)
    )
    gain_one = jnp.sum(grad_mid * normed_one, axis=0)
    shift_one = jnp.sum(grad_mid, axis=0)
    grad_sum_one = norm_back(grad_mid, normed_one, inv_std_one, gains[0])
    bias_one = jnp.sum(grad_sum_one, axis=0)
    grad_attn = grad_sum_one.astype(BF16)
    grad_attn_swap = swap(grad_attn)
    output_grad = dot_tn(context_a, grad_attn) + dot_tn(context_swap, grad_attn_swap)
    grad_context_a = dot_nt(grad_attn, output_weight).astype(BF16)
    grad_context_b = dot_nt(grad_attn, output_other).astype(BF16)

    barrier = lax.optimization_barrier
    steps_a, steps_b = ring_steps(ring_bits(False)), ring_steps(ring_bits(True))
    out_keep, out_send = begin(
        steps_a[0], jnp.concatenate([ffn_out_low, output_grad.astype(BF16)])
    )
    in_keep, in_send = begin(steps_b[0], ffn_in_low)
    (grad_context_a, grad_context_b), out_send, in_send = barrier(
        ((grad_context_a, grad_context_b), out_send, in_send)
    )
    grads_a, grads_b, scores_a, scores_b = attend_back(
        window, (qkv_a, qkv_b), (grad_context_a, grad_context_b), (probs_a, probs_b)
    )
    grads_swap = swap(grads_b)
    width = qkv_weight.shape[2]
    early = input_back(grads_a, grads_b, qkv_weight, qkv_other, grad_sum_one, features, inputs)
    early, out_keep, in_keep = barrier((early, out_keep, in_keep))
    input_grad, layout_part, product, columns = early
    out_sum = finish(steps_a[0], out_keep, out_send)
    in_sum = finish(steps_b[0], in_keep, in_send)

    out_keep, out_send = begin(steps_a[1], out_sum)
    in_keep, in_send = begin(steps_b[1], in_sum)
    product, scores_a, scores_b, out_send, in_send = barrier(
        (product, scores_a, scores_b, out_send, in_send)
    )
    sides = jnp.stack([side_of(steps[0][1]) for steps in (steps_a, steps_b)]).astype(jnp.int32)
    late = pair_back(sides, inputs_swap, grads_swap, product, columns)
    tables = table_sums(window, (scores_a, scores_b), buckets)
    late, tables, out_keep, in_keep = barrier((late, tables, out_keep, in_keep))
    a_keep, a_send, b_keep, b_send, qv_sums = late
    out_sum = finish(steps_a[1], out_keep, out_send)
    in_sum = finish(steps_b[1], in_keep, in_send)

    plans = {
        "out": (0, steps_a[2:]),
        "in": (0, steps_b[2:]),
        "a": (0, steps_a),
        "b": (0, steps_b),
        "c": (1, steps_b),
    }
    sums = {"out": out_sum, "in": in_sum}
    last = len(steps_a) - 1
    for number in range(last + 2):
        if number == 1:
            other = swap(other_shared).astype(F32)
            pack_c = own_shared + jnp.pad(
                other, ((0, own_shared.shape[0] - other.shape[0]), (0, 0))
            )
            pack_c = pack_c.astype(BF16)
            sums["c"] = pack_c
        opened = {
            name: begin(steps[number - first], sums[name])
            for name, (first, steps) in plans.items()
            if first <= number < first + len(steps) and name in sums
        }
        if number == 0:
            opened["a"], opened["b"] = (a_keep, a_send), (b_keep, b_send)
        sends = {name: send for name, (_, send) in opened.items()}
        if number == 0:
            sends, tables, qv_sums, layout_part = barrier((sends, tables, qv_sums, layout_part))
            cut = (layout_part.shape[0] + 6) // lax.axis_size("tensor")
            own_shared, other_shared = small_parts(
                window,
                layout_part,
                (gain_one, gain_two, shift_one, shift_two, bias_one, bias_two),
                tables,
                qv_sums,
                grad_pre_a,
                grad_pre_swap,
                cut,
            )
        elif number == last - 1:
            small_send = sends.pop("c")
            sends = barrier(sends)
            sends["c"], sums["out"], sums["in"] = barrier(
                (small_send, sums["out"], sums["in"])
            )
        elif number == last + 1:
            sends, sums["a"], sums["b"] = barrier((sends, sums["a"], sums["b"]))
        elif number == last:
            sends, early_pairs = barrier((sends, (sums["out"], sums["in"])))
            settled = settle(sides, *early_pairs, ffn_out_low.shape[0])
            kept_late, settled = barrier(((opened["a"][0], opened["b"][0]), settled))
            opened["a"], opened["b"] = ((kept, None) for kept in kept_late)
        else:
            sends = barrier(sends)
        for name, (kept, _) in opened.items():
            first, steps = plans[name]
            step = steps[number - first]
            if name == "c" and number == last:
                kept, sums["a"], sums["b"] = barrier((kept, sums["a"], sums["b"]))
            if name in ("out", "in") and number == last - 2:
                sums[name] = (kept, across(step, sends[name]))
            else:
                sums[name] = finish(step, kept, sends[name])
    pack_a, pack_b, pack_c = (sums[name] for name in ("a", "b", "c"))
    ffn_out_grad, output_grad, ffn_in_grad, early_square = settled

    square = sum(
        jnp.sum(jnp.square(member.astype(F32)))
        for member in (pack_a, pack_b, pack_c)
    )
    square = square + early_square[0, 0]
    qkv_grad = jnp.stack(
        [
            jnp.concatenate([part[:, c * width : (c + 1) * width] for part in (pack_a, pack_b)])
            for c in range(3)
        ]
    ).astype(F32)
    own_low = pack_c[:cut]
    small = pack_c[cut : cut + 4].astype(F32)
    table_grad = small[0, : relative_table.size].reshape(relative_table.shape)
    qv_bias_grad = small[1].reshape(query_value_bias.shape)
    ffn_bias_grad = small[2:4].reshape(-1)
    first_turn = turn == 0
    other_low = swap(own_low)
    shared = jnp.where(
        first_turn,
        jnp.concatenate([own_low, other_low]),
        jnp.concatenate([other_low, own_low]),
    ).astype(F32)
    layout_grad = shared[: layout_part.shape[0]]
    gains_grad, shifts_grad, biases_grad = jnp.split(shared[layout_part.shape[0] :], 3)

    grad_norm = jnp.sqrt(square + swap(square))
    clip_factor = clip_limit / jnp.maximum(grad_norm, clip_limit)
    updated = update(
        clip_factor,
        (
            ffn_in_grad,
            ffn_bias_grad,
            ffn_out_grad,
            qkv_grad.reshape(-1, width),
            qv_bias_grad,
            output_grad,
            table_grad,
            own_low.astype(F32),
        ),
        (master_flat, moment_one, moment_two, ema_flat),
    )
    return (
        hidden_out,
        input_grad,
        layout_grad,
        gains_grad,
        shifts_grad,
        biases_grad,
        qkv_grad,
        qv_bias_grad,
        output_grad,
        ffn_in_grad,
        ffn_bias_grad,
        ffn_out_grad,
        table_grad,
        grad_norm,
    ) + tuple(updated)


def solution(mesh):
    return jax.shard_map(
        per_device,
        mesh=mesh,
        in_specs=(
            P(("dp", "tensor"), None),
            P(("dp", "tensor"), None),
            P(None, ("dp", "tensor")),
            P("dp", None),
            P(None, "dp", None, None),
            P(),
            P(),
            P(),
            P(),
            P(None, None, "tensor"),
            P(None, "tensor"),
            P("tensor", None),
            P(None, "tensor"),
            P("tensor"),
            P("tensor", None),
            P(None, None, "tensor"),
            P("tensor", "dp"),
            P("tensor", "dp"),
            P("tensor", "dp"),
            P("tensor", "dp"),
        ),
        out_specs=(
            P(("dp", "tensor"), None),
            P(("dp", "tensor"), None),
            P(),
            P(),
            P(),
            P(),
            P(None, None, "tensor"),
            P(None, "tensor"),
            P("tensor", None),
            P(None, "tensor"),
            P("tensor"),
            P("tensor", None),
            P(None, None, "tensor"),
            P(),
            P("tensor", "dp"),
            P("tensor", "dp"),
            P("tensor", "dp"),
            P("tensor", "dp"),
            P("tensor", "dp"),
        ),
        check_vma=False,
    )
```

```python
import math

import jax
import jax.numpy as jnp
from jax import lax
from jax.experimental import pallas as pl
from jax.experimental.pallas import tpu as pltpu
from jax.sharding import PartitionSpec as P

NB = 32
FEAT = 256
STEP = 10
BLOCK = 128
CHUNK = 32
ATTEND_FLOPS = 1 << 33
BACK_FLOPS = 1 << 35
NO_COST = pl.CostEstimate(flops=1, transcendentals=0, bytes_accessed=1)


norm_eps = 1e-05
learn_rate = 0.02
beta_one = 0.9
beta_two = 0.999
adam_eps = 1e-08
decay_rate = 0.01
average_rate = 0.5
clip_limit = 1.0
mask_fill = -1e30

F32 = jnp.float32
BF16 = jnp.bfloat16
NT = (((1,), (1,)), ((), ()))
TN = (((0,), (0,)), ((), ()))


def dot(left, right):
    return jnp.dot(left, right, preferred_element_type=F32)


def dot_nt(left, right):
    return lax.dot_general(left, right, NT, preferred_element_type=F32)


def dot_tn(left, right):
    return lax.dot_general(left, right, TN, preferred_element_type=F32)


def box_features(coords):
    count = FEAT // 8
    freqs = jnp.exp(-math.log(10000.0) * jnp.arange(count, dtype=F32) / count)
    angles = coords.astype(F32)[:, None, :] * freqs[None, :, None]
    waves = jnp.stack([jnp.sin(angles), jnp.cos(angles)], axis=1)
    return waves.reshape(FEAT, coords.shape[1])


def normalize(value):
    centre = value - jnp.mean(value, axis=-1, keepdims=True)
    inv_std = lax.rsqrt(jnp.mean(centre * centre, axis=-1, keepdims=True) + norm_eps)
    return (centre * inv_std, inv_std)


def norm_back(grad_out, normed, inv_std, gain):
    scaled = grad_out * gain
    return inv_std * (
        scaled
        - jnp.mean(scaled, axis=-1, keepdims=True)
        - normed * jnp.mean(scaled * normed, axis=-1, keepdims=True)
    )


def attend(which, inputs, weight, bias, docs, buckets, table):
    rows, model = inputs.shape
    width = weight.shape[2]
    heads, _, nb = table.shape
    pairs = heads // 2
    half = width // heads
    span = 3 * BLOCK
    blocks = rows // BLOCK
    scale = 1.0 / math.sqrt(half)
    def body(
        which_ref, x_ref, w_ref, bias_ref, doc_ref, b_ref, t_ref, qkv_ref, ctx_ref, p_ref
    ):
        block = pl.program_id(0)

        @pl.when(block == 0)
        def _():
            for c in range(3):
                made = dot(x_ref[...], w_ref[c])
                if c != 1:
                    made = made + bias_ref[c // 2 : c // 2 + 1, :].astype(F32)
                qkv_ref[:, c * width : (c + 1) * width] = made.astype(BF16)

        start = pl.multiple_of(jnp.clip(block - 1, 0, blocks - 3) * BLOCK, BLOCK)
        own_rows = pl.ds(pl.multiple_of(block * BLOCK, BLOCK), BLOCK)
        key_rows = pl.ds(start, span)
        windows = docs.shape[0]

        def docs_at(lanes, count):
            here = doc_ref[:, lanes].astype(F32)
            mine = lax.broadcasted_iota(jnp.int32, (windows, count), 0) == which_ref[0]
            return jnp.sum(jnp.where(mine, here, 0.0), axis=0, keepdims=True)

        diagonal = lax.broadcasted_iota(jnp.int32, (BLOCK, BLOCK), 0) == (
            lax.broadcasted_iota(jnp.int32, (BLOCK, BLOCK), 1)
        )
        docs_here = jnp.broadcast_to(docs_at(own_rows, BLOCK), (BLOCK, BLOCK))
        column = jnp.sum(jnp.where(diagonal, docs_here, 0.0), axis=1, keepdims=True)
        same = column == docs_at(key_rows, span)
        first = b_ref[0, 0, :, key_rows]
        second = b_ref[1, 0, :, key_rows]
        low_lane = lax.broadcasted_iota(jnp.int32, (BLOCK, 2 * half), 1) < half

        def shifted(p, c):
            return pl.ds(pl.multiple_of(c * width + p * 2 * half, 2 * half), 2 * half)

        def one_pair(p, carry):
            cols = shifted(p, 0)
            q2 = qkv_ref[own_rows, cols]
            k2 = qkv_ref[key_rows, shifted(p, 1)]
            v2 = qkv_ref[key_rows, shifted(p, 2)]
            outs = []
            for e in range(2):
                qm = jnp.where(low_lane == (e == 0), q2, jnp.zeros_like(q2))
                raw = dot_nt(qm, k2)
                rows_xy = jnp.concatenate(
                    [t_ref[2 * p + e].astype(F32), jnp.zeros((2, BLOCK - nb), F32)], axis=1
                )
                row_x = jnp.broadcast_to(rows_xy[0:1], (BLOCK, BLOCK))
                row_y = jnp.broadcast_to(rows_xy[1:2], (BLOCK, BLOCK))
                bias = jnp.concatenate(
                    [
                        jnp.take_along_axis(
                            row_x, first[:, c : c + BLOCK], axis=1, mode="promise_in_bounds"
                        )
                        + jnp.take_along_axis(
                            row_y, second[:, c : c + BLOCK], axis=1, mode="promise_in_bounds"
                        )
                        for c in range(0, span, BLOCK)
                    ],
                    axis=1,
                )
                scores = jnp.where(same, raw * scale + bias, mask_fill)
                top = jnp.max(scores, axis=1, keepdims=True)
                weights = jnp.exp(scores - top)
                probs = weights * (1.0 / jnp.sum(weights, axis=1, keepdims=True))
                p_ref[2 * p + e, 0] = probs
                outs.append(dot(probs.astype(BF16), v2))
            ctx_ref[:, cols] = jnp.where(low_lane, outs[0], outs[1]).astype(BF16)
            return carry

        lax.fori_loop(0, pairs, one_pair, 0, unroll=True)

    return pl.pallas_call(
        body,
        grid_spec=pltpu.PrefetchScalarGridSpec(
            num_scalar_prefetch=1,
            grid=(blocks,),
            in_specs=[
                pl.BlockSpec((rows, model), lambda i, w: (0, 0)),
                pl.BlockSpec((3, model, width), lambda i, w: (0, 0, 0)),
                pl.BlockSpec((2, width), lambda i, w: (0, 0)),
                pl.BlockSpec(docs.shape, lambda i, w: (0, 0)),
                pl.BlockSpec((2, 1, BLOCK, rows), lambda i, w: (0, w[0], i, 0)),
                pl.BlockSpec(table.shape, lambda i, w: (0, 0, 0)),
            ],
            out_specs=[
                pl.BlockSpec((rows, 3 * width), lambda i, w: (0, 0)),
                pl.BlockSpec((BLOCK, width), lambda i, w: (i, 0)),
                pl.BlockSpec((heads, 1, BLOCK, span), lambda i, w: (0, i, 0, 0)),
            ],
        ),
        out_shape=[
            jax.ShapeDtypeStruct((rows, 3 * width), BF16),
            jax.ShapeDtypeStruct((rows, width), BF16),
            jax.ShapeDtypeStruct((heads, blocks, BLOCK, span), F32),
        ],
        cost_estimate=pl.CostEstimate(flops=ATTEND_FLOPS, transcendentals=0, bytes_accessed=1 << 23),
        name="attend",
    )(which, inputs, weight, bias, docs, buckets, table)


def attend_back(which, qkvs, grads, probs):
    rows, width = qkvs[0].shape[0], qkvs[0].shape[1] // 3
    heads, blocks, _, span = probs[0].shape
    pairs = heads // 2
    half = width // heads
    scale = 1.0 / math.sqrt(half)

    def body(qkv_a, qkv_b, g_a, g_b, p_a, p_b, d_a, d_b, s_a, s_b, acc_a, acc_b):
        block = pl.program_id(0)
        start = pl.multiple_of(jnp.clip(block - 1, 0, blocks - 3) * BLOCK, BLOCK)
        own_rows = pl.ds(pl.multiple_of(block * BLOCK, BLOCK), BLOCK)
        key_rows = pl.ds(start, span)
        low_lane = lax.broadcasted_iota(jnp.int32, (BLOCK, 2 * half), 1) < half

        @pl.when(block == 0)
        def _():
            acc_a[...] = jnp.zeros_like(acc_a)
            acc_b[...] = jnp.zeros_like(acc_b)

        for qkv_ref, g_ref, p_ref, d_ref, s_ref, sums in (
            (qkv_a, g_a, p_a, d_a, s_a, acc_a),
            (qkv_b, g_b, p_b, d_b, s_b, acc_b),
        ):

            def shifted(p, c):
                return pl.ds(pl.multiple_of(c * width + p * 2 * half, 2 * half), 2 * half)

            def one_pair(p, carry):
                cols = shifted(p, 0)
                q2 = qkv_ref[own_rows, cols]
                g2 = g_ref[:, cols]
                k2 = qkv_ref[key_rows, shifted(p, 1)]
                v2 = qkv_ref[key_rows, shifted(p, 2)]
                dqs = []
                dk = sums[0, key_rows, cols]
                dv = sums[1, key_rows, cols]
                for e in range(2):
                    mine = low_lane == (e == 0)
                    qm = jnp.where(mine, q2, jnp.zeros_like(q2))
                    gm = jnp.where(mine, g2, jnp.zeros_like(g2))
                    pr = p_ref[2 * p + e, 0]
                    gp = dot_nt(gm, v2)
                    gs = pr * (gp - jnp.sum(pr * gp, axis=1, keepdims=True))
                    s_ref[2 * p + e, 0] = gs
                    raw = (gs * scale).astype(BF16)
                    dqs.append(dot(raw, k2))
                    dk = dk + dot_tn(raw, qm)
                    dv = dv + dot_tn(pr.astype(BF16), gm)
                d_ref[own_rows, cols] = jnp.where(low_lane, dqs[0], dqs[1]).astype(BF16)
                sums[0, key_rows, cols] = dk
                sums[1, key_rows, cols] = dv
                return carry

            lax.fori_loop(0, pairs, one_pair, 0, unroll=True)

        @pl.when(block == blocks - 1)
        def _():
            for d_ref, sums in ((d_a, acc_a), (d_b, acc_b)):
                d_ref[:, width : 2 * width] = sums[0].astype(BF16)
                d_ref[:, 2 * width :] = sums[1].astype(BF16)

    whole = pl.BlockSpec((rows, 3 * width), lambda i: (0, 0))
    part = pl.BlockSpec((BLOCK, width), lambda i: (i, 0))
    prob = pl.BlockSpec((heads, 1, BLOCK, span), lambda i: (0, i, 0, 0))
    shape = jax.ShapeDtypeStruct((rows, 3 * width), BF16)
    score = jax.ShapeDtypeStruct(probs[0].shape, F32)
    return pl.pallas_call(
        body,
        grid=(blocks,),
        in_specs=[whole, whole, part, part, prob, prob],
        out_specs=[whole, whole, prob, prob],
        scratch_shapes=[
            pltpu.VMEM((2, rows, width), F32),
            pltpu.VMEM((2, rows, width), F32),
        ],
        out_shape=[shape, shape, score, score],
        input_output_aliases={4: 2, 5: 3},
        cost_estimate=pl.CostEstimate(
            flops=BACK_FLOPS, transcendentals=0, bytes_accessed=1 << 24
        ),
        name="attend_back",
    )(*qkvs, *grads, *probs)


def table_sums(which, scores, buckets):
    heads, blocks, _, span = scores[0].shape
    nb = NB
    rows = blocks * BLOCK
    group = 8
    codes = 2 * nb
    lanes = 2 * 2 * heads * group

    def body(which_ref, s_a, s_b, b_ref, tab_ref, acc_ref):
        block = pl.program_id(0)
        start = pl.multiple_of(jnp.clip(block - 1, 0, blocks - 3) * BLOCK, BLOCK)
        key_rows = pl.ds(start, span)

        @pl.when(block == 0)
        def _():
            acc_ref[...] = jnp.zeros_like(acc_ref)

        code_ids = lax.broadcasted_iota(jnp.int32, (nb, span), 0).astype(F32).astype(BF16)
        one, zero = jnp.ones((), BF16), jnp.zeros((), BF16)

        def one_side(r8):
            b0 = b_ref[0, 0, r8, key_rows].astype(F32)
            b1 = b_ref[1, 0, r8, key_rows].astype(F32)
            pieces = []
            for r in range(group):
                for b in (b0, b1):
                    row = jnp.broadcast_to(b[r : r + 1], (nb, span)).astype(BF16)
                    pieces.append(jnp.where(row == code_ids, one, zero))
            gg = jnp.concatenate(
                [ref[:, 0, r8, :].reshape(heads * group, span) for ref in (s_a, s_b)], axis=0
            )
            upper = gg.astype(BF16)
            lower = (gg - upper.astype(F32)).astype(BF16)
            return jnp.concatenate(pieces, axis=0), jnp.concatenate([upper, lower], axis=0)

        def two_groups(g, carry):
            sides = [
                one_side(pl.ds(pl.multiple_of((2 * g + k) * group, group), group))
                for k in range(2)
            ]
            onehot, both = (jnp.concatenate(parts, axis=1) for parts in zip(*sides))
            acc_ref[...] += dot_nt(onehot, both)
            return carry

        lax.fori_loop(0, BLOCK // group // 2, two_groups, 0)

        @pl.when(block == blocks - 1)
        def _():
            lane_row = lax.broadcasted_iota(jnp.int32, (codes, lanes), 1) % group
            total = jnp.zeros((codes, lanes), F32)
            for r in range(group):
                total = total + jnp.where(
                    lane_row == r, acc_ref[r * codes : (r + 1) * codes, :], 0.0
                )
            tab_ref[...] = total

    prob = pl.BlockSpec((heads, 1, BLOCK, span), lambda i, w: (0, i, 0, 0))
    return pl.pallas_call(
        body,
        grid_spec=pltpu.PrefetchScalarGridSpec(
            num_scalar_prefetch=1,
            grid=(blocks,),
            in_specs=[
                prob,
                prob,
                pl.BlockSpec((2, 1, BLOCK, rows), lambda i, w: (0, w[0], i, 0)),
            ],
            out_specs=pl.BlockSpec((codes, lanes), lambda i, w: (0, 0)),
            scratch_shapes=[pltpu.VMEM((group * codes, lanes), F32)],
        ),
        out_shape=jax.ShapeDtypeStruct((codes, lanes), F32),
        cost_estimate=NO_COST,
        name="table_sums",
    )(which, *scores, buckets)


def input_back(grads_a, grads_b, weight_a, weight_b, grad_sum, features, inputs):
    width = weight_a.shape[2]

    def body(g_a, g_b, w_a, w_b, sum_ref, f_ref, x_ref, in_ref, lay_ref, prod_ref, col_ref):
        total = sum_ref[...]
        for g_ref, w_ref in ((g_a, w_a), (g_b, w_b)):
            for c in range(3):
                total = total + dot_nt(g_ref[:, c * width : (c + 1) * width], w_ref[c])
        in_ref[...] = total
        lay_ref[...] = dot(f_ref[...], total.astype(BF16))
        prod_ref[...] = dot_tn(x_ref[...], g_a[...])
        col_ref[...] = jnp.sum(g_a[...].astype(F32), axis=0, keepdims=True)

    model = inputs.shape[1]
    return pl.pallas_call(
        body,
        out_shape=[
            jax.ShapeDtypeStruct(grad_sum.shape, F32),
            jax.ShapeDtypeStruct((features.shape[0], model), F32),
            jax.ShapeDtypeStruct((model, 3 * width), F32),
            jax.ShapeDtypeStruct((1, 3 * width), F32),
        ],
        cost_estimate=NO_COST,
        name="input_back",
    )(grads_a, grads_b, weight_a, weight_b, grad_sum, features, inputs)


def pair_back(sides, inputs, grads, product, columns):
    model = inputs.shape[1]
    wide = grads.shape[1]
    part = model // 4

    def body(side_ref, x_ref, g_ref, prod_ref, col_ref, *refs):
        outs, sum_ref, whole = refs[:4], refs[4], refs[5]
        whole[...] = (prod_ref[...] + dot_tn(x_ref[...], g_ref[...])).astype(BF16)
        for k, out_ref in enumerate(outs):
            side = side_ref[k // 2] if k % 2 == 0 else 1 - side_ref[k // 2]
            first = pl.multiple_of((k // 2) * 2 * part + side * part, 16)
            out_ref[...] = whole[pl.ds(first, part), :]
        sum_ref[...] = col_ref[...] + jnp.sum(g_ref[...].astype(F32), axis=0, keepdims=True)

    def full(value):
        return pl.BlockSpec(value.shape, lambda i, w: (0,) * value.ndim)

    operands = (inputs, grads, product, columns)
    outs = [jax.ShapeDtypeStruct((part, wide), BF16)] * 4
    outs.append(jax.ShapeDtypeStruct((1, wide), F32))
    return pl.pallas_call(
        body,
        grid_spec=pltpu.PrefetchScalarGridSpec(
            num_scalar_prefetch=1,
            grid=(1,),
            in_specs=[full(value) for value in operands],
            out_specs=[full(value) for value in outs],
            scratch_shapes=[pltpu.VMEM((model, wide), BF16)],
        ),
        out_shape=outs,
        cost_estimate=NO_COST,
        name="pair_back",
    )(sides, *operands)


def small_parts(turn, layout, stats, tables, columns, pre_a, pre_b, cut):
    rows, model = layout.shape
    width = model // 2
    tall = -(-(cut + 1) // 16) * 16
    used = cut + 2 + pre_a.shape[1] // model
    unit = 8 * lax.axis_size("dp")
    full_rows = -(-used // unit) * unit

    def body(turn_ref, lay_ref, *refs):
        stat_refs, refs = refs[:6], refs[6:]
        tab_ref, col_ref, a_ref, b_ref, own_ref, other_ref, low, high = refs
        lanes = tab_ref.shape[1] // 2
        heads = lanes // 16
        codes = tab_ref.shape[0]
        table = tab_ref[:, 0:lanes] + tab_ref[:, lanes : 2 * lanes]
        table = jnp.concatenate([table, jnp.zeros((codes, BLOCK - lanes), F32)], axis=1)
        for step in (1, 2, 4):
            table = table + pltpu.roll(table, BLOCK - step, 1)
        code = lax.broadcasted_iota(jnp.int32, (codes, BLOCK), 0)
        lane = lax.broadcasted_iota(jnp.int32, (codes, BLOCK), 1)

        def table_row(side, ref):
            for c in range(0, codes * heads, BLOCK):
                index = side * heads * 8 + (lane + c) % heads * 8
                value = jnp.take_along_axis(table, index, axis=1, mode="promise_in_bounds")
                value = jnp.where((lane + c) // heads == code, value, 0.0)
                ref[cut : cut + 1, c : c + BLOCK] = jnp.sum(value, axis=0, keepdims=True)

        low[...] = jnp.zeros_like(low)
        high[...] = jnp.zeros_like(high)
        low[0:cut, :] = lay_ref[0:cut, :]
        high[0 : rows - cut, :] = lay_ref[cut:rows, :]
        for k, ref in enumerate(stat_refs):
            high[rows - cut + k : rows - cut + k + 1, :] = ref[...].reshape(1, model)
        first = jnp.full(low.shape, turn_ref[0], jnp.int32) == 0
        own_ref[...] = jnp.zeros_like(own_ref)
        own_ref[0:tall, :] = jnp.where(first, low[...], high[...])
        table_row(0, own_ref)
        own_ref[cut + 1 : cut + 2, 0:width] = col_ref[:, 0:width]
        own_ref[cut + 1 : cut + 2, width:model] = col_ref[:, 2 * width : 3 * width]
        total = jnp.sum(a_ref[...].astype(F32), axis=0, keepdims=True) + jnp.sum(
            b_ref[...].astype(F32), axis=0, keepdims=True
        )
        for k in range(used - cut - 2):
            own_ref[cut + 2 + k : cut + 3 + k, :] = total[:, k * model : (k + 1) * model]
        low[...] = jnp.where(first, high[...], low[...])
        table_row(1, low)
        other_ref[...] = low[...].astype(BF16)

    def full(value):
        return pl.BlockSpec(value.shape, lambda i, w: (0,) * value.ndim)

    operands = (layout, *stats, tables, columns, pre_a, pre_b)
    outs = [
        jax.ShapeDtypeStruct((full_rows, model), F32),
        jax.ShapeDtypeStruct((tall, model), BF16),
    ]
    return pl.pallas_call(
        body,
        grid_spec=pltpu.PrefetchScalarGridSpec(
            num_scalar_prefetch=1,
            grid=(1,),
            in_specs=[full(value) for value in operands],
            out_specs=[full(value) for value in outs],
            scratch_shapes=[pltpu.VMEM((tall, model), F32)] * 2,
        ),
        out_shape=outs,
        cost_estimate=NO_COST,
        name="small_parts",
    )(turn, *operands)


def settle(sides, out_pair, in_pair, out_rows):
    half, model = out_pair[0].shape
    thin, wide = in_pair[0].shape

    def body(side_ref, out_kept, out_got, in_kept, in_got, out_ref, rest_ref, in_ref, sum_ref):
        total = jnp.zeros((1, 1), F32)
        for k, (kept, got) in enumerate(((out_kept, out_got), (in_kept, in_got))):
            left, right = kept[...].astype(F32), got[...].astype(F32)
            total = total + jnp.sum(left * left + right * right).reshape(1, 1)
            first = jnp.full(left.shape, side_ref[k], jnp.int32) == 0
            low, high = jnp.where(first, left, right), jnp.where(first, right, left)
            if k == 0:
                out_ref[0:half, :] = low
                out_ref[half:out_rows, :] = high[0 : out_rows - half]
                rest_ref[...] = high[out_rows - half :]
            else:
                in_ref[0:thin, :] = low
                in_ref[thin:, :] = high
        sum_ref[...] = total

    def full(value):
        return pl.BlockSpec(value.shape, lambda i, w: (0,) * value.ndim)

    operands = (*out_pair, *in_pair)
    outs = [
        jax.ShapeDtypeStruct((out_rows, model), F32),
        jax.ShapeDtypeStruct((2 * half - out_rows, model), F32),
        jax.ShapeDtypeStruct((2 * thin, wide), F32),
        jax.ShapeDtypeStruct((1, 1), F32),
    ]
    return pl.pallas_call(
        body,
        grid_spec=pltpu.PrefetchScalarGridSpec(
            num_scalar_prefetch=1,
            grid=(1,),
            in_specs=[full(value) for value in operands],
            out_specs=[full(value) for value in outs],
        ),
        out_shape=outs,
        cost_estimate=NO_COST,
        name="settle",
    )(sides, *operands)


def swap(value):
    size = lax.axis_size("tensor")
    return lax.ppermute(value, "tensor", [(i, (i + 1) % size) for i in range(size)])


def ring_bits(turned):
    size = lax.axis_size("dp")
    bits = [1 << k for k in range(size.bit_length() - 1)]
    return bits[1::-1] + bits[2:] if turned else bits


def ring_steps(bits):
    return [(True, bit) for bit in bits] + [(False, bit) for bit in reversed(bits)]


def side_of(bit):
    return (lax.axis_index("dp") >> (bit.bit_length() - 1)) & 1


def begin(step, value):
    scatter, bit = step
    if not scatter:
        return value, value
    side = side_of(bit)
    half = value.shape[0] // 2
    part = lambda where: lax.dynamic_slice_in_dim(
        value, where * half, half, 0, allow_negative_indices=False
    )
    return part(side), part(1 - side)


def across(step, send):
    size = lax.axis_size("dp")
    return lax.ppermute(send, "dp", [(i, i ^ step[1]) for i in range(size)])


def finish(step, kept, send):
    scatter, bit = step
    received = across(step, send)
    return kept + received if scatter else merge(step, kept, received)


def merge(step, kept, received):
    low = side_of(step[1]) == 0
    return jnp.concatenate([jnp.where(low, kept, received), jnp.where(low, received, kept)])


def ring_run(steps, value):
    for step in steps:
        value = finish(step, *begin(step, value))
    return value


def update(clip_factor, grads, state):
    share = state[0].shape[1] // BLOCK
    start = lax.axis_index("dp").astype(jnp.int32) * share
    wide, wide_info, thin, thin_info = [], [], [], []
    base = 0
    row = 0
    for grad in grads:
        rows = grad.size // BLOCK
        if grad.ndim == 2 and grad.shape[1] % BLOCK == 0 and grad.shape[0] > 16:
            lanes = grad.shape[1] // BLOCK
            grad = jnp.pad(grad, ((0, -grad.shape[0] % 8), (0, 0)))
            slab = min(grad.shape[0], -(-(share // lanes + 18) // 8) * 8)
            wide.append(grad)
            wide_info.append((base, lanes, grad.shape[0], slab))
        else:
            thin.append(jnp.pad(grad.reshape(rows, BLOCK), ((0, -rows % 8), (0, 0))))
            thin_info.append((base, row, rows))
            row += rows + -rows % 8
        base += rows
    thin_all = jnp.concatenate(thin)
    margin = -(-max(info[1] * info[3] for info in wide_info) // 8) * 8 + 8

    def slab_start(first, info):
        base, lanes, rows, slab = info
        wanted = jnp.maximum(first - base, 0) // (lanes * 8) * 8
        return pl.multiple_of(jnp.minimum(wanted, rows - slab), 8)

    def body(start_ref, clip_ref, *refs):
        wide_refs = refs[: len(wide)]
        thin_ref = refs[len(wide)]
        master, one, two, ema = refs[len(wide) + 1 : len(wide) + 5]
        new_master, new_one, new_two, new_ema, copy, own = refs[len(wide) + 5 :]
        first = start_ref[0]
        own[margin : margin + share, :] = jnp.zeros((share, BLOCK), F32)
        for ref, info in zip(wide_refs, wide_info):
            base, lanes, rows, slab = info

            @pl.when((first < base + rows * lanes) & (first + share > base))
            def _():
                place = margin + base + slab_start(first, info) * lanes - first
                for k in range(lanes):
                    own[pl.ds(place + k, slab, stride=lanes), :] = ref[
                        :, k * BLOCK : (k + 1) * BLOCK
                    ]

        for base, row, rows in thin_info:

            @pl.when((first < base + rows) & (first + share > base))
            def _():
                own[pl.ds(margin + base - first, rows), :] = thin_ref[row : row + rows, :]

        scale = clip_ref[0]

        def advance(row, rows):
            many = -(-rows // 8) * 8
            grad = own[pl.ds(pl.multiple_of(margin + row, 8), many), :].reshape(1, many * BLOCK)
            grad = grad[:, : rows * BLOCK] * scale
            place = (slice(None), pl.ds(pl.multiple_of(row * BLOCK, 8 * BLOCK), rows * BLOCK))
            moment = beta_one * one[place] + (1.0 - beta_one) * grad
            second = beta_two * two[place] + (1.0 - beta_two) * grad * grad
            new_one[place] = moment
            new_two[place] = second
            step_size = (
                moment
                / (1.0 - beta_one**STEP)
                / (jnp.sqrt(second / (1.0 - beta_two**STEP)) + adam_eps)
            )
            weight = master[place]
            weight = weight - learn_rate * (step_size + decay_rate * weight)
            new_master[place] = weight
            new_ema[place] = average_rate * ema[place] + (1.0 - average_rate) * weight
            copy[place] = weight.astype(BF16)

        def many_rows(number, carry):
            advance(number * CHUNK, CHUNK)
            return carry

        lax.fori_loop(0, share // CHUNK, many_rows, 0)
        if share % CHUNK:
            advance(share // CHUNK * CHUNK, share % CHUNK)

    plain = pl.BlockSpec((1, share * BLOCK), lambda i, s: (0, 0))
    specs = [pl.BlockSpec(memory_space=pltpu.SMEM)]
    for grad, info in zip(wide, wide_info):
        specs.append(
            pl.BlockSpec(
                (pl.Element(info[3]), pl.Element(grad.shape[1])),
                lambda i, s, info=info: (slab_start(s[0], info), 0),
            )
        )
    specs.append(pl.BlockSpec(thin_all.shape, lambda i, s: (0, 0)))
    flat = jax.ShapeDtypeStruct((1, share * BLOCK), F32)
    return pl.pallas_call(
        body,
        grid_spec=pltpu.PrefetchScalarGridSpec(
            num_scalar_prefetch=1,
            grid=(1,),
            in_specs=specs + [plain] * 4,
            out_specs=[plain] * 5,
            scratch_shapes=[pltpu.VMEM((2 * margin + share + 8, BLOCK), F32)],
        ),
        out_shape=[flat] * 4 + [jax.ShapeDtypeStruct((1, share * BLOCK), BF16)],
        name="update",
    )(
        start.reshape(1),
        clip_factor.reshape(1),
        *wide,
        thin_all,
        *state,
    )


def per_device(
    hidden_in,
    cotangent,
    box_coords,
    doc_ids,
    buckets,
    layout_weight,
    norm_gains,
    norm_shifts,
    branch_biases,
    qkv_weight,
    query_value_bias,
    output_weight,
    ffn_in_weight,
    ffn_in_bias,
    ffn_out_weight,
    relative_table,
    master_flat,
    moment_one,
    moment_two,
    ema_flat,
):
    turn = lax.axis_index("tensor")
    window = turn.astype(jnp.int32).reshape(1)
    gains = norm_gains.astype(F32)
    norm_offsets = norm_shifts.astype(F32)
    biases = branch_biases.astype(F32)

    table_own = jnp.transpose(relative_table, (2, 0, 1))
    qkv_other = swap(qkv_weight)
    qv_bias_other = swap(query_value_bias)
    table_other = swap(table_own)
    output_other = swap(output_weight)
    ffn_in_other = swap(ffn_in_weight)
    ffn_bias_other = swap(ffn_in_bias)
    ffn_out_other = swap(ffn_out_weight)

    features = box_features(box_coords).astype(BF16)
    embedded = hidden_in.astype(F32) + dot_tn(features, layout_weight)
    inputs = embedded.astype(BF16)
    inputs_swap = swap(inputs)

    qkv_a, context_a, probs_a = attend(
        window, inputs, qkv_weight, query_value_bias, doc_ids, buckets, table_own
    )
    qkv_b, context_b, probs_b = attend(
        window, inputs, qkv_other, qv_bias_other, doc_ids, buckets, table_other
    )
    context_swap = swap(context_b)
    attn_out = dot(context_a, output_weight) + dot(context_b, output_other) + biases[0]
    normed_one, inv_std_one = normalize(embedded + attn_out)
    mid_norm = normed_one * gains[0] + norm_offsets[0]
    mid_low = mid_norm.astype(BF16)
    mid_swap = swap(mid_low)

    def expand(weight, bias):
        pre = dot(mid_low, weight) + bias.astype(F32)
        share = 0.5 + 0.5 * lax.erf(pre * math.sqrt(0.5))
        slope = share + pre * (math.sqrt(0.5 / math.pi) * jnp.exp(-0.5 * pre * pre))
        return (pre * share).astype(BF16), slope

    hidden_a, slope_a = expand(ffn_in_weight, ffn_in_bias)
    hidden_b, slope_b = expand(ffn_in_other, ffn_bias_other)
    hidden_swap = swap(hidden_b)
    branch = dot(hidden_a, ffn_out_weight) + dot(hidden_b, ffn_out_other) + biases[1]
    normed_two, inv_std_two = normalize(mid_norm + branch)
    hidden_out = (normed_two * gains[1] + norm_offsets[1]).astype(BF16)
    grad_out = cotangent.astype(F32)
    gain_two = jnp.sum(grad_out * normed_two, axis=0)
    shift_two = jnp.sum(grad_out, axis=0)
    grad_sum_two = norm_back(grad_out, normed_two, inv_std_two, gains[1])
    bias_two = jnp.sum(grad_sum_two, axis=0)
    grad_branch = grad_sum_two.astype(BF16)
    grad_branch_swap = swap(grad_branch)

    grad_pre_b = (slope_b * dot_nt(grad_branch, ffn_out_other)).astype(BF16)
    grad_pre_swap = swap(grad_pre_b)
    grad_pre_a = (slope_a * dot_nt(grad_branch, ffn_out_weight)).astype(BF16)
    ffn_out_low = (
        dot_tn(hidden_a, grad_branch) + dot_tn(hidden_swap, grad_branch_swap)
    ).astype(BF16)
    ffn_in_low = (dot_tn(mid_low, grad_pre_a) + dot_tn(mid_swap, grad_pre_swap)).astype(BF16)
    grad_mid = (
        grad_sum_two + dot_nt(grad_pre_a, ffn_in_weight) + dot_nt(grad_pre_b, ffn_in_other)
    )
    gain_one = jnp.sum(grad_mid * normed_one, axis=0)
    shift_one = jnp.sum(grad_mid, axis=0)
    grad_sum_one = norm_back(grad_mid, normed_one, inv_std_one, gains[0])
    bias_one = jnp.sum(grad_sum_one, axis=0)
    grad_attn = grad_sum_one.astype(BF16)
    grad_attn_swap = swap(grad_attn)
    output_grad = dot_tn(context_a, grad_attn) + dot_tn(context_swap, grad_attn_swap)
    grad_context_a = dot_nt(grad_attn, output_weight).astype(BF16)
    grad_context_b = dot_nt(grad_attn, output_other).astype(BF16)

    barrier = lax.optimization_barrier
    steps_a, steps_b = ring_steps(ring_bits(False)), ring_steps(ring_bits(True))
    out_keep, out_send = begin(
        steps_a[0], jnp.concatenate([ffn_out_low, output_grad.astype(BF16)])
    )
    in_keep, in_send = begin(steps_b[0], ffn_in_low)
    (grad_context_a, grad_context_b), out_send, in_send = barrier(
        ((grad_context_a, grad_context_b), out_send, in_send)
    )
    grads_a, grads_b, scores_a, scores_b = attend_back(
        window, (qkv_a, qkv_b), (grad_context_a, grad_context_b), (probs_a, probs_b)
    )
    grads_swap = swap(grads_b)
    width = qkv_weight.shape[2]
    early = input_back(grads_a, grads_b, qkv_weight, qkv_other, grad_sum_one, features, inputs)
    early, out_keep, in_keep = barrier((early, out_keep, in_keep))
    input_grad, layout_part, product, columns = early
    out_sum = finish(steps_a[0], out_keep, out_send)
    in_sum = finish(steps_b[0], in_keep, in_send)

    out_keep, out_send = begin(steps_a[1], out_sum)
    in_keep, in_send = begin(steps_b[1], in_sum)
    product, scores_a, scores_b, out_send, in_send = barrier(
        (product, scores_a, scores_b, out_send, in_send)
    )
    sides = jnp.stack([side_of(steps[0][1]) for steps in (steps_a, steps_b)]).astype(jnp.int32)
    late = pair_back(sides, inputs_swap, grads_swap, product, columns)
    tables = table_sums(window, (scores_a, scores_b), buckets)
    late, tables, out_keep, in_keep = barrier((late, tables, out_keep, in_keep))
    a_keep, a_send, b_keep, b_send, qv_sums = late
    out_sum = finish(steps_a[1], out_keep, out_send)
    in_sum = finish(steps_b[1], in_keep, in_send)

    plans = {
        "out": (0, steps_a[2:]),
        "in": (0, steps_b[2:]),
        "a": (0, steps_a),
        "b": (0, steps_b),
        "c": (1, steps_b),
    }
    sums = {"out": out_sum, "in": in_sum}
    last = len(steps_a) - 1
    late_got = {}
    for number in range(last + 2):
        if number == 1:
            other = swap(other_shared).astype(F32)
            pack_c = own_shared + jnp.pad(
                other, ((0, own_shared.shape[0] - other.shape[0]), (0, 0))
            )
            pack_c = pack_c.astype(BF16)
            sums["c"] = pack_c
        opened = {
            name: begin(steps[number - first], sums[name])
            for name, (first, steps) in plans.items()
            if first <= number < first + len(steps) and name in sums
        }
        if number == 0:
            opened["a"], opened["b"] = (a_keep, a_send), (b_keep, b_send)
        sends = {name: send for name, (_, send) in opened.items()}
        if number == 0:
            sends, tables, qv_sums, layout_part = barrier((sends, tables, qv_sums, layout_part))
            cut = (layout_part.shape[0] + 6) // lax.axis_size("tensor")
            own_shared, other_shared = small_parts(
                window,
                layout_part,
                (gain_one, gain_two, shift_one, shift_two, bias_one, bias_two),
                tables,
                qv_sums,
                grad_pre_a,
                grad_pre_swap,
                cut,
            )
        elif number == last - 1:
            small_send = sends.pop("c")
            sends = barrier(sends)
            sends["c"], sums["out"], sums["in"] = barrier(
                (small_send, sums["out"], sums["in"])
            )
        elif number == last + 1:
            sends, sums["a"], sums["b"] = barrier((sends, sums["a"], sums["b"]))
        elif number == last:
            sends, early_pairs = barrier((sends, (sums["out"], sums["in"])))
            settled = settle(sides, *early_pairs, ffn_out_low.shape[0])
        else:
            sends = barrier(sends)
        for name, (kept, _) in opened.items():
            first, steps = plans[name]
            step = steps[number - first]
            if name == "c" and number == last:
                late_got, settled = barrier((late_got, settled))
                for late in ("a", "b"):
                    sums[late] = merge(plans[late][1][last], *late_got[late])
                kept, sums["a"], sums["b"] = barrier((kept, sums["a"], sums["b"]))
            if name in ("a", "b") and number == last:
                late_got[name] = (kept, across(step, sends[name]))
            elif name in ("out", "in") and number == last - 2:
                sums[name] = (kept, across(step, sends[name]))
            else:
                sums[name] = finish(step, kept, sends[name])
    pack_a, pack_b, pack_c = (sums[name] for name in ("a", "b", "c"))
    ffn_out_grad, output_grad, ffn_in_grad, early_square = settled

    square = sum(
        jnp.sum(jnp.square(member.astype(F32)))
        for member in (pack_a, pack_b, pack_c)
    )
    square = square + early_square[0, 0]
    qkv_grad = jnp.stack(
        [
            jnp.concatenate([part[:, c * width : (c + 1) * width] for part in (pack_a, pack_b)])
            for c in range(3)
        ]
    ).astype(F32)
    own_low = pack_c[:cut]
    small = pack_c[cut : cut + 4].astype(F32)
    table_grad = small[0, : relative_table.size].reshape(relative_table.shape)
    qv_bias_grad = small[1].reshape(query_value_bias.shape)
    ffn_bias_grad = small[2:4].reshape(-1)
    first_turn = turn == 0
    other_low = swap(own_low)
    shared = jnp.where(
        first_turn,
        jnp.concatenate([own_low, other_low]),
        jnp.concatenate([other_low, own_low]),
    ).astype(F32)
    layout_grad = shared[: layout_part.shape[0]]
    gains_grad, shifts_grad, biases_grad = jnp.split(shared[layout_part.shape[0] :], 3)

    grad_norm = jnp.sqrt(square + swap(square))
    clip_factor = clip_limit / jnp.maximum(grad_norm, clip_limit)
    updated = update(
        clip_factor,
        (
            ffn_in_grad,
            ffn_bias_grad,
            ffn_out_grad,
            qkv_grad.reshape(-1, width),
            qv_bias_grad,
            output_grad,
            table_grad,
            own_low.astype(F32),
        ),
        (master_flat, moment_one, moment_two, ema_flat),
    )
    return (
        hidden_out,
        input_grad,
        layout_grad,
        gains_grad,
        shifts_grad,
        biases_grad,
        qkv_grad,
        qv_bias_grad,
        output_grad,
        ffn_in_grad,
        ffn_bias_grad,
        ffn_out_grad,
        table_grad,
        grad_norm,
    ) + tuple(updated)


def solution(mesh):
    return jax.shard_map(
        per_device,
        mesh=mesh,
        in_specs=(
            P(("dp", "tensor"), None),
            P(("dp", "tensor"), None),
            P(None, ("dp", "tensor")),
            P("dp", None),
            P(None, "dp", None, None),
            P(),
            P(),
            P(),
            P(),
            P(None, None, "tensor"),
            P(None, "tensor"),
            P("tensor", None),
            P(None, "tensor"),
            P("tensor"),
            P("tensor", None),
            P(None, None, "tensor"),
            P("tensor", "dp"),
            P("tensor", "dp"),
            P("tensor", "dp"),
            P("tensor", "dp"),
        ),
        out_specs=(
            P(("dp", "tensor"), None),
            P(("dp", "tensor"), None),
            P(),
            P(),
            P(),
            P(),
            P(None, None, "tensor"),
            P(None, "tensor"),
            P("tensor", None),
            P(None, "tensor"),
            P("tensor"),
            P("tensor", None),
            P(None, None, "tensor"),
            P(),
            P("tensor", "dp"),
            P("tensor", "dp"),
            P("tensor", "dp"),
            P("tensor", "dp"),
            P("tensor", "dp"),
        ),
        check_vma=False,
    )
```
